32 devices in a mesh: seq: 8 (over z, y), tok: 4 (over x, core).
Axes of the slice: x: 2, y: 2, z: 4, core: 2. Of those that a mesh axis runs over, the one named last changes fastest.
Arguments:
- tokens: bfloat16 [8, 1024, 1024], P('seq', 'tok'), may hold values from -6 to 6
- out_grad: bfloat16 [8, 1024, 1024], P('seq', 'tok'), may hold values from -6 to 6
- segments: int32 [8, 1024], P('seq'), may hold values from 0 to 2, never falling along the last dimension, each value on 1 to 512 neighbouring positions
- adapter_index: int32 [8], P('seq'), may hold values from 0 to 7
- qkv_weight: bfloat16 [1024, 3072], P('tok', 'seq'), may hold values from -0.1875 to 0.1875
- out_weight: bfloat16 [1024, 1024], P('tok', 'seq'), may hold values from -0.75 to 0.75
- in_weight: bfloat16 [1024, 5248], P('tok', 'seq'), may hold values from -0.1875 to 0.1875
- out2_weight: bfloat16 [2624, 1024], P('tok', 'seq'), may hold values from -0.15625 to 0.15625
- attn_gain: bfloat16 [1024], P('tok'), may hold values from 0.099609375 to 1.8984375
- mlp_gain: bfloat16 [1024], P('tok'), may hold values from 0.099609375 to 1.8984375
- qkv_down: bfloat16 [8, 16, 1024], replicated, may hold values from -0.1875 to 0.1875
- qkv_up: bfloat16 [8, 16, 3072], replicated, may hold values from -0.5 to 0.5
- out_down: bfloat16 [8, 16, 1024], replicated, may hold values from -0.1875 to 0.1875
- out_up: bfloat16 [8, 16, 1024], replicated, may hold values from -1.5 to 1.5
- in_down: bfloat16 [8, 16, 1024], replicated, may hold values from -0.1875 to 0.1875
- in_up: bfloat16 [8, 16, 5248], replicated, may hold values from -0.5 to 0.5
- out2_down: bfloat16 [8, 16, 2624], replicated, may hold values from -0.125 to 0.125
- out2_up: bfloat16 [8, 16, 1024], replicated, may hold values from -0.5 to 0.5
Outputs:
- layer_out: bfloat16 [8, 1024, 1024], P('seq', 'tok')
- input_grad: bfloat16 [8, 1024, 1024], P('seq', 'tok')
- qkv_down_grad: float32 [8, 16, 1024], replicated
- qkv_up_grad: float32 [8, 16, 3072], replicated
- out_down_grad: float32 [8, 16, 1024], replicated
- out_up_grad: float32 [8, 16, 1024], replicated
- in_down_grad: float32 [8, 16, 1024], replicated
- in_up_grad: float32 [8, 16, 5248], replicated
- out2_down_grad: float32 [8, 16, 2624], replicated
- out2_up_grad: float32 [8, 16, 1024], replicated
The draws below stay inside these ranges and needn't reach their ends.
Inputs may be any that keep to these rules, and one draw needn't show every extreme that they name: `segments`: within a sequence the document numbers never fall; each document has 1 to 512 tokens, one of each sequence exactly 512.
All inputs are finite; a program needn't handle non-finite values.
Results may differ from the reference program's by a relative error of at most 0.018.
Values may be sent and summed in bfloat16 or wider, within the bound.
No kernel may reach another device: no remote copies, remote signals or barrier semaphores. Data moves between devices by JAX's collectives and lax.ppermute only.
A program may use at most 128 MiB of HBM per device.

```python
import math
import jax
import jax.numpy as jnp
import numpy as np
from jax import lax

D = 1024
HEADS = 16
HEAD_DIM = 64
FF = 2624
RANK = 16
ADAPTERS = 8
SEQ_LEN = 1024
SEQUENCES = 8
DOC_MOST = 512
DOCS = 3


def place_ends(values, rng, smallest, largest):
    index_at = [jax.random.randint(jax.random.fold_in(rng, axis), (), 0, length) for axis, length in enumerate(values.shape)]
    main_axis = values.shape.index(max(values.shape))
    beside = index_at[:main_axis] + [(index_at[main_axis] + 1) % values.shape[main_axis]] + index_at[main_axis + 1:]
    return values.at[tuple(index_at)].set(smallest).at[tuple(beside)].set(largest)


def levels(own_key, shape, cuts, smallest, top_value):
    def one(axis_at, shards_of):
        draws = jax.random.uniform(jax.random.fold_in(jax.random.fold_in(own_key, 6), axis_at), (shards_of,), jnp.float32, smallest / len(cuts), top_value / len(cuts))
        return jnp.repeat(jnp.exp(draws), shape[axis_at] // shards_of).reshape((-1,) + (1,) * (len(shape) - axis_at - 1))

    level = one(*cuts[0])
    for cut in cuts[1:]:
        level = level * one(*cut)
    return level


def length_profile(count, total, bound, slope):
    weights = [(1 << 20) // math.isqrt(rank ** slope) + 1 for rank in range(2, count + 1)]
    surplus, given = total - bound - (count - 1), [1] * (count - 1)
    while surplus > 0:
        movable = [i for i in range(count - 1) if given[i] < bound]
        whole, budget = sum([weights[i] for i in movable]), surplus
        for i in movable:
            extra = min(bound - given[i], max(1, budget * weights[i] // whole), surplus)
            given[i] = given[i] + extra
            surplus = surplus - extra
    return np.array([bound] + given)


def uneven_parts(key, amount, total, limit, skew):
    if amount == 2:
        one = jax.random.randint(key, (), max(1, total - limit), min(limit, total - 1) + 1)
        return jnp.stack([one, total - one])
    tallies = jnp.asarray(length_profile(amount, total, limit, skew), jnp.int32)
    couples = (amount - 1) // 2
    donor, taker = tallies[1:1 + 2 * couples:2], tallies[2:2 + 2 * couples:2]
    margin = jnp.minimum(donor - 1, limit - taker)
    shifted = jax.random.randint(jax.random.fold_in(key, 1), (couples,), 0, 1 << 20) % (margin + 1)
    tallies = tallies.at[1:1 + 2 * couples:2].set(donor - shifted).at[2:2 + 2 * couples:2].set(taker + shifted)
    return tallies[jax.random.permutation(jax.random.fold_in(key, 2), amount)]


def centred(key, shape, width, limit, cuts=(), held_as=jnp.bfloat16):
    array = width * jax.random.normal(key, shape, jnp.float32)
    if cuts:
        array = array * levels(key, shape, cuts, -0.22, 0.18)
    return jnp.clip(array, -limit, limit).astype(held_as)


def setup_inputs(seed: int = 0) -> dict:
    key_of = jax.random.split(jax.random.key(seed), 19)
    tokens = centred(key_of[0], (SEQUENCES, SEQ_LEN, D), 1.0, 6.0, ((0, 8), (1, 4)))
    out_grad = centred(key_of[1], (SEQUENCES, SEQ_LEN, D), 1.0, 6.0, ((0, 8), (1, 4)))
    segments = jax.vmap(lambda own: jnp.searchsorted(jnp.cumsum(uneven_parts(own, DOCS, SEQ_LEN, DOC_MOST, 1)), jnp.arange(SEQ_LEN), side="right"))(jax.random.split(key_of[2], SEQUENCES)).reshape((SEQUENCES, SEQ_LEN)).astype(jnp.int32)
    adapter_index = place_ends(jax.random.randint(key_of[3], (SEQUENCES,), 0, ADAPTERS), jax.random.fold_in(key_of[3], 1), 0, ADAPTERS - 1).astype(jnp.int32)
    qkv_weight = centred(key_of[4], (D, 3 * D), D ** -0.5, 0.1875, ((0, 4), (1, 8)))
    out_weight = centred(key_of[5], (D, D), (D // 16) ** -0.5, 0.75, ((0, 4), (1, 8)))
    in_weight = centred(key_of[6], (D, 2 * FF), D ** -0.5, 0.1875, ((0, 4), (1, 8)))
    out2_weight = centred(key_of[7], (FF, D), (FF // 2) ** -0.5, 0.15625, ((0, 4), (1, 8)))
    attn_gain = jnp.clip(1.0 + 0.18 * jax.random.normal(key_of[8], (D,), jnp.float32), 0.099609375, 1.8984375).astype(jnp.bfloat16)
    mlp_gain = jnp.clip(1.0 + 0.18 * jax.random.normal(key_of[9], (D,), jnp.float32), 0.099609375, 1.8984375).astype(jnp.bfloat16)
    qkv_down = centred(key_of[10], (ADAPTERS, RANK, D), D ** -0.5, 0.1875)
    qkv_up = centred(key_of[11], (ADAPTERS, RANK, 3 * D), (8 * RANK) ** -0.5, 0.5)
    out_down = centred(key_of[12], (ADAPTERS, RANK, D), D ** -0.5, 0.1875)
    out_up = centred(key_of[13], (ADAPTERS, RANK, D), RANK ** -0.5, 1.5)
    in_down = centred(key_of[14], (ADAPTERS, RANK, D), D ** -0.5, 0.1875)
    in_up = centred(key_of[15], (ADAPTERS, RANK, 2 * FF), (8 * RANK) ** -0.5, 0.5)
    out2_down = centred(key_of[16], (ADAPTERS, RANK, FF), FF ** -0.5, 0.125)
    out2_up = centred(key_of[17], (ADAPTERS, RANK, D), (8 * RANK) ** -0.5, 0.5)
    return dict(tokens=tokens, out_grad=out_grad, segments=segments, adapter_index=adapter_index, qkv_weight=qkv_weight, out_weight=out_weight, in_weight=in_weight, out2_weight=out2_weight, attn_gain=attn_gain, mlp_gain=mlp_gain, qkv_down=qkv_down, qkv_up=qkv_up, out_down=out_down, out_up=out_up, in_down=in_down, in_up=in_up, out2_down=out2_down, out2_up=out2_up)


HIGH = lax.Precision.HIGHEST
EPS = 1e-05
THETA = 160000.0

@jax.custom_vjp
def low(v):
    return lax.optimization_barrier(v.astype(jnp.bfloat16)).astype(jnp.float32)

@jax.custom_vjp
def low_back(v):
    return v

def low_keep(v):
    return (low(v), None)

def low_pass(kept, grad):
    return (grad,)

def back_keep(v):
    return (v, None)

def back_low(kept, grad):
    return (low(grad),)
low.defvjp(low_keep, low_pass)
low_back.defvjp(back_keep, back_low)

def matmul(left, right):
    return jnp.dot(left, right, precision=HIGH, preferred_element_type=jnp.float32)

def layer_norm(values, gain_vec):
    middle = lax.optimization_barrier(jnp.mean(values, axis=-1, keepdims=True))
    centered = values - middle
    spread = lax.optimization_barrier(jnp.mean(centered * centered, axis=-1, keepdims=True))
    return centered * lax.rsqrt(spread + EPS) * gain_vec

def rotary(values, positions):
    head_width = values.shape[-1]
    half_width = head_width // 2
    exponent = jnp.arange(0, head_width, 2).astype(jnp.float32) / head_width
    inverse = 1.0 / THETA ** exponent
    phases = positions.astype(jnp.float32)[:, None] * inverse[None, :]
    cosine = jnp.concatenate([jnp.cos(phases), jnp.cos(phases)], -1)[:, None, :]
    sine_part = jnp.concatenate([jnp.sin(phases), jnp.sin(phases)], -1)[:, None, :]
    turned = jnp.concatenate([-values[..., half_width:], values[..., :half_width]], -1)
    return values * cosine + turned * sine_part

def adapted(inputs, weight, down_rows, up_rows):
    narrow = low(low_back(matmul(inputs, down_rows.T)))
    return matmul(inputs, weight) + matmul(narrow, up_rows)

def head_attention(query, key_rows, value_rows, doc_mask):
    raw_scores = low_back(matmul(query, key_rows.T))
    scores = jnp.where(doc_mask, raw_scores * 0.125, -1e+30)
    row_max = lax.optimization_barrier(jnp.max(scores, axis=-1, keepdims=True))
    expd = jnp.exp(scores - row_max)
    attn_prob = expd / lax.optimization_barrier(jnp.sum(expd, axis=-1, keepdims=True))
    return matmul(low(attn_prob), value_rows)

def sequence_forward(inputs, segment, pick_index, frozen, tables):
    qkv_weight, out_weight, in_weight, out2_weight, attn_gain, mlp_gain = frozen
    chosen = [table_rows[pick_index] for table_rows in tables]
    length = inputs.shape[0]
    positions = jnp.arange(length)
    norm_one = low(layer_norm(inputs, attn_gain))
    qkv = low_back(adapted(norm_one, qkv_weight, chosen[0], chosen[1]))
    head_shape = (length, HEADS, HEAD_DIM)
    query = low(rotary(qkv[:, :D].reshape(head_shape), positions))
    key_rows = low(rotary(qkv[:, D:2 * D].reshape(head_shape), positions))
    value_rows = low(qkv[:, 2 * D:].reshape(head_shape))
    doc_mask = segment[:, None] == segment[None, :]
    head_step = jax.checkpoint(head_attention)
    per_head = lax.map(lambda head_item: head_step(head_item[0], head_item[1], head_item[2], doc_mask), (query.transpose(1, 0, 2), key_rows.transpose(1, 0, 2), value_rows.transpose(1, 0, 2)))
    attn = low(low_back(per_head.transpose(1, 0, 2).reshape(length, D)))
    middle = inputs + low_back(adapted(attn, out_weight, chosen[2], chosen[3]))
    norm_two = low(layer_norm(middle, mlp_gain))
    gate_up = low_back(adapted(norm_two, in_weight, chosen[4], chosen[5]))
    act = low(jax.nn.gelu(gate_up[:, :FF], approximate=False) * gate_up[:, FF:])
    return middle + low_back(adapted(act, out2_weight, chosen[6], chosen[7]))

def reference(tokens, out_grad, segments, adapter_index, qkv_weight, out_weight, in_weight, out2_weight, attn_gain, mlp_gain, qkv_down, qkv_up, out_down, out_up, in_down, in_up, out2_down, out2_up):
    frozen = tuple((weight.astype(jnp.float32) for weight in (qkv_weight, out_weight, in_weight, out2_weight, attn_gain, mlp_gain)))
    tables = tuple((table_rows.astype(jnp.float32) for table_rows in (qkv_down, qkv_up, out_down, out_up, in_down, in_up, out2_down, out2_up)))
    inputs = tokens.astype(jnp.float32)

    def forward(values, adapter_tables):

        def per_seq(carry, seq_item):
            return (carry, sequence_forward(seq_item[0], seq_item[1], seq_item[2], frozen, adapter_tables))
        return lax.scan(per_seq, jnp.zeros((), jnp.float32), (values, segments, adapter_index))[1]
    result, pull_back = jax.vjp(forward, inputs, tables)
    grad_inputs, grad_tables = pull_back(out_grad.astype(jnp.float32))
    return (result.astype(jnp.bfloat16), grad_inputs.astype(jnp.bfloat16), grad_tables[0], grad_tables[1], grad_tables[2], grad_tables[3], grad_tables[4], grad_tables[5], grad_tables[6], grad_tables[7])
```

```python
import functools

import jax
import jax.numpy as jnp
from jax import lax
from jax.experimental import pallas as pl
from jax.experimental.pallas import tpu as pltpu
from jax.sharding import PartitionSpec as P

HEADS = 16
HEAD_DIM = 64
EPS = 1e-05
THETA = 160000.0
F32 = jnp.float32
BF16 = jnp.bfloat16
MIB = 1024 * 1024


def nn(a, b):
    return lax.dot_general(a, b, (((1,), (0,)), ((), ())), preferred_element_type=F32)


def nt(a, b):
    return lax.dot_general(a, b, (((1,), (1,)), ((), ())), preferred_element_type=F32)


def tn(a, b):
    return lax.dot_general(a, b, (((0,), (0,)), ((), ())), preferred_element_type=F32)


def call(kernel, out_shape, args, scratch=(), smem=(), micros=1, name=None):
    out_shape = list(out_shape)
    size = lambda a: a.size * a.dtype.itemsize
    moved = sum(size(a) for a in args) + sum(size(o) for o in out_shape)
    flops = max(micros, 1) * 10**9
    specs = [
        pl.BlockSpec(memory_space=pltpu.SMEM if n in smem else pltpu.VMEM)
        for n in range(len(args))
    ]
    return pl.pallas_call(
        kernel,
        out_shape=out_shape,
        in_specs=specs,
        out_specs=[pl.BlockSpec(memory_space=pltpu.VMEM) for _ in out_shape],
        scratch_shapes=list(scratch),
        compiler_params=pltpu.CompilerParams(vmem_limit_bytes=60 * MIB),
        cost_estimate=pl.CostEstimate(
            flops=int(flops), bytes_accessed=int(moved), transcendentals=0
        ),
        name=name,
    )(*args)


def shape(dims, dtype):
    return jax.ShapeDtypeStruct(tuple(dims), dtype)


def to_slot(refs, index, value):
    for n, ref in enumerate(refs):

        @pl.when(index == n)
        def _(ref=ref):
            ref[...] = value


def normalized(rows):
    mean = jnp.mean(rows, axis=-1, keepdims=True)
    centered = rows - mean
    scale = lax.rsqrt(jnp.mean(centered * centered, axis=-1, keepdims=True) + EPS)
    return centered * scale, scale


def norm_back(rows, gain, grad):
    unit, scale = normalized(rows)
    weighted = grad * gain
    first = jnp.mean(weighted, axis=-1, keepdims=True)
    second = jnp.mean(weighted * unit, axis=-1, keepdims=True)
    return (weighted - first - unit * second) * scale


def swapped(rows):
    width = rows.shape[1]
    if width % 128:
        half = HEAD_DIM // 2
        parts = []
        for start in range(0, width, HEAD_DIM):
            parts += [rows[:, start + half : start + HEAD_DIM], rows[:, start : start + half]]
        return jnp.concatenate(parts, axis=1)
    lane = lax.broadcasted_iota(jnp.int32, rows.shape, 1)
    ahead = pltpu.roll(rows, width - HEAD_DIM // 2, 1)
    behind = pltpu.roll(rows, HEAD_DIM // 2, 1)
    return jnp.where(lane % HEAD_DIM < HEAD_DIM // 2, ahead, behind)


def widened(table, width):
    if width <= table.shape[1]:
        return table[:, :width]
    return jnp.concatenate([table] * (width // table.shape[1]), axis=1)


def head_part(rows, head):
    lane = lax.broadcasted_iota(jnp.int32, rows.shape, 1)
    return jnp.where(lane // HEAD_DIM == head, rows, jnp.zeros_like(rows))


def norm_kernel(tokens, norm_out, gain_out):
    count, rows, width = tokens.shape
    rows = rows - 16
    part = width // count
    for n in range(count):
        gain_out[:, n * part : (n + 1) * part] = tokens[n, rows:, :part].astype(F32)[:2]

    def step(n, _):
        unit, _ = normalized(tokens[n, :rows].astype(F32))
        at = pl.ds(pl.multiple_of(n * rows, rows), rows)
        norm_out[at, :] = (unit * gain_out[0:1, :]).astype(BF16)
        return 0

    lax.fori_loop(0, count, step, 0)


def qkv_kernel(pieces, block, place, norm, down, ups, cosine, sine, *refs):
    weights, (query, key, value, whole) = refs[:pieces], refs[pieces : pieces + 4]
    width = query.shape[1]
    if pieces == 1:
        whole[...] = weights[0][...]
    else:
        out_weight = refs[pieces + 4]
        unit = width // 2
        first = 0
        for n in range(pieces):
            depth = weights[n].shape[0]
            spot = place[n]
            half, part = spot // 4, lax.rem(spot, 4)
            down_at = pl.ds(pl.multiple_of(part * width + first, depth), depth)
            double, single = place[pieces + half], place[pieces + 2]
            whole[double, down_at, :] = weights[n][:, :width]
            across = pl.ds(pl.multiple_of(half * unit, unit), unit)
            whole[single, down_at, across] = weights[n][:, width : width + unit]
            across = pl.ds(pl.multiple_of(spot * unit, unit), unit)
            out_weight[first : first + depth, across] = weights[n][:, width + unit :]
            first = (first + depth) % width
    for kind in range(3):
        whole[kind] = (whole[kind].astype(F32) + tn(down[...], ups[kind])).astype(BF16)

    def step(n, _):
        at = pl.ds(pl.multiple_of(n * block, block), block)
        rows = norm[at, :]
        cos, sin = widened(cosine[at, :], width), widened(sine[at, :], width)
        for kind, out in enumerate((query, key, value)):
            part = nn(rows, whole[kind])
            if kind < 2:
                part = part * cos + swapped(part) * sin
            if kind == 0:
                part = part.astype(BF16).astype(F32) * 0.125
            out[at, :] = part.astype(BF16)
        return 0

    lax.fori_loop(0, norm.shape[0] // block, step, 0)


def chunked(ref, base, value):
    count = -(-value.shape[1] // 128)
    for n in range(count):
        part = value[:, n * 128 : (n + 1) * 128].astype(ref.dtype)
        if part.shape[1] < 128:
            ref[base + n] = jnp.zeros(ref.shape[1:], ref.dtype)
            ref[base + n, :, : part.shape[1]] = part
        else:
            ref[base + n] = part
    return base + count


def attend_kernel(count, order, query, key, value, seg_col, seg_row, *refs):
    outs, (log_total, value_t, bias) = refs[:count], refs[count:]
    block = outs[0].shape[0]
    width = query.shape[1]
    value_t[...] = value[...].T

    def step(n, _):
        at = pl.ds(pl.multiple_of(order[n] * block, block), block)
        rows = query[at, :]
        bias[...] = jnp.where(seg_col[...] == seg_row[:, at], 0.0, -1e30)
        parts = []
        for head in range(width // HEAD_DIM):
            scores = nt(key[...], head_part(rows, head)) + bias[...]
            top = jnp.max(scores, axis=0, keepdims=True)
            raised = jnp.exp(scores - top)
            total = jnp.sum(raised, axis=0, keepdims=True)
            log_total[head : head + 1, at] = top + jnp.log(total)
            prob = (raised * (1.0 / total)).astype(BF16)
            parts.append(nn(value_t[head * HEAD_DIM : (head + 1) * HEAD_DIM, :], prob))
        mixed = jnp.concatenate(parts, axis=0).T
        to_slot(outs, n, mixed.astype(BF16))
        return 0

    lax.fori_loop(0, count, step, 0)


def out_kernel(count, order, inputs, gain, down, up, *refs):
    attn, weights = refs[:count], refs[count : 2 * count]
    middle, norm, narrow = refs[2 * count :]
    width = attn[0].shape[1]
    total = inputs[...].astype(F32)
    thin = jnp.zeros(narrow.shape, F32)
    for n in range(count):
        total = total + nn(attn[n][...], weights[n][...])
        thin = thin + nt(attn[n][...], down[order[n]])
    thin = thin.astype(BF16)
    total = total + nn(thin, up[...])
    middle[...] = total
    narrow[...] = thin
    norm[...] = (normalized(total)[0] * gain[1:2, :]).astype(BF16)


def mlp_pre_kernel(packed, order, place, down_in, up_in, down_out, up_out, grads, *refs):
    pieces = 9 if packed else 2
    weights, (w_in, w_out, grad_act) = refs[:pieces], refs[pieces:]
    hidden, width = w_out.shape
    if packed:
        depth, thin = width // 4, width // 8
        first = 0
        for n in range(pieces):
            rows = slice(first, first + weights[n].shape[0])
            spot = place[n]
            across = pl.ds(pl.multiple_of(lax.rem(spot, 4) * depth, depth), depth)
            w_in[spot // 4, rows, across] = weights[n][:, :depth]
            across = pl.ds(pl.multiple_of(spot * thin, thin), thin)
            w_out[rows, across] = weights[n][:, depth:]
            first = rows.stop % hidden
    else:
        w_in[...] = weights[0][...]
        w_out[...] = weights[1][...]
    for n in range(2):
        w_in[n] = (w_in[n].astype(F32) + tn(up_in[n], down_in[...])).astype(BF16)
    w_out[...] = (w_out[...].astype(F32) + tn(down_out[...], up_out[...])).astype(BF16)

    for n in range(grads.shape[0]):
        grad_act[n] = nt(grads[order[n]], w_out[...])


def mlp_kernel(count, first, w_in, grad_act, *refs):
    norms, backs, (act_out, grad_out) = refs[:count], refs[count : 2 * count], refs[2 * count :]
    rows = norms[0].shape[0]
    for n in range(count):
        norm = norms[n][...]
        inputs, gate = nt(norm, w_in[0]), nt(norm, w_in[1])
        phi = 0.5 + 0.5 * lax.erf(inputs * (0.5**0.5))
        gelu = inputs * phi
        act_out[n] = (gelu * gate).astype(BF16)
        back_act = grad_act[first + n]
        slope = phi + inputs * (jnp.exp(-0.5 * inputs * inputs) * 0.3989422804014327)
        grad_inputs = (back_act * gate * slope).astype(BF16)
        grad_gate = (back_act * gelu).astype(BF16)
        grad_out[0, n] = grad_inputs
        grad_out[1, n] = grad_gate
        backs[n][...] = (nn(grad_inputs, w_in[0]) + nn(grad_gate, w_in[1])).astype(BF16)


def mlp_post_kernel(count, first, order, pick, down_in, up_in, down_out, up_out, w_out, *refs):
    acts, grads, out_grad, refs = refs[:2], refs[2:4], refs[4], refs[5:]
    norms, outs = refs[:count], refs[count : 2 * count]
    terms, norm_all, act_all, grad_all = refs[2 * count : 2 * count + 4]
    down_in_grad, up_in_grad, down_out_grad, up_out_grad = refs[2 * count + 4 :]
    for n in range(count):
        norm_all[n] = norms[n][...]
        act_all[n] = acts[n // 2][n % 2]
        for h in range(2):
            grad_all[h, n] = grads[n // 2][h, n % 2]
    for ref in (down_in_grad, up_in_grad, down_out_grad, up_out_grad):
        ref[...] = jnp.zeros_like(ref)

    def step(n, _):
        act, norm = act_all[n], norm_all[n]
        grad = out_grad[order[first + n]]
        to_slot(outs, n, nn(act, w_out[...]).astype(BF16))
        narrow = nt(norm, down_in[...]).astype(BF16)
        narrow_two = nt(act, down_out[...]).astype(BF16)
        inner = nt(grad, up_out[...]).astype(BF16)
        inner_in = (nt(grad_all[0, n], up_in[0]) + nt(grad_all[1, n], up_in[1])).astype(BF16)
        down_in_grad[...] += tn(inner_in, norm)
        up_in_grad[0] += tn(narrow, grad_all[0, n])
        up_in_grad[1] += tn(narrow, grad_all[1, n])
        down_out_grad[...] += tn(inner, act)
        up_out_grad[...] += tn(narrow_two, grad)
        return 0

    lax.fori_loop(0, count, step, 0)
    at = chunked(terms, 0, up_in_grad[0])
    at = chunked(terms, at, up_in_grad[1])
    at = chunked(terms, at, down_out_grad[...])
    terms[at] = jnp.full(terms.shape[1:], pick[0].astype(F32)).astype(terms.dtype)
    at = chunked(terms, at + 1, down_in_grad[...])
    chunked(terms, at, up_out_grad[...])


def out_back_kernel(count, parts, order, middle, out_grad, gain, down, up, narrow, *refs):
    back, refs = refs[:parts], refs[parts:]
    attn, weights = refs[:count], refs[count : 2 * count]
    grad_mid, refs = refs[2 * count], refs[2 * count + 1 :]
    slots, (terms, down_grad) = refs[:count], refs[count:]
    total = back[0][...].astype(F32)
    for ref in back[1:]:
        total = total + ref[...].astype(F32)
    grad = out_grad[...].astype(F32) + norm_back(middle[...], gain[1:2, :], total)
    grad_mid[...] = grad
    low = grad.astype(BF16)
    inner = nt(low, up[...]).astype(BF16)
    chunks = middle.shape[1] // 128
    chunked(terms, chunks, tn(narrow[...], low))
    for n in range(count):
        slots[n][...] = (nt(low, weights[n][...]) + nn(inner, down[order[n]])).astype(BF16)
        down_grad[order[n]] = tn(inner, attn[n][...])
    chunked(terms, 0, jnp.concatenate([down_grad[n] for n in range(count)], axis=1))


def attend_back_kernel(
    count, order, query, key, value, seg_col, seg_row, log_total, cosine, sine, weights, *refs
):
    grads, outs = refs[:count], refs[count : 2 * count]
    grad_qkv, key_t, bias, grad_all, grad_q, grad_k, grad_v = refs[2 * count :]
    block = outs[0].shape[0]
    width = query.shape[1]
    key_t[...] = key[...].T
    for n in range(count):
        grad_all[n * block : (n + 1) * block, :] = grads[n][...]
    for ref in (grad_k, grad_v):
        ref[...] = jnp.zeros_like(ref)

    def step(n, _):
        at = pl.ds(pl.multiple_of(order[n] * block, block), block)
        rows = query[at, :]
        grad = grad_all[pl.ds(pl.multiple_of(n * block, block), block), :]
        bias[...] = jnp.where(seg_col[...] == seg_row[:, at], 0.0, -1e30)
        parts = []
        for head in range(width // HEAD_DIM):
            own = head_part(rows, head)
            own_grad = head_part(grad, head)
            scores = nt(key[...], own) + bias[...]
            prob = jnp.exp(scores - log_total[head : head + 1, at])
            grad_prob = nt(value[...], own_grad)
            dots = jnp.sum(prob * grad_prob, axis=0, keepdims=True)
            grad_s = (prob * (grad_prob - dots)).astype(BF16)
            grad_k[...] += nn(grad_s, own)
            grad_v[...] += nn(prob.astype(BF16), own_grad)
            parts.append(nn(key_t[head * HEAD_DIM : (head + 1) * HEAD_DIM, :], grad_s))
        grad_q[at, :] = jnp.concatenate(parts, axis=0).T * 0.125
        return 0

    lax.fori_loop(0, count, step, 0)

    def finish(n, _):
        at = pl.ds(pl.multiple_of(order[n] * block, block), block)
        cos, sin = widened(cosine[at, :], width), widened(sine[at, :], width)
        low = []
        for ref in (grad_q, grad_k):
            part = ref[at, :]
            low.append((part * cos - swapped(part) * sin).astype(BF16))
        low.append(grad_v[at, :].astype(BF16))
        total = 0.0
        for kind in range(3):
            grad_qkv[kind, at, :] = low[kind]
            total = total + nt(low[kind], weights[kind])
        to_slot(outs, n, total.astype(BF16))
        return 0

    lax.fori_loop(0, count, finish, 0)


def qkv_terms_kernel(pick, norm, grad_qkv, down, ups, terms):
    narrow = nt(norm[...], down[...]).astype(BF16)
    inner = sum(nt(grad_qkv[kind], ups[kind]) for kind in range(3)).astype(BF16)
    at = 0
    for kind in range(3):
        at = chunked(terms, at, tn(narrow, grad_qkv[kind]))
    terms[at] = jnp.full(terms.shape[1:], pick[0].astype(F32)).astype(terms.dtype)
    chunked(terms, at + 1, tn(inner, norm[...]))


def last_kernel(parts, inputs, grad_mid, gain, *refs):
    out = refs[parts]
    total = refs[0][...].astype(F32)
    for ref in refs[1:parts]:
        total = total + ref[...].astype(F32)
    back = norm_back(inputs[...].astype(F32), gain[0:1, :], total)
    out[...] = (grad_mid[...] + back).astype(BF16)


def pair_kernel(local, count, across, *refs):
    own, came, out = refs[:count], refs[count : 2 * count], refs[2 * count]
    out[pl.ds(across[0] * local, local)] = own[0][:local]
    out[pl.ds((1 - across[0]) * local, local)] = came[0][:local]
    at = 2 * local
    for n in range(count):
        first = local if n == 0 else 0
        size = own[n].shape[0] - first
        total = own[n][first:].astype(F32) + came[n][first:].astype(F32)
        out[at : at + size] = total.astype(BF16)
        at += size


def stack_kernel(pieces, place, *refs):
    out = refs[pieces]
    first = 0
    for n in range(pieces):
        size = refs[n].shape[0]
        out[place[n], first : first + size] = refs[n][...]
        first = (first + size) % out.shape[1]


def spread_kernel(widths, local, core, mine, other, *refs):
    outs, both = refs[: len(widths)], refs[len(widths)]
    both[core[0]] = mine[...]
    both[1 - core[0]] = other[...]
    for out in outs:
        out[...] = jnp.zeros_like(out)

    def step(n, _):
        pick = jnp.max(both[0, n, local - 1].astype(F32)).astype(jnp.int32)
        at, rest = 0, 2 * local
        for out, width in zip(outs, widths):
            if not width:
                for first in range(0, out.shape[2], 128):
                    term = both[0, n, rest].astype(F32) + both[1, n, rest].astype(F32)
                    out[pick, :, first : first + 128] += term
                    rest += 1
                continue
            blocks = -(-width // 128)
            for group in range(out.shape[2] // (4 * width)):
                for tok in range(4):
                    first = (group * 4 + tok) * width
                    base = (tok // 2) * local + at
                    parts = [both[tok % 2, n, base + m] for m in range(blocks)]
                    term = jnp.concatenate(parts, axis=1)[:, :width].astype(F32)
                    out[pick, :, first : first + width] += term
                at += blocks
        return 0

    lax.fori_loop(0, mine.shape[0], step, 0)


class Exchange:
    def __init__(self, size):
        self.size = size
        self.direct = size == 4
        own = lax.axis_index("tok")
        steps = jnp.arange(size, dtype=jnp.int32)
        self.order = jnp.bitwise_xor(own, steps) if self.direct else steps

    def swap(self, block, bits):
        pairs = [(n, n ^ bits) for n in range(self.size)]
        return lax.ppermute(block, "tok", pairs)

    def gather(self, block):
        if not self.direct:
            whole = lax.all_gather(block, "tok", axis=0)
            return [whole[n] for n in range(self.size)]
        across = self.swap(block, 2)
        return [block, self.swap(block, 1), across, self.swap(across, 1)]

    def hop(self, block):
        if not self.direct:
            return self.gather(block)
        return [block, self.swap(block, 1), self.swap(block, 2)]

    def land(self, parts):
        if not self.direct:
            return parts
        return parts + [self.swap(parts[2], 1)]

    def turn(self, slots):
        if not self.direct:
            whole = lax.all_to_all(jnp.stack(slots), "tok", 0, 0)
            return [whole[n] for n in range(self.size)]
        return [slots[0]] + [self.swap(slots[n], n) for n in range(1, self.size)]

    def reduce(self, slots):
        if not self.direct:
            return [lax.psum_scatter(jnp.stack(slots), "tok", scatter_dimension=0)]
        near, both = self.halve(slots)
        return [slots[0], near, self.swap(both, 2)]

    def halve(self, slots):
        near, far = self.swap(slots[1], 1), self.swap(slots[3], 1)
        return near, (slots[2].astype(F32) + far.astype(F32)).astype(slots[2].dtype)

    def slots_of(self, whole):
        return [lax.dynamic_index_in_dim(whole, self.order[n], 0, False) for n in range(self.size)]


RING = (0, 2, 4, 6, 7, 5, 3, 1)


def meet(*arrays):
    return lax.optimization_barrier(arrays)


class Ring:
    def __init__(self, block):
        self.blocks, self.shifts = [block], [0]
        self.right = self.left = block
        rows = block.shape[0]
        self.half = rows // 32 * 16 if block.ndim == 2 else rows // 2
        self.ahead = [(RING[n], RING[(n + 1) % len(RING)]) for n in range(len(RING))]
        self.behind = [(b, a) for a, b in self.ahead]

    def step(self):
        step = len(self.blocks) // 2 + 1
        if step == len(RING) // 2:
            self.right, self.left = self.right[: self.half], self.left[self.half :]
        self.right = lax.ppermute(self.right, "seq", self.ahead)
        self.left = lax.ppermute(self.left, "seq", self.behind)
        self.blocks += [self.right, self.left]
        self.shifts += [-step, step]

    def meet(self, *arrays):
        self.right, self.left, *arrays = meet(self.right, self.left, *arrays)
        if len(self.blocks) > 1:
            self.blocks[-2:] = [self.right, self.left]
        return arrays

    def came(self):
        own, size = lax.axis_index("seq"), len(RING)
        place = jnp.where(own % 2 == 0, own // 2, size - 1 - own // 2)
        came = jnp.remainder(place + jnp.array(self.shifts, jnp.int32), size)
        came = jnp.where(came < size // 2, 2 * came, 2 * (size - 1 - came) + 1)
        return came.astype(jnp.int32)


def owner_of_columns(seq, tok):
    double, single, seen = [], [], [0] * tok
    kinds = [[0, 0, 0] for _ in range(tok)]
    for s in range(seq):
        first = 3 * s + s % 2
        owner = first % seq // 2
        double.append((owner, seen[owner]))
        kinds[owner][seen[owner]] = first // seq
        seen[owner] += 1
        last = 3 * s + 2 * (1 - s % 2)
        single.append((last % seq // 2, last % 2))
        kinds[last % seq // 2][2] = last // seq
    return double, single, kinds


def body(
    tokens,
    out_grad,
    segments,
    adapter_index,
    qkv_weight,
    out_weight,
    in_weight,
    out2_weight,
    attn_gain,
    mlp_gain,
    qkv_down,
    qkv_up,
    out_down,
    out_up,
    in_down,
    in_up,
    out2_down,
    out2_up,
):
    seq, tok = lax.axis_size("seq"), lax.axis_size("tok")
    own_seq, own_tok = lax.axis_index("seq"), lax.axis_index("tok")
    move = Exchange(tok)
    fast = tok == 4 and seq == 8
    order = move.order
    adapters, rank, width = qkv_down.shape
    length = segments.shape[1]
    rows = tokens.shape[1]
    heads = HEADS // tok
    lanes = heads * HEAD_DIM
    hidden = out2_weight.shape[0]
    hidden_all = hidden * tok
    inputs, out_grad = tokens[0], out_grad[0]
    pick = adapter_index[0]

    def chosen(table, start=0, size=None):
        size = table.shape[2] if size is None else size
        return lax.dynamic_slice(table, (pick, 0, start), (1, rank, size))[0]

    gain_rows = jnp.pad(jnp.stack([attn_gain, mlp_gain]), ((0, 14), (0, width - width // tok)))
    token_all = lax.all_gather(jnp.concatenate([inputs, gain_rows], axis=0), "tok", axis=0)
    norm_one, gain = call(
        norm_kernel,
        [shape((length, width), BF16), shape((2, width), F32)],
        [token_all],
        name="norm_one",
    )
    token_all, out_grad_in = meet(token_all, out_grad)
    grad_all = lax.all_gather(out_grad_in, "tok", axis=0)
    if fast:
        unit = width // seq
        double, single, kinds = owner_of_columns(seq, tok)
        odd = (own_seq % 2) * unit
        parts = []
        for owners, start, size in ((double, odd, 2 * unit), (single, 2 * (unit - odd), unit)):
            pairs = [
                (s * tok + t, (owners[s][1] * tok + t) * tok + owners[s][0])
                for s in range(seq)
                for t in range(tok)
            ]
            piece = lax.dynamic_slice_in_dim(qkv_weight, start, size, 1)
            parts.append(lax.ppermute(piece, ("seq", "tok"), pairs))
        ring = Ring(jnp.concatenate(parts + [out_weight], axis=1))
        ring.step()
        ring.step()
        (in_piece,) = ring.meet(in_weight.T)
        pairs = [
            (s * tok + t, ((s // tok) * tok + t) * tok + s % tok)
            for s in range(seq)
            for t in range(tok)
        ]
        in_piece = lax.ppermute(in_piece, ("seq", "tok"), pairs)
        ring.step()
        norm_one, gain = ring.meet(norm_one, gain)
        ring.step()
        mlp_piece = jnp.concatenate([in_piece, out2_weight], axis=1)
        (mlp_piece,) = ring.meet(mlp_piece)
        qkv_pieces = ring.blocks
        place = jnp.concatenate([ring.came(), jnp.array(kinds, jnp.int32)[own_tok]])
        mlp_ring = Ring(mlp_piece)
        mlp_ring.step()
    else:

        def columns(weight, count):
            block = lax.all_gather(weight, "seq", axis=1, tiled=True)
            split = block.reshape(block.shape[0], count, tok, -1).transpose(2, 1, 0, 3)
            turned = lax.all_to_all(split, "tok", 0, 0)
            return turned.transpose(1, 0, 2, 3).reshape(count, width, -1)

        qkv_pieces = [columns(qkv_weight, 3)]
        place = jnp.zeros((1,), jnp.int32)
        own_out = lax.all_gather(out_weight, "seq", axis=1, tiled=True)
        mlp_weights = [
            columns(in_weight, 2).transpose(0, 2, 1),
            lax.all_gather(out2_weight, "seq", axis=1, tiled=True),
        ]

    down_one = chosen(qkv_down)
    up_one = jnp.stack([chosen(qkv_up, n * width + own_tok * lanes, lanes) for n in range(3)])
    down_attn = chosen(out_down).reshape(rank, tok, lanes).transpose(1, 0, 2)
    up_attn = chosen(out_up)
    down_two = chosen(in_down)
    up_two = jnp.stack([chosen(in_up, n * hidden_all + own_tok * hidden, hidden) for n in range(2)])
    down_last = chosen(out2_down, own_tok * hidden, hidden)
    up_last = chosen(out2_up)
    exponent = jnp.arange(0, HEAD_DIM, 2).astype(F32) / HEAD_DIM
    inverse = 1.0 / THETA**exponent
    phases = jnp.arange(length).astype(F32)[:, None] * jnp.tile(inverse, 4)[None, :]
    sign = jnp.where(jnp.arange(2 * HEAD_DIM) % HEAD_DIM < HEAD_DIM // 2, -1.0, 1.0)
    cosine, sine = jnp.cos(phases), jnp.sin(phases) * sign[None, :]
    seg_col = segments.reshape(length, 1)

    query, key, value, w_qkv, *own_row = call(
        functools.partial(qkv_kernel, len(qkv_pieces), rows),
        [shape((length, lanes), BF16)] * 3
        + [shape((3, width, lanes), BF16)]
        + [shape((lanes, width), BF16)] * fast,
        [place, norm_one, down_one, up_one, cosine, sine] + qkv_pieces,
        smem=(0,),
        name="qkv",
    )
    if fast:
        query, key, value = mlp_ring.meet(query, key, value)
        mlp_ring.step()
    out_parts = move.hop(own_row[0] if fast else own_out)
    *attn_slots, log_total = call(
        functools.partial(attend_kernel, tok),
        [shape((rows, lanes), BF16)] * tok + [shape((heads, length), F32)],
        [order, query, key, value, seg_col, segments],
        smem=(0,),
        scratch=[pltpu.VMEM((lanes, length), BF16), pltpu.VMEM((length, rows), F32)],
        name="attend",
    )
    attn_slots, out_parts = meet(attn_slots, out_parts)
    if fast:
        attn_slots = mlp_ring.meet(*attn_slots)
        mlp_ring.step()
    attn = move.turn(attn_slots)
    out_weights = move.land(out_parts)
    if fast:
        attn = mlp_ring.meet(*attn)
        mlp_ring.step()
        mlp_weights, mlp_came = mlp_ring.blocks, mlp_ring.came()
    else:
        mlp_came = place
    middle, norm_two, narrow_attn = call(
        functools.partial(out_kernel, tok),
        [shape((rows, width), F32), shape((rows, width), BF16), shape((rows, rank), BF16)],
        [order, inputs, gain, down_attn, up_attn] + attn + out_weights,
        smem=(0,),
        name="out",
    )
    norm_slots = move.gather(norm_two)
    pieces = lambda columns: -(-columns // 128)
    early_local, late_local = 3 * pieces(hidden) + 1, 3 * pieces(lanes) + 1
    wide = pieces(width)
    w_in, w_out, grad_act = call(
        functools.partial(mlp_pre_kernel, fast),
        [
            shape((2, hidden, width), BF16),
            shape((hidden, width), BF16),
            shape((tok, rows, hidden), F32),
        ],
        [order, mlp_came, down_two, up_two, down_last, up_last, grad_all] + mlp_weights,
        smem=(0, 1),
        name="mlp_pre",
    )
    back_slots, acts, grads_z = [], [], []
    for first in range(0, tok, 2):
        *backs, act, grad_z = call(
            functools.partial(mlp_kernel, 2, first),
            [shape((rows, width), BF16)] * 2
            + [shape((2, rows, hidden), BF16), shape((2, 2, rows, hidden), BF16)],
            [w_in, grad_act] + norm_slots[first : first + 2],
            name="mlp",
        )
        back_slots += backs
        acts.append(act)
        grads_z.append(grad_z)
    pieces = lambda columns: -(-columns // 128)
    early_local, late_local = 3 * pieces(hidden) + 1, 3 * pieces(lanes) + 1
    wide = pieces(width)
    back_two = move.reduce(back_slots)
    grad_mid, *rest = call(
        functools.partial(out_back_kernel, tok, len(back_two)),
        [shape((rows, width), F32)]
        + [shape((rows, lanes), BF16)] * tok
        + [shape((2 * wide, rank, 128), BF16)],
        [order, middle, out_grad, gain, down_attn, up_attn, narrow_attn]
        + back_two
        + attn
        + out_weights,
        smem=(0,),
        scratch=[pltpu.VMEM((tok, rank, lanes), F32)],
        name="out_back",
    )
    attn_grads, out_terms = move.turn(rest[:tok]), rest[tok]
    out_slots, early = [], []
    for first in range(0, tok, 4):
        pair = slice(first // 2, first // 2 + 2)
        *outs, terms = call(
            functools.partial(mlp_post_kernel, 4, first),
            [shape((rows, width), BF16)] * 4
            + [shape((early_local + 2 * wide, rank, 128), BF16 if fast else F32)],
            [order, adapter_index, down_two, up_two, down_last, up_last, w_out]
            + acts[pair]
            + grads_z[pair]
            + [grad_all]
            + norm_slots[first : first + 4],
            smem=(0, 1),
            scratch=[
                pltpu.VMEM((4, rows, width), BF16),
                pltpu.VMEM((4, rows, hidden), BF16),
                pltpu.VMEM((2, 4, rows, hidden), BF16),
                pltpu.VMEM((rank, width), F32),
                pltpu.VMEM((2, rank, hidden), F32),
                pltpu.VMEM((rank, hidden), F32),
                pltpu.VMEM((rank, width), F32),
            ],
            name="mlp_post",
        )
        out_slots += outs
        early.append(terms)
    early = sum(early[1:], early[0])
    *one_slots, grad_qkv = call(
        functools.partial(attend_back_kernel, tok),
        [shape((rows, width), BF16)] * tok + [shape((3, length, lanes), BF16)],
        [order, query, key, value, seg_col, segments, log_total, cosine, sine, w_qkv] + attn_grads,
        smem=(0,),
        scratch=[
            pltpu.VMEM((lanes, length), BF16),
            pltpu.VMEM((length, rows), F32),
            pltpu.VMEM((length, lanes), BF16),
            pltpu.VMEM((length, lanes), F32),
            pltpu.VMEM((length, lanes), F32),
            pltpu.VMEM((length, lanes), F32),
        ],
        name="attend_back",
    )
    late = call(
        qkv_terms_kernel,
        [shape((late_local + wide, rank, 128), BF16)],
        [adapter_index, norm_one, grad_qkv, down_one, up_one],
        smem=(0,),
        name="qkv_terms",
    )[0]
    out_sums = move.reduce(out_slots)
    layer_out = (middle + sum(part.astype(F32) for part in out_sums)).astype(BF16)

    def last_of(back_one):
        return call(
            functools.partial(last_kernel, len(back_one)),
            [shape((rows, width), BF16)],
            [inputs, grad_mid, gain] + back_one,
            name="last",
        )[0]

    grads = lambda columns: shape((adapters, rank, columns), F32)
    if fast:
        across, core = (own_tok // 2).reshape(1), (own_tok % 2).reshape(1)

        def paired(local, terms, came):
            size = sum(term.shape[0] for term in terms) + local
            return call(
                functools.partial(pair_kernel, local, len(terms)),
                [shape((size, rank, 128), BF16)],
                [across] + terms + came,
                smem=(0,),
                name="pair",
            )[0]

        def spread(whole, local, widths, columns):
            return call(
                functools.partial(spread_kernel, widths, local),
                [grads(size) for size in columns],
                [core, whole, move.swap(whole, 1)],
                smem=(0,),
                scratch=[pltpu.VMEM((2,) + whole.shape, BF16)],
                name="spread",
            )

        terms = [early, out_terms]
        early = paired(early_local, terms, [move.swap(term, 2) for term in terms])
        early = lax.all_gather(early, "seq", axis=0)
        near, both = move.halve(one_slots)
        both, late_came = meet(both, move.swap(late, 2))
        back_one = [one_slots[0], near, move.swap(both, 2)]
        ring = Ring(paired(late_local, [late], [late_came]))
        ring.step()
        ring.step()
        early, back_one[2] = ring.meet(early, back_one[2])
        ring.step()
        (
            in_up_grad,
            out2_down_grad,
            in_down_grad,
            out2_up_grad,
            out_down_grad,
            out_up_grad,
        ) = spread(
            early,
            early_local,
            (hidden, hidden, 0, 0, 0, 0),
            (2 * hidden_all, hidden_all) + (width,) * 4,
        )
        (in_up_grad,) = ring.meet(in_up_grad)
        ring.step()
        (input_grad,) = ring.meet(last_of(back_one))
        late = call(
            functools.partial(stack_kernel, len(ring.blocks)),
            [shape((seq,) + ring.blocks[0].shape, BF16)],
            [ring.came()] + ring.blocks,
            smem=(0,),
            name="stack",
        )[0]
        qkv_up_grad, qkv_down_grad = spread(late, late_local, (lanes, 0), (3 * width, width))
    else:
        input_grad = last_of(move.reduce(one_slots))
        picked = (pick == jnp.arange(adapters)).astype(F32)[:, None, None]

        def term(blocks, columns):
            return blocks.astype(F32).transpose(1, 0, 2).reshape(rank, -1)[:, :columns]

        def placed(terms, first, groups, columns):
            total = jnp.zeros((rank, groups * tok * columns), F32)
            for group in range(groups):
                at = first + group * pieces(columns)
                part = term(terms[at : at + pieces(columns)], columns)
                start = (group * tok + own_tok) * columns
                total = lax.dynamic_update_slice(total, part, (0, start))
            return total

        whole = lambda terms, at: term(terms[at : at + wide], width)
        sums = (
            whole(late, late_local),
            placed(late, 0, 3, lanes),
            whole(out_terms, 0),
            whole(out_terms, wide),
            whole(early, early_local),
            placed(early, 0, 2, hidden),
            placed(early, 2 * pieces(hidden), 1, hidden),
            whole(early, early_local + wide),
        )
        summed = lax.psum(tuple(picked * part[None] for part in sums), ("seq", "tok"))
        qkv_down_grad, qkv_up_grad, out_down_grad, out_up_grad = summed[:4]
        in_down_grad, in_up_grad, out2_down_grad, out2_up_grad = summed[4:]
    return (
        layer_out[None],
        input_grad[None],
        qkv_down_grad,
        qkv_up_grad,
        out_down_grad,
        out_up_grad,
        in_down_grad,
        in_up_grad,
        out2_down_grad,
        out2_up_grad,
    )


def solution(mesh):
    grid = P("tok", "seq")
    split = P("seq", "tok", None)
    return jax.shard_map(
        body,
        mesh=mesh,
        in_specs=(split, split, P("seq", None), P("seq"), grid, grid, grid, grid, P("tok"), P("tok"))
        + (P(),) * 8,
        out_specs=(split, split) + (P(),) * 8,
        check_vma=False,
    )
```

```python
import functools

import jax
import jax.numpy as jnp
from jax import lax
from jax.experimental import pallas as pl
from jax.experimental.pallas import tpu as pltpu
from jax.sharding import PartitionSpec as P

HEADS = 16
HEAD_DIM = 64
EPS = 1e-05
THETA = 160000.0
F32 = jnp.float32
BF16 = jnp.bfloat16
MIB = 1024 * 1024
RING = (0, 2, 4, 6, 7, 5, 3, 1)


def nn(a, b):
    return lax.dot_general(a, b, (((1,), (0,)), ((), ())), preferred_element_type=F32)


def nt(a, b):
    return lax.dot_general(a, b, (((1,), (1,)), ((), ())), preferred_element_type=F32)


def tn(a, b):
    return lax.dot_general(a, b, (((0,), (0,)), ((), ())), preferred_element_type=F32)


def shape(dims, dtype):
    return jax.ShapeDtypeStruct(tuple(dims), dtype)


PIECE = 256 * 1024


def cuts(dims, item):
    size = item
    for n in dims:
        size *= n
    if size <= PIECE * 3 // 2 or len(dims) == 1:
        return [()]
    if len(dims) == 2:
        step = max(dims[0] * PIECE // size // 16 * 16, 16)
        return [(pl.ds(n, min(step, dims[0] - n)),) for n in range(0, dims[0], step)]
    return [(n,) + rest for n in range(dims[0]) for rest in cuts(dims[1:], item)]


def start_copies(source, target, semaphore):
    for at in cuts(target.shape, target.dtype.itemsize):
        one, two = (source.at[at], target.at[at]) if at else (source, target)
        pltpu.make_async_copy(one, two, semaphore).start()
    return pltpu.make_async_copy(source, target, semaphore)


class Late:
    def __init__(self, source, target, semaphore):
        self.target, self.there = target, False
        self.copy = start_copies(source, target, semaphore)

    def get(self):
        if not self.there:
            self.copy.wait()
            self.there = True
        return self.target


class Here:
    def __init__(self, ref):
        self.ref = ref

    def get(self):
        return self.ref

    def send(self):
        pass


class Early:
    def __init__(self, target, source, semaphore):
        self.ref, self.sent = source, False
        self.ends = (source, target, semaphore)

    def send(self):
        if not self.sent:
            self.copy = start_copies(*self.ends)
            self.sent = True


class Pick:
    def __init__(self, table, pick, start=None, size=None):
        self.table, self.pick = table, pick
        self.start, self.size = start, table.shape[2] if size is None else size


def call(kernel, out_shape, args, scratch=(), smem=(), early=(), name=None):
    picks = {n: a for n, a in enumerate(args) if isinstance(a, Pick)}
    operands = [a.table if isinstance(a, Pick) else a for a in args]
    chosen = [next(iter(picks.values())).pick] if picks else []
    late = list(picks)
    buffers = [
        pltpu.VMEM((args[n].table.shape[1], args[n].size), args[n].table.dtype) for n in late
    ]
    buffers += [pltpu.VMEM(out_shape[n].shape, out_shape[n].dtype) for n in early]
    first_in = len(chosen)

    def body(*refs):
        pick, refs = refs[:first_in], refs[first_in:]
        ins, refs = list(refs[: len(args)]), refs[len(args) :]
        outs, refs = list(refs[: len(out_shape)]), refs[len(out_shape) :]
        own, refs = refs[: len(scratch)], refs[len(scratch) :]
        semaphores = refs[-1]
        for at, n in enumerate(late):
            entry = picks[n]
            columns = slice(None) if entry.start is None else pl.ds(entry.start(), entry.size)
            source = ins[n].at[pick[0][0], :, columns]
            ins[n] = Late(source, refs[at], semaphores.at[at])
        for n in range(len(args)):
            if n not in picks and n not in smem:
                ins[n] = Here(ins[n])
        for at, n in enumerate(early, len(late)):
            outs[n] = Early(outs[n], refs[at], semaphores.at[at])
        kernel(*ins, *outs, *own)
        for n in late:
            ins[n].get()
        for n in early:
            outs[n].send()
            outs[n].copy.wait()

    spaces = [pltpu.SMEM] * first_in + [
        pltpu.SMEM if n in smem else pl.ANY if n in picks else pltpu.VMEM
        for n in range(len(args))
    ]
    return pl.pallas_call(
        body,
        out_shape=list(out_shape),
        in_specs=[pl.BlockSpec(memory_space=space) for space in spaces],
        out_specs=[
            pl.BlockSpec(memory_space=pl.ANY if n in early else pltpu.VMEM)
            for n in range(len(out_shape))
        ],
        scratch_shapes=list(scratch)
        + buffers
        + [pltpu.SemaphoreType.DMA((max(len(late) + len(early), 1),))],
        compiler_params=pltpu.CompilerParams(vmem_limit_bytes=60 * MIB),
        cost_estimate=pl.CostEstimate(flops=1, bytes_accessed=1, transcendentals=0),
        name=name,
    )(*chosen, *operands)


def owner(n, direct):
    return jnp.bitwise_xor(lax.axis_index("tok"), n) if direct else n


def rows_of(n, size):
    if isinstance(n, int):
        return pl.ds(n * size, size)
    return pl.ds(pl.multiple_of(n * size, size), size)


def came_from(n):
    own, size = lax.axis_index("seq"), len(RING)
    place = jnp.where(lax.rem(own, 2) == 0, own // 2, size - 1 - own // 2)
    shift = (0, -1, 1, -2, 2, -3, 3, -4, 4)[n]
    came = lax.rem(place + shift + size, size)
    return jnp.where(came < size // 2, 2 * came, 2 * (size - 1 - came) + 1)


def to_slot(refs, index, value):
    for n, ref in enumerate(refs):

        @pl.when(index == n)
        def _(ref=ref):
            ref[...] = value


def normalized(rows):
    mean = jnp.mean(rows, axis=-1, keepdims=True)
    centered = rows - mean
    scale = lax.rsqrt(jnp.mean(centered * centered, axis=-1, keepdims=True) + EPS)
    return centered * scale, scale


def norm_back(rows, gain, grad):
    unit, scale = normalized(rows)
    weighted = grad * gain
    first = jnp.mean(weighted, axis=-1, keepdims=True)
    second = jnp.mean(weighted * unit, axis=-1, keepdims=True)
    return (weighted - first - unit * second) * scale


def swapped(rows):
    width = rows.shape[1]
    if width % 128:
        half = HEAD_DIM // 2
        parts = []
        for start in range(0, width, HEAD_DIM):
            parts += [rows[:, start + half : start + HEAD_DIM], rows[:, start : start + half]]
        return jnp.concatenate(parts, axis=1)
    lane = lax.broadcasted_iota(jnp.int32, rows.shape, 1)
    ahead = pltpu.roll(rows, width - HEAD_DIM // 2, 1)
    behind = pltpu.roll(rows, HEAD_DIM // 2, 1)
    return jnp.where(lane % HEAD_DIM < HEAD_DIM // 2, ahead, behind)


def widened(table, width):
    if width <= table.shape[1]:
        return table[:, :width]
    return jnp.concatenate([table] * (width // table.shape[1]), axis=1)


def head_part(rows, head):
    lane = lax.broadcasted_iota(jnp.int32, rows.shape, 1)
    return jnp.where(lane // HEAD_DIM == head, rows, jnp.zeros_like(rows))


def chunked(ref, base, value):
    count = -(-value.shape[1] // 128)
    for n in range(count):
        part = value[:, n * 128 : (n + 1) * 128].astype(ref.dtype)
        if part.shape[1] < 128:
            ref[base + n] = jnp.zeros(ref.shape[1:], ref.dtype)
            ref[base + n, :, : part.shape[1]] = part
        else:
            ref[base + n] = part
    return base + count


def halves(keep, at, send, first, value):
    core = lax.rem(lax.axis_index("tok"), 2)
    half = value.shape[1] // 256
    for n in range(2 * half):
        part = value[:, n * 128 : (n + 1) * 128].astype(keep.dtype)

        @pl.when(core == n // half)
        def _(part=part, n=n):
            keep[at + n % half] = part

        @pl.when(core != n // half)
        def _(part=part, n=n):
            send[first + n % half] = part


def labelled(ref, at, pick):
    ref[at] = jnp.full(ref.shape[1:], pick[0].astype(F32)).astype(ref.dtype)


def document_range(block, rows, seg_scalar, seg_row):
    first = seg_scalar[0, block * rows].astype(F32)
    last = seg_scalar[0, block * rows + rows - 1].astype(F32)
    below = jnp.sum(jnp.where(seg_row < first, 1.0, 0.0)).astype(jnp.int32)
    upto = jnp.sum(jnp.where(seg_row <= last, 1.0, 0.0)).astype(jnp.int32)
    return below // rows, (upto + rows - 1) // rows


def prepare_kernel(tokens, gain_one, gain_two, weight, token_out, double, single):
    weight, odd = weight.get(), lax.rem(lax.axis_index("seq"), 2)
    unit = single.shape[1]

    @pl.when(odd == 0)
    def _():
        double[...] = weight[:, : 2 * unit]
        single[...] = weight[:, 2 * unit :]

    @pl.when(odd == 1)
    def _():
        double[...] = weight[:, unit:]
        single[...] = weight[:, :unit]

    tokens = tokens.get()
    rows, part = tokens.shape[0], gain_one.get().shape[0]
    token_out[:rows] = tokens[...]
    token_out[rows:] = jnp.zeros((16, tokens.shape[1]), BF16)
    both = [gain.get()[...].astype(F32).reshape(1, part) for gain in (gain_one, gain_two)]
    token_out[rows : rows + 2, :part] = jnp.concatenate(both, axis=0).astype(BF16)


def adapters_kernel(tok, *refs):
    tables, outs = refs[:8], refs[8:]
    down_one, up_one, down_attn, up_attn, down_two, up_two, down_last, up_last = outs
    for n in (1, 5, 6):
        tables[n].get()
    for table, out in ((0, down_one), (2, down_attn), (3, up_attn), (4, down_two), (7, up_last)):
        out[...] = tables[table].get()[...]
    own = lax.axis_index("tok")
    for n in range(tok):

        @pl.when(own == n)
        def _(n=n):
            down_last[...] = tables[6].get()[:, columns_of(n, 0, down_last.shape[1], tok)]
            for kind in range(3):
                size = up_one.shape[2]
                up_one[kind] = tables[1].get()[:, columns_of(n, kind, size, tok)]
            for kind in range(2):
                size = up_two.shape[2]
                up_two[kind] = tables[5].get()[:, columns_of(n, kind, size, tok)]


def columns_of(own, group, size, tok):
    start = (group * tok + own) * size
    return slice(start, start + size)


def qkv_kernel(pieces, kinds, tokens, down, ups, cosine, sine, *refs):
    weights, refs = refs[:pieces], refs[pieces:]
    norm, gain, query, key, value, whole = refs[:6]
    width = query.shape[1]
    if pieces == 1:
        whole[...] = weights[0].get()[...]
    else:
        out_weight = refs[6]
        unit = width // 2
        own = lax.axis_index("tok")
        first = 0
        for n in range(pieces):
            piece = weights[n].get()
            depth = piece.shape[0]
            spot = came_from(n)
            half, part = spot // 4, lax.rem(spot, 4)
            down_at = pl.ds(pl.multiple_of(part * width + first, depth), depth)
            double, single = kinds[3 * own + half], kinds[3 * own + 2]
            whole[double, down_at, :] = piece[:, :width]
            across = pl.ds(pl.multiple_of(half * unit, unit), unit)
            whole[single, down_at, across] = piece[:, width : width + unit]
            across = pl.ds(pl.multiple_of(spot * unit, unit), unit)
            out_weight[first : first + depth, across] = piece[:, width + unit :]
            first = (first + depth) % width
    for kind in range(3):
        product = tn(down.get()[...], ups.get()[kind])
        whole[kind] = (whole[kind].astype(F32) + product).astype(BF16)
    tokens, cosine, sine = tokens.get(), cosine.get(), sine.get()
    count, block = tokens.shape[0], tokens.shape[1] - 16
    for n in range(count):
        part = gain.shape[1] // count
        gain[:, n * part : (n + 1) * part] = tokens[n, block:, :part].astype(F32)[:2]

    def step(n, _):
        at = rows_of(n, block)
        unit, _ = normalized(tokens[n, :block].astype(F32))
        rows = (unit * gain[0:1, :]).astype(BF16)
        norm[at, :] = rows
        cos, sin = widened(cosine[at, :], width), widened(sine[at, :], width)
        for kind, out in enumerate((query, key, value)):
            part = nn(rows, whole[kind])
            if kind < 2:
                part = part * cos + swapped(part) * sin
            if kind == 0:
                part = part.astype(BF16).astype(F32) * 0.125
            out[at, :] = part.astype(BF16)
        return 0

    lax.fori_loop(0, count, step, 0)


def attend_kernel(count, direct, seg_scalar, query, key, value, segments, *refs):
    outs, (log_total, mixed_t, value_t, seg_t) = refs[:count], refs[count:]
    segments = segments.get()
    seg_row = segments[...].astype(F32)
    seg_t[...] = jnp.broadcast_to(seg_row, (128, seg_row.shape[1])).T
    query, key, value = query.get(), key.get(), value.get()
    block = outs[0].shape[0]
    width = query.shape[1]
    heads = width // HEAD_DIM
    value_t[...] = value[...].T
    parts = [slice(head * HEAD_DIM, (head + 1) * HEAD_DIM) for head in range(heads)]

    def step(n, _):
        place = owner(n, direct)
        at = rows_of(place, block)
        rows = query[at, :]
        own = [head_part(rows, head) for head in range(heads)]
        seg_here = segments[:, at].astype(F32)

        def against(m, carry):
            tops, sums, mixed = carry
            keys = rows_of(m, block)
            column = widened(seg_t[keys, :], block)
            bias = jnp.where(column == seg_here, 0.0, -1e30)
            near = key[keys, :]
            scores = [nt(near, part) + bias for part in own]
            now = [
                jnp.maximum(top, jnp.max(part, axis=0, keepdims=True))
                for top, part in zip(tops, scores)
            ]
            raised = [jnp.exp(part - top) for part, top in zip(scores, now)]
            scale = [jnp.exp(before - top) for before, top in zip(tops, now)]
            added = [nn(value_t[part, keys], up.astype(BF16)) for part, up in zip(parts, raised)]
            sums = [
                total * by + jnp.sum(up, axis=0, keepdims=True)
                for total, by, up in zip(sums, scale, raised)
            ]
            mixed = [old * by + new for old, by, new in zip(mixed, scale, added)]
            return now, sums, mixed

        start = (
            [jnp.full((1, block), -2e30, F32)] * heads,
            [jnp.zeros((1, block), F32)] * heads,
            [jnp.zeros((HEAD_DIM, block), F32)] * heads,
        )
        first, last = document_range(place, block, seg_scalar, seg_row)
        tops, sums, mixed = lax.fori_loop(first, last, against, start)
        for head in range(heads):
            log_total[head : head + 1, at] = tops[head] + jnp.log(sums[head])
            mixed_t[n, parts[head], :] = mixed[head] * (1.0 / sums[head])
        to_slot(outs, n, mixed_t[n].T.astype(BF16))
        return 0

    lax.fori_loop(0, count, step, 0)


def features(n, width, direct):
    if not direct:
        return slice(n * width, (n + 1) * width)
    return pl.ds(pl.multiple_of(owner(n, direct) * width, width), width)


def out_kernel(count, direct, inputs, gain, down, up, *refs):
    attn, weights = refs[:count], refs[count : 2 * count]
    middle, norm, narrow = refs[2 * count :]
    down = down.get()
    total = inputs.get()[...].astype(F32)
    thin = jnp.zeros(narrow.shape, F32)
    for n in range(count):
        rows = attn[n].get()[...]
        total = total + nn(rows, weights[n].get()[...])
        thin = thin + nt(rows, down[:, features(n, rows.shape[1], direct)])
    thin = thin.astype(BF16)
    total = total + nn(thin, up.get()[...])
    middle[...] = total
    narrow[...] = thin
    norm[...] = (normalized(total)[0] * gain.get()[1:2, :]).astype(BF16)


def mlp_pre_kernel(packed, direct, down_in, up_in, down_out, up_out, grads, *refs):
    pieces = 9 if packed else 2
    weights, refs = refs[:pieces], refs[pieces:]
    w_in, w_out, grad_early, grad_late = refs
    hidden, width = w_out.shape
    if packed:
        depth, thin = width // 4, width // 8
        first = 0
        for n in range(pieces):
            piece = weights[n].get()
            rows = slice(first, first + piece.shape[0])
            spot = came_from(n)
            across = pl.ds(pl.multiple_of(lax.rem(spot, 4) * depth, depth), depth)
            w_in[spot // 4, rows, across] = piece[:, :depth]
            across = pl.ds(pl.multiple_of(spot * thin, thin), thin)
            w_out[rows, across] = piece[:, depth:]
            first = rows.stop % hidden
    else:
        w_in[...] = weights[0].get()[...]
        w_out[...] = weights[1].get()[...]
    for n in range(2):
        w_in[n] = (w_in[n].astype(F32) + tn(up_in.get()[n], down_in.get()[...])).astype(BF16)
    w_out[...] = (w_out[...].astype(F32) + tn(down_out.get()[...], up_out.get()[...])).astype(BF16)
    grads = grads.get()
    for n in range(grads.shape[0]):
        target = grad_early if n < 2 else grad_late
        target[n if n < 2 else n - 2] = nt(grads[owner(n, direct)], w_out[...])


def mlp_kernel(count, first, w_in, grad_act, *refs):
    norms, backs, (act_out, grad_out) = refs[:count], refs[count : 2 * count], refs[2 * count :]
    w_in, grad_act = w_in.get(), grad_act.get()
    for n in range(count):
        norm = norms[n].get()[...]
        inputs, gate = nt(norm, w_in[0]), nt(norm, w_in[1])
        phi = 0.5 + 0.5 * lax.erf(inputs * (0.5**0.5))
        gelu = inputs * phi
        act_out[n] = (gelu * gate).astype(BF16)
        back_act = grad_act[first + n]
        slope = phi + inputs * (jnp.exp(-0.5 * inputs * inputs) * 0.3989422804014327)
        grad_inputs = (back_act * gate * slope).astype(BF16)
        grad_gate = (back_act * gelu).astype(BF16)
        grad_out[0, n] = grad_inputs
        grad_out[1, n] = grad_gate
        backs[n][...] = (nn(grad_inputs, w_in[0]) + nn(grad_gate, w_in[1])).astype(BF16)


def mlp_terms_kernel(count, first, direct, pick, down_in, up_in, down_out, up_out, *refs):
    acts, grads, out_grad, refs = refs[:2], refs[2:4], refs[4], refs[5:]
    norms, terms = refs[:count], refs[count]
    down_in_grad = down_out_grad = up_out_grad = 0.0
    up_in_grad = [0.0, 0.0]
    down_in, up_in, down_out, up_out = down_in.get(), up_in.get(), down_out.get(), up_out.get()
    for n in range(count):
        norm = norms[n].get()[...]
        narrow = nt(norm, down_in[...]).astype(BF16)
        back = [grads[n // 2].get()[h, n % 2] for h in range(2)]
        inner_in = (nt(back[0], up_in[0]) + nt(back[1], up_in[1])).astype(BF16)
        down_in_grad = down_in_grad + tn(inner_in, norm)
        for h in range(2):
            up_in_grad[h] = up_in_grad[h] + tn(narrow, back[h])
        act = acts[n // 2].get()[n % 2]
        grad = out_grad.get()[owner(first + n, direct)]
        narrow_two = nt(act, down_out[...]).astype(BF16)
        inner = nt(grad, up_out[...]).astype(BF16)
        down_out_grad = down_out_grad + tn(inner, act)
        up_out_grad = up_out_grad + tn(narrow_two, grad)
    at = chunked(terms, 0, up_in_grad[0])
    at = chunked(terms, at, up_in_grad[1])
    at = chunked(terms, at, down_out_grad)
    labelled(terms, at, pick)
    at = chunked(terms, at + 1, down_in_grad)
    chunked(terms, at, up_out_grad)


def mlp_out_kernel(count, w_out, *refs):
    acts, outs = refs[: count // 2], refs[count // 2 :]
    w_out = w_out.get()
    for n in range(count):
        outs[n].ref[...] = nn(acts[n // 2].get()[n % 2], w_out[...]).astype(BF16)
        outs[n].send()


def out_back_kernel(count, parts, direct, middle, out_grad, gain, down, up, narrow, *refs):
    back, refs = refs[:parts], refs[parts:]
    attn, weights = refs[:count], refs[count : 2 * count]
    grad_mid, refs = refs[2 * count], refs[2 * count + 1 :]
    slots, (keep, send, down_grad) = refs[:count], refs[count:]
    total = sum(ref.get()[...].astype(F32) for ref in back)
    grad = out_grad.get()[...].astype(F32)
    grad = grad + norm_back(middle.get()[...], gain.get()[1:2, :], total)
    grad_mid[...] = grad
    low = grad.astype(BF16)
    down = down.get()
    inner = nt(low, up.get()[...]).astype(BF16)
    for n in range(count):
        rows = attn[n].get()[...]
        own = features(n, rows.shape[1], direct)
        slots[n][...] = (nt(low, weights[n].get()[...]) + nn(inner, down[:, own])).astype(BF16)
        down_grad[:, own] = tn(inner, rows)
    half = grad.shape[1] // 256
    halves(keep, half, send, half, tn(narrow.get()[...], low))
    halves(keep, 0, send, 0, down_grad[...])


def attend_back_kernel(
    count, direct, seg_scalar, pick, query, key, value, segments, log_total, mixed_t, cosine, sine,
    down, ups, norm, *refs
):
    grads, (grad_qkv, keep, send) = refs[:count], refs[count : count + 3]
    key_t, seg_t, grad_q, grad_k, grad_v, query_t, grad_all = refs[count + 3 :]
    segments = segments.get()
    seg_row = segments[...].astype(F32)
    seg_t[...] = jnp.broadcast_to(seg_row, (128, seg_row.shape[1])).T
    for ref in (grad_k, grad_v):
        ref[...] = jnp.zeros_like(ref)
    query, key, value = query.get(), key.get(), value.get()
    log_total, mixed_t = log_total.get(), mixed_t.get()
    block = grads[0].get().shape[0]
    width = query.shape[1]
    heads = width // HEAD_DIM
    key_t[...] = key[...].T
    for n in range(count):
        grad_all[n] = grads[n].get()[...]
    parts = [slice(head * HEAD_DIM, (head + 1) * HEAD_DIM) for head in range(heads)]

    def step(n, _):
        place = owner(n, direct)
        at = rows_of(place, block)
        rows, grad = query[at, :], grad_all[n]
        own = [head_part(rows, head) for head in range(heads)]
        own_grad = [head_part(grad, head) for head in range(heads)]
        product = grad.astype(F32).T * mixed_t[n]
        dots = [jnp.sum(product[part], axis=0, keepdims=True) for part in parts]
        query_t[...] = jnp.zeros_like(query_t)
        seg_here = segments[:, at].astype(F32)

        def against(m, _):
            keys = rows_of(m, block)
            column = widened(seg_t[keys, :], block)
            bias = jnp.where(column == seg_here, 0.0, -1e30)
            near, near_value = key[keys, :], value[keys, :]
            probs = [
                jnp.exp(nt(near, own[head]) + bias - log_total[head : head + 1, at])
                for head in range(heads)
            ]
            grad_probs = [nt(near_value, part) for part in own_grad]
            grad_s = [
                (prob * (grad_prob - dot)).astype(BF16)
                for prob, grad_prob, dot in zip(probs, grad_probs, dots)
            ]
            sum_v = sum(nn(prob.astype(BF16), part) for prob, part in zip(probs, own_grad))
            sum_k = sum(nn(part, mine) for part, mine in zip(grad_s, own))
            for head in range(heads):
                query_t[parts[head], :] += nn(key_t[parts[head], keys], grad_s[head])
            grad_k[keys, :] += sum_k
            grad_v[keys, :] += sum_v
            return 0

        first, last = document_range(place, block, seg_scalar, seg_row)
        lax.fori_loop(first, last, against, 0)
        grad_q[at, :] = query_t[...].T * 0.125
        return 0

    lax.fori_loop(0, count, step, 0)
    cosine, sine = cosine.get(), sine.get()

    def finish(n, _):
        at = rows_of(n, block)
        cos, sin = widened(cosine[at, :], width), widened(sine[at, :], width)
        for kind, ref in enumerate((grad_q, grad_k)):
            part = ref[at, :]
            grad_qkv[kind, at, :] = (part * cos - swapped(part) * sin).astype(BF16)
        grad_qkv[2, at, :] = grad_v[at, :].astype(BF16)
        return 0

    lax.fori_loop(0, count, finish, 0)
    norm = norm.get()
    inner = sum(nt(grad_qkv[kind], ups.get()[kind]) for kind in range(3))
    narrow = nt(norm[...], down.get()[...]).astype(BF16)
    at = 0
    for kind in range(3):
        at = chunked(keep, at, tn(narrow, grad_qkv[kind]))
    labelled(keep, at, pick)
    halves(keep, at + 1, send, 0, tn(inner.astype(BF16), norm[...]))


def qkv_back_kernel(count, direct, grad_qkv, weights, *outs):
    block = outs[0].ref.shape[0]
    grad_qkv, weights = grad_qkv.get(), weights.get()
    for n in list(range(1, count, 2)) + list(range(0, count, 2)):
        at = rows_of(owner(n, direct), block)
        total = sum(nt(grad_qkv[kind, at, :], weights[kind]) for kind in range(3))
        outs[n].ref[...] = total.astype(BF16)
        outs[n].send()


def last_kernel(parts, out_parts, inputs, grad_mid, middle, gain, *refs):
    backs, outs = refs[:parts], refs[parts : parts + out_parts]
    input_grad, layer_out = refs[parts + out_parts :]
    total = middle.get()[...] + sum(ref.get()[...].astype(F32) for ref in outs)
    layer_out.ref[...] = total.astype(BF16)
    layer_out.send()
    total = sum(ref.get()[...].astype(F32) for ref in backs)
    back = norm_back(inputs.get()[...].astype(F32), gain.get()[0:1, :], total)
    input_grad.ref[...] = (grad_mid.get()[...] + back).astype(BF16)


def add_kernel(one, two, out):
    out[...] = (one.get()[...].astype(F32) + two.get()[...].astype(F32)).astype(out.dtype)


def pair_kernel(local, own, came, out):
    own, came = own.get(), came.get()
    across = lax.axis_index("tok") // 2
    out[pl.ds(across * local, local)] = own[:local]
    out[pl.ds((1 - across) * local, local)] = came[:local]
    out[2 * local :] = (own[local:].astype(F32) + came[local:].astype(F32)).astype(BF16)


def late_kernel(local, keep, came, out_keep, out_came, out):
    keep, out_keep = keep.get(), out_keep.get()
    out[:local] = keep[:local]
    half = keep.shape[0] - local
    total = keep[local:].astype(F32) + came.get()[...].astype(F32)
    out[local : local + half] = total.astype(BF16)
    total = out_keep[...].astype(F32) + out_came.get()[...].astype(F32)
    out[local + half :] = total.astype(BF16)


def merge_kernel(local, own, across, beside, diagonal, out):
    row, place = lax.axis_index("tok") // 2, lax.rem(lax.axis_index("seq"), 2)
    for n, one, two in ((place, own, across), (1 - place, beside, diagonal)):
        one, two = one.get(), two.get()
        out[n, pl.ds(row * local, local)] = one[:local]
        out[n, pl.ds((1 - row) * local, local)] = two[:local]
        out[n, 2 * local :] = (one[local:].astype(F32) + two[local:].astype(F32)).astype(BF16)


def stack_kernel(*refs):
    out = refs[-1]
    own = lax.axis_index("seq") // 2
    for n, ref in enumerate(refs[:-1]):
        block = ref.get()
        size = block.shape[0]
        out[pl.ds(jnp.bitwise_xor(own, n) * size, size)] = block[...]


def spread_kernel(widths, local, mine, other, *refs):
    outs, both = refs[: len(widths)], refs[len(widths)]
    core = lax.rem(lax.axis_index("tok"), 2)
    for out in outs:
        out[...] = jnp.zeros_like(out)
    mine, other = mine.get(), other.get()
    both[core] = mine[...]
    both[1 - core] = other[...]

    def step(n, _):
        pick = jnp.max(both[0, n, local - 1].astype(F32)).astype(jnp.int32)
        at, rest = 0, 2 * local
        for out, width in zip(outs, widths):
            if width <= 0:
                chunks = out.shape[2] // 128
                for m in range(chunks):
                    if width == 0:
                        term = both[0, n, rest + m].astype(F32) + both[1, n, rest + m].astype(F32)
                    else:
                        term = both[2 * m // chunks, n, rest + m % (chunks // 2)].astype(F32)
                    out[pick, :, m * 128 : (m + 1) * 128] += term
                rest += chunks if width == 0 else chunks // 2
                continue
            blocks = -(-width // 128)
            for group in range(out.shape[2] // (4 * width)):
                for tok in range(4):
                    first = (group * 4 + tok) * width
                    base = (tok // 2) * local + at
                    parts = [both[tok % 2, n, base + m] for m in range(blocks)]
                    term = jnp.concatenate(parts, axis=1)[:, :width].astype(F32)
                    out[pick, :, first : first + width] += term
                at += blocks
        return 0

    lax.fori_loop(0, mine.shape[0], step, 0)


class Exchange:
    def __init__(self, size):
        self.size = size
        self.direct = size == 4

    def swap(self, block, bits):
        pairs = [(n, n ^ bits) for n in range(self.size)]
        return lax.ppermute(block, "tok", pairs)

    def hop(self, block):
        if not self.direct:
            whole = lax.all_gather(block, "tok", axis=0)
            return [whole[n] for n in range(self.size)]
        return [block, self.swap(block, 1), self.swap(block, 2)]

    def land(self, parts):
        if not self.direct:
            return parts
        return parts + [self.swap(parts[2], 1)]

    def turn(self, slots):
        if not self.direct:
            whole = lax.all_to_all(jnp.stack(slots), "tok", 0, 0)
            return [whole[n] for n in range(self.size)]
        return [slots[0]] + [self.swap(slots[n], n) for n in range(1, self.size)]

    def halve(self, slots):
        near, far = self.swap(slots[1], 1), self.swap(slots[3], 1)
        both = call(add_kernel, [shape(far.shape, far.dtype)], [slots[2], far], name="add")[0]
        return near, both

    def reduce(self, slots):
        if not self.direct:
            return [lax.psum_scatter(jnp.stack(slots), "tok", scatter_dimension=0)]
        near, both = self.halve(slots)
        return [slots[0], near, self.swap(both, 2)]


def meet(*arrays):
    return lax.optimization_barrier(arrays)


class Ring:
    def __init__(self, block):
        self.blocks = [block]
        self.right = self.left = block
        self.half = block.shape[0] // 32 * 16
        self.ahead = [(RING[n], RING[(n + 1) % len(RING)]) for n in range(len(RING))]
        self.behind = [(b, a) for a, b in self.ahead]

    def step(self):
        step = len(self.blocks) // 2 + 1
        if step == len(RING) // 2:
            self.right, self.left = self.right[: self.half], self.left[self.half :]
        self.right = lax.ppermute(self.right, "seq", self.ahead)
        self.left = lax.ppermute(self.left, "seq", self.behind)
        self.blocks += [self.right, self.left]

    def meet(self, *arrays):
        self.right, self.left, *arrays = meet(self.right, self.left, *arrays)
        if len(self.blocks) > 1:
            self.blocks[-2:] = [self.right, self.left]
        return arrays


def owner_of_columns(seq, tok):
    double, single, seen = [], [], [0] * tok
    kinds = [[0, 0, 0] for _ in range(tok)]
    for s in range(seq):
        first = 3 * s + s % 2
        own = first % seq // 2
        double.append((own, seen[own]))
        kinds[own][seen[own]] = first // seq
        seen[own] += 1
        last = 3 * s + 2 * (1 - s % 2)
        single.append((last % seq // 2, last % 2))
        kinds[last % seq // 2][2] = last // seq
    return double, single, kinds


def body(
    tokens,
    out_grad,
    segments,
    adapter_index,
    qkv_weight,
    out_weight,
    in_weight,
    out2_weight,
    attn_gain,
    mlp_gain,
    qkv_down,
    qkv_up,
    out_down,
    out_up,
    in_down,
    in_up,
    out2_down,
    out2_up,
):
    seq, tok = lax.axis_size("seq"), lax.axis_size("tok")
    own_tok = lax.axis_index("tok")
    move = Exchange(tok)
    direct = move.direct
    fast = direct and seq == 8
    adapters, rank, width = qkv_down.shape
    length = segments.shape[1]
    rows = tokens.shape[1]
    heads = HEADS // tok
    lanes = heads * HEAD_DIM
    hidden = out2_weight.shape[0]
    hidden_all = hidden * tok
    inputs, out_grad = tokens[0], out_grad[0]
    pick = adapter_index[0]
    pieces = lambda columns: -(-columns // 128)
    early_local, late_local = 3 * pieces(hidden) + 1, 3 * pieces(lanes) + 1
    wide = pieces(width)

    sizes = ((width, 0), (lanes, 3), (width, 0), (width, 0), (width, 0), (hidden, 2), (hidden, 1), (width, 0))
    tables = (qkv_down, qkv_up, out_down, out_up, in_down, in_up, out2_down, out2_up)
    if fast:
        adapters_own = call(
            functools.partial(adapters_kernel, tok),
            [
                shape((groups,) * (groups > 1) + (rank, columns), BF16)
                for columns, groups in sizes
            ],
            [Pick(table, adapter_index) for table in tables],
            name="adapters",
        )
    else:

        def chosen(table, columns, groups):
            parts = []
            for group in range(max(groups, 1)):
                start = (group * tok + own_tok) * columns if groups else 0
                parts.append(lax.dynamic_slice(table, (pick, 0, start), (1, rank, columns))[0])
            return jnp.stack(parts) if groups > 1 else parts[0]

        adapters_own = [chosen(table, *size) for table, size in zip(tables, sizes)]

    exponent = jnp.arange(0, HEAD_DIM, 2).astype(F32) / HEAD_DIM
    inverse = 1.0 / THETA**exponent
    phases = jnp.arange(length).astype(F32)[:, None] * jnp.tile(inverse, 4)[None, :]
    sign = jnp.where(jnp.arange(2 * HEAD_DIM) % HEAD_DIM < HEAD_DIM // 2, -1.0, 1.0)
    cosine, sine = jnp.cos(phases), jnp.sin(phases) * sign[None, :]

    if fast:
        unit = width // seq
        double, single, kinds = owner_of_columns(seq, tok)
        kinds = jnp.array(sum(kinds, []), jnp.int32)
        token_block, *parts = call(
            prepare_kernel,
            [
                shape((rows + 16, width), BF16),
                shape((qkv_weight.shape[0], 2 * unit), BF16),
                shape((qkv_weight.shape[0], unit), BF16),
            ],
            [inputs, attn_gain, mlp_gain, qkv_weight],
            name="prepare",
        )
        for n, owners in enumerate((double, single)):
            pairs = [
                (s * tok + t, (owners[s][1] * tok + t) * tok + owners[s][0])
                for s in range(seq)
                for t in range(tok)
            ]
            parts[n] = lax.ppermute(parts[n], ("seq", "tok"), pairs)
        together = meet(token_block, cosine, sine, *adapters_own, *parts)
        token_block, cosine, sine, adapters_own = *together[:3], together[3:11]
        parts = list(together[11:])
        ring = Ring(jnp.concatenate(parts + [out_weight], axis=1))
        ring.step()
        ring.step()
        in_piece, out_grad_in = ring.meet(in_weight.T, out_grad)
        pairs = [
            (s * tok + t, ((s // tok) * tok + t) * tok + s % tok)
            for s in range(seq)
            for t in range(tok)
        ]
        in_piece = lax.ppermute(in_piece, ("seq", "tok"), pairs)
        ring.step()
        ring.step()
        mlp_piece = jnp.concatenate([in_piece, out2_weight], axis=1)
        (mlp_piece,) = ring.meet(mlp_piece)
        qkv_pieces = ring.blocks
        mlp_ring = Ring(mlp_piece)
        mlp_ring.step()
    else:

        def columns(weight, count):
            block = lax.all_gather(weight, "seq", axis=1, tiled=True)
            split = block.reshape(block.shape[0], count, tok, -1).transpose(2, 1, 0, 3)
            turned = lax.all_to_all(split, "tok", 0, 0)
            return turned.transpose(1, 0, 2, 3).reshape(count, width, -1)

        gain_rows = jnp.stack([attn_gain, mlp_gain])
        gain_rows = jnp.pad(gain_rows, ((0, 14), (0, width - width // tok)))
        token_block = jnp.concatenate([inputs, gain_rows], axis=0)
        out_grad_in = out_grad
        qkv_pieces = [columns(qkv_weight, 3)]
        kinds = jnp.zeros((1,), jnp.int32)
        own_out = lax.all_gather(out_weight, "seq", axis=1, tiled=True)
        mlp_weights = [
            columns(in_weight, 2).transpose(0, 2, 1),
            lax.all_gather(out2_weight, "seq", axis=1, tiled=True),
        ]
    token_all = lax.all_gather(token_block, "tok", axis=0)
    grad_all = lax.all_gather(out_grad_in, "tok", axis=0)

    down_one, up_one, down_attn, up_attn, down_two, up_two, down_last, up_last = adapters_own

    norm_one, gain, query, key, value, w_qkv, *own_row = call(
        functools.partial(qkv_kernel, len(qkv_pieces)),
        [shape((length, width), BF16), shape((2, width), F32)]
        + [shape((length, lanes), BF16)] * 3
        + [shape((3, width, lanes), BF16)]
        + [shape((lanes, width), BF16)] * fast,
        [kinds, token_all, down_one, up_one, cosine, sine] + qkv_pieces,
        smem=(0,),
        name="qkv",
    )
    if fast:
        query, key, value = mlp_ring.meet(query, key, value)
        mlp_ring.step()
    out_parts = move.hop(own_row[0] if fast else own_out)
    *attn_slots, log_total, mixed_t = call(
        functools.partial(attend_kernel, tok, direct),
        [shape((rows, lanes), BF16)] * tok
        + [shape((heads, length), F32), shape((tok, lanes, rows), F32)],
        [segments, query, key, value, segments],
        smem=(0,),
        scratch=[pltpu.VMEM((lanes, length), BF16), pltpu.VMEM((length, 128), F32)],
        name="attend",
    )
    attn_slots, out_parts = meet(attn_slots, out_parts)
    if fast:
        attn_slots = mlp_ring.meet(*attn_slots)
        mlp_ring.step()
    attn = move.turn(attn_slots)
    out_weights = move.land(out_parts)
    middle, norm_two, narrow_attn = call(
        functools.partial(out_kernel, tok, direct),
        [shape((rows, width), F32), shape((rows, width), BF16), shape((rows, rank), BF16)],
        [inputs, gain, down_attn, up_attn] + attn + out_weights,
        name="out",
    )
    if fast:
        (norm_two,) = mlp_ring.meet(norm_two)
        mlp_ring.step()
        mlp_weights = mlp_ring.blocks
    norm_slots = move.hop(norm_two)
    w_in, w_out, *grad_acts = call(
        functools.partial(mlp_pre_kernel, fast, direct),
        [
            shape((2, hidden, width), BF16),
            shape((hidden, width), BF16),
            shape((2, rows, hidden), F32),
            shape((tok - 2, rows, hidden), F32),
        ],
        [down_two, up_two, down_last, up_last, grad_all] + mlp_weights,
        name="mlp_pre",
    )
    back_slots, acts, grads_z = [], [], []
    for first in range(0, tok, 2):
        *backs, act, grad_z = call(
            functools.partial(mlp_kernel, 2, max(first - 2, 0)),
            [shape((rows, width), BF16)] * 2
            + [shape((2, rows, hidden), BF16), shape((2, 2, rows, hidden), BF16)],
            [w_in, grad_acts[min(first, 1)]] + norm_slots[first : first + 2],
            name="mlp",
        )
        if first == 0:
            *backs, norm_slots[2] = meet(*backs, norm_slots[2])
            norm_slots = move.land(norm_slots)
        back_slots += backs
        acts.append(act)
        grads_z.append(grad_z)
    back_two = move.reduce(back_slots)
    out_slots, early = [], []
    for first in range(0, tok, 4):
        pair = slice(first // 2, first // 2 + 2)
        terms = call(
            functools.partial(mlp_terms_kernel, 4, first, direct),
            [shape((early_local + 2 * wide, rank, 128), BF16 if fast else F32)],
            [adapter_index, down_two, up_two, down_last, up_last]
            + acts[pair]
            + grads_z[pair]
            + [grad_all]
            + norm_slots[first : first + 4],
            smem=(0,),
            name="mlp_terms",
        )[0]
        early.append(terms)
        terms, *acts[pair] = meet(terms, *acts[pair])
        out_slots += call(
            functools.partial(mlp_out_kernel, 4),
            [shape((rows, width), BF16)] * 4,
            [w_out] + acts[pair],
            early=(0, 1, 2, 3),
            name="mlp_out",
        )
    early = sum(early[1:], early[0])
    if fast:
        back_two[2], *out_slots = meet(back_two[2], *out_slots)
        early = call(
            functools.partial(pair_kernel, early_local),
            [shape((early_local + early.shape[0], rank, 128), BF16)],
            [early, move.swap(early, 2)],
            name="pair",
        )[0]
        back_two[2], early = meet(back_two[2], early)
        early = lax.all_gather(early, "seq", axis=0)
    grad_mid, *rest = call(
        functools.partial(out_back_kernel, tok, len(back_two), direct),
        [shape((rows, width), F32)]
        + [shape((rows, lanes), BF16)] * tok
        + [shape((wide, rank, 128), BF16)] * 2,
        [middle, out_grad, gain, down_attn, up_attn, narrow_attn] + back_two + attn + out_weights,
        scratch=[pltpu.VMEM((rank, width), F32)],
        name="out_back",
    )
    out_keep, out_send = rest[tok:]
    attn_grads = move.turn(rest[:tok])
    if fast:
        attn_grads, out_slots = meet(attn_grads, out_slots)
    out_parts = move.turn(out_slots) if fast else move.reduce(out_slots)
    grad_qkv, keep, send = call(
        functools.partial(attend_back_kernel, tok, direct),
        [
            shape((3, length, lanes), BF16),
            shape((late_local + wide // 2, rank, 128), BF16),
            shape((wide // 2, rank, 128), BF16),
        ],
        [segments, adapter_index, query, key, value, segments, log_total, mixed_t, cosine, sine]
        + [down_one, up_one, norm_one]
        + attn_grads,
        smem=(0, 1),
        scratch=[
            pltpu.VMEM((lanes, length), BF16),
            pltpu.VMEM((length, 128), F32),
            pltpu.VMEM((length, lanes), F32),
            pltpu.VMEM((length, lanes), F32),
            pltpu.VMEM((length, lanes), F32),
            pltpu.VMEM((lanes, rows), F32),
            pltpu.VMEM((tok, rows, lanes), BF16),
        ],
        name="attend_back",
    )

    def slots_of_one(grad_qkv):
        return call(
            functools.partial(qkv_back_kernel, tok, direct),
            [shape((rows, width), BF16)] * tok,
            [grad_qkv, w_qkv],
            early=tuple(range(tok)),
            name="qkv_back",
        )

    def last_of(back_one):
        return call(
            functools.partial(last_kernel, len(back_one), len(out_parts)),
            [shape((rows, width), BF16)] * 2,
            [inputs, grad_mid, middle, gain] + back_one + out_parts,
            early=(0, 1),
            name="last",
        )

    grads = lambda columns: shape((adapters, rank, columns), F32)
    if fast:

        def spread(whole, local, widths, columns):
            return call(
                functools.partial(spread_kernel, widths, local),
                [grads(size) for size in columns],
                [whole, move.swap(whole, 1)],
                scratch=[pltpu.VMEM((2,) + whole.shape, BF16)],
                name="spread",
            )

        keep, early, *out_parts = meet(keep, early, *out_parts)
        late = call(
            functools.partial(late_kernel, late_local),
            [shape((late_local + 3 * wide // 2, rank, 128), BF16)],
            [keep, move.swap(send, 1), out_keep, move.swap(out_send, 1)],
            name="late",
        )[0]
        diagonal = [(s * tok + t, (s ^ 1) * tok + (t ^ 2)) for s in range(seq) for t in range(tok)]
        came = [
            late,
            move.swap(late, 2),
            lax.ppermute(late, "seq", [(s, s ^ 1) for s in range(seq)]),
            lax.ppermute(late, ("seq", "tok"), diagonal),
        ]
        late, grad_qkv = meet(late, grad_qkv)
        one_slots = slots_of_one(grad_qkv)
        near, both = move.halve(one_slots)
        both, *came = meet(both, *came)
        back_one = [one_slots[0], near, move.swap(both, 2)]
        merged = call(
            functools.partial(merge_kernel, late_local),
            [shape((2, late_local + late.shape[0], rank, 128), BF16)],
            came,
            name="merge",
        )[0]
        blocks = [merged]
        for bits in (2, 4, 6):
            pairs = [(s, s ^ bits) for s in range(seq)]
            blocks.append(lax.ppermute(merged, "seq", pairs))
        in_up_grad, out2_down_grad, in_down_grad, out2_up_grad = spread(
            early, early_local, (hidden, hidden, 0, 0), (2 * hidden_all, hidden_all, width, width)
        )
        input_grad, layer_out = last_of(back_one)
        in_up_grad, input_grad, *blocks = meet(in_up_grad, input_grad, *blocks)
        late = call(
            stack_kernel, [shape((seq,) + merged.shape[1:], BF16)], blocks, name="stack"
        )[0]
        qkv_up_grad, qkv_down_grad, out_down_grad, out_up_grad = spread(
            late, late_local, (lanes, -1, -1, -1), (3 * width, width, width, width)
        )
    else:
        input_grad, layer_out = last_of(move.reduce(slots_of_one(grad_qkv)))
        picked = (pick == jnp.arange(adapters)).astype(F32)[:, None, None]

        def term(blocks, columns):
            return blocks.astype(F32).transpose(1, 0, 2).reshape(rank, -1)[:, :columns]

        def placed(terms, first, groups, columns):
            total = jnp.zeros((rank, groups * tok * columns), F32)
            for group in range(groups):
                at = first + group * pieces(columns)
                part = term(terms[at : at + pieces(columns)], columns)
                start = (group * tok + own_tok) * columns
                total = lax.dynamic_update_slice(total, part, (0, start))
            return total

        whole = lambda terms, at: term(terms[at : at + wide], width)

        def joined(kept, at, sent, first):
            half = wide // 2
            mine, other = kept[at : at + half], sent[first : first + half]
            swap = own_tok % 2 == 1
            low, high = jnp.where(swap, other, mine), jnp.where(swap, mine, other)
            return term(jnp.concatenate([low, high]), width)

        sums = (
            joined(keep, late_local, send, 0),
            placed(keep, 0, 3, lanes),
            joined(out_keep, 0, out_send, 0),
            joined(out_keep, wide // 2, out_send, wide // 2),
            whole(early, early_local),
            placed(early, 0, 2, hidden),
            placed(early, 2 * pieces(hidden), 1, hidden),
            whole(early, early_local + wide),
        )
        summed = lax.psum(tuple(picked * part[None] for part in sums), ("seq", "tok"))
        qkv_down_grad, qkv_up_grad, out_down_grad, out_up_grad = summed[:4]
        in_down_grad, in_up_grad, out2_down_grad, out2_up_grad = summed[4:]
    return (
        layer_out[None],
        input_grad[None],
        qkv_down_grad,
        qkv_up_grad,
        out_down_grad,
        out_up_grad,
        in_down_grad,
        in_up_grad,
        out2_down_grad,
        out2_up_grad,
    )


def solution(mesh):
    grid = P("tok", "seq")
    split = P("seq", "tok", None)
    return jax.shard_map(
        body,
        mesh=mesh,
        in_specs=(split, split, P("seq", None), P("seq"), grid, grid, grid, grid, P("tok"), P("tok"))
        + (P(),) * 8,
        out_specs=(split, split) + (P(),) * 8,
        check_vma=False,
    )
```

```python
import functools

import jax
import jax.numpy as jnp
from jax import lax
from jax.experimental import pallas as pl
from jax.experimental.pallas import tpu as pltpu
from jax.sharding import PartitionSpec as P

HEADS = 16
HEAD_DIM = 64
EPS = 1e-05
THETA = 160000.0
F32 = jnp.float32
BF16 = jnp.bfloat16
MIB = 1024 * 1024
RING = (0, 2, 4, 6, 7, 5, 3, 1)


def nn(a, b):
    return lax.dot_general(a, b, (((1,), (0,)), ((), ())), preferred_element_type=F32)


def nt(a, b):
    return lax.dot_general(a, b, (((1,), (1,)), ((), ())), preferred_element_type=F32)


def tn(a, b):
    return lax.dot_general(a, b, (((0,), (0,)), ((), ())), preferred_element_type=F32)


def shape(dims, dtype):
    return jax.ShapeDtypeStruct(tuple(dims), dtype)


PIECE = 256 * 1024


def cuts(dims, item):
    size = item
    for n in dims:
        size *= n
    if size <= PIECE * 3 // 2 or len(dims) == 1:
        return [()]
    if len(dims) == 2:
        step = max(dims[0] * PIECE // size // 16 * 16, 16)
        return [(pl.ds(n, min(step, dims[0] - n)),) for n in range(0, dims[0], step)]
    return [(n,) + rest for n in range(dims[0]) for rest in cuts(dims[1:], item)]


def start_copies(source, target, semaphore):
    for at in cuts(target.shape, target.dtype.itemsize):
        one, two = (source.at[at], target.at[at]) if at else (source, target)
        pltpu.make_async_copy(one, two, semaphore).start()
    return pltpu.make_async_copy(source, target, semaphore)


class Late:
    def __init__(self, source, target, semaphore):
        self.target, self.there = target, False
        self.copy = start_copies(source, target, semaphore)

    def get(self):
        if not self.there:
            self.copy.wait()
            self.there = True
        return self.target


class Here:
    def __init__(self, ref):
        self.ref = ref

    def get(self):
        return self.ref

    def send(self):
        pass


class Early:
    def __init__(self, target, source, semaphore):
        self.ref, self.sent = source, False
        self.ends = (source, target, semaphore)

    def send(self):
        if not self.sent:
            self.copy = start_copies(*self.ends)
            self.sent = True


class Pick:
    def __init__(self, table, pick, start=None, size=None):
        self.table, self.pick = table, pick
        self.start, self.size = start, table.shape[2] if size is None else size


def call(kernel, out_shape, args, scratch=(), smem=(), early=(), name=None):
    picks = {n: a for n, a in enumerate(args) if isinstance(a, Pick)}
    operands = [a.table if isinstance(a, Pick) else a for a in args]
    chosen = [next(iter(picks.values())).pick] if picks else []
    late = list(picks)
    buffers = [
        pltpu.VMEM((args[n].table.shape[1], args[n].size), args[n].table.dtype) for n in late
    ]
    buffers += [pltpu.VMEM(out_shape[n].shape, out_shape[n].dtype) for n in early]
    first_in = len(chosen)

    def body(*refs):
        pick, refs = refs[:first_in], refs[first_in:]
        ins, refs = list(refs[: len(args)]), refs[len(args) :]
        outs, refs = list(refs[: len(out_shape)]), refs[len(out_shape) :]
        own, refs = refs[: len(scratch)], refs[len(scratch) :]
        semaphores = refs[-1]
        for at, n in enumerate(late):
            entry = picks[n]
            columns = slice(None) if entry.start is None else pl.ds(entry.start(), entry.size)
            source = ins[n].at[pick[0][0], :, columns]
            ins[n] = Late(source, refs[at], semaphores.at[at])
        for n in range(len(args)):
            if n not in picks and n not in smem:
                ins[n] = Here(ins[n])
        for at, n in enumerate(early, len(late)):
            outs[n] = Early(outs[n], refs[at], semaphores.at[at])
        kernel(*ins, *outs, *own)
        for n in late:
            ins[n].get()
        for n in early:
            outs[n].send()
            outs[n].copy.wait()

    spaces = [pltpu.SMEM] * first_in + [
        pltpu.SMEM if n in smem else pl.ANY if n in picks else pltpu.VMEM
        for n in range(len(args))
    ]
    return pl.pallas_call(
        body,
        out_shape=list(out_shape),
        in_specs=[pl.BlockSpec(memory_space=space) for space in spaces],
        out_specs=[
            pl.BlockSpec(memory_space=pl.ANY if n in early else pltpu.VMEM)
            for n in range(len(out_shape))
        ],
        scratch_shapes=list(scratch)
        + buffers
        + [pltpu.SemaphoreType.DMA((max(len(late) + len(early), 1),))],
        compiler_params=pltpu.CompilerParams(vmem_limit_bytes=60 * MIB),
        cost_estimate=pl.CostEstimate(flops=1, bytes_accessed=1, transcendentals=0),
        name=name,
    )(*chosen, *operands)


def owner(n, direct):
    return jnp.bitwise_xor(lax.axis_index("tok"), n) if direct else n


def rows_of(n, size):
    if isinstance(n, int):
        return pl.ds(n * size, size)
    return pl.ds(pl.multiple_of(n * size, size), size)


def came_from(n):
    own, size = lax.axis_index("seq"), len(RING)
    place = jnp.where(lax.rem(own, 2) == 0, own // 2, size - 1 - own // 2)
    shift = (0, -1, 1, -2, 2, -3, 3, -4, 4)[n]
    came = lax.rem(place + shift + size, size)
    return jnp.where(came < size // 2, 2 * came, 2 * (size - 1 - came) + 1)


def to_slot(refs, index, value):
    for n, ref in enumerate(refs):

        @pl.when(index == n)
        def _(ref=ref):
            ref[...] = value


def normalized(rows):
    mean = jnp.mean(rows, axis=-1, keepdims=True)
    centered = rows - mean
    scale = lax.rsqrt(jnp.mean(centered * centered, axis=-1, keepdims=True) + EPS)
    return centered * scale, scale


def norm_back(rows, gain, grad):
    unit, scale = normalized(rows)
    weighted = grad * gain
    first = jnp.mean(weighted, axis=-1, keepdims=True)
    second = jnp.mean(weighted * unit, axis=-1, keepdims=True)
    return (weighted - first - unit * second) * scale


def swapped(rows):
    width = rows.shape[1]
    if width % 128:
        half = HEAD_DIM // 2
        parts = []
        for start in range(0, width, HEAD_DIM):
            parts += [rows[:, start + half : start + HEAD_DIM], rows[:, start : start + half]]
        return jnp.concatenate(parts, axis=1)
    lane = lax.broadcasted_iota(jnp.int32, rows.shape, 1)
    ahead = pltpu.roll(rows, width - HEAD_DIM // 2, 1)
    behind = pltpu.roll(rows, HEAD_DIM // 2, 1)
    return jnp.where(lane % HEAD_DIM < HEAD_DIM // 2, ahead, behind)


def widened(table, width):
    if width <= table.shape[1]:
        return table[:, :width]
    return jnp.concatenate([table] * (width // table.shape[1]), axis=1)


def head_part(rows, head):
    lane = lax.broadcasted_iota(jnp.int32, rows.shape, 1)
    return jnp.where(lane // HEAD_DIM == head, rows, jnp.zeros_like(rows))


def chunked(ref, base, value):
    count = -(-value.shape[1] // 128)
    for n in range(count):
        part = value[:, n * 128 : (n + 1) * 128].astype(ref.dtype)
        if part.shape[1] < 128:
            ref[base + n] = jnp.zeros(ref.shape[1:], ref.dtype)
            ref[base + n, :, : part.shape[1]] = part
        else:
            ref[base + n] = part
    return base + count


def halves(keep, at, send, first, value):
    core = lax.rem(lax.axis_index("tok"), 2)
    half = value.shape[1] // 256
    for n in range(2 * half):
        part = value[:, n * 128 : (n + 1) * 128].astype(keep.dtype)

        @pl.when(core == n // half)
        def _(part=part, n=n):
            keep[at + n % half] = part

        @pl.when(core != n // half)
        def _(part=part, n=n):
            send[first + n % half] = part


def labelled(ref, at, pick):
    ref[at] = jnp.full(ref.shape[1:], pick[0].astype(F32)).astype(ref.dtype)


def document_range(block, rows, seg_scalar, seg_row):
    first = seg_scalar[0, block * rows].astype(F32)
    last = seg_scalar[0, block * rows + rows - 1].astype(F32)
    below = jnp.sum(jnp.where(seg_row < first, 1.0, 0.0)).astype(jnp.int32)
    upto = jnp.sum(jnp.where(seg_row <= last, 1.0, 0.0)).astype(jnp.int32)
    return below // rows, (upto + rows - 1) // rows


def prepare_kernel(tokens, gain_one, gain_two, weight, token_out, double, single):
    weight, odd = weight.get(), lax.rem(lax.axis_index("seq"), 2)
    unit = single.shape[1]

    @pl.when(odd == 0)
    def _():
        double[...] = weight[:, : 2 * unit]
        single[...] = weight[:, 2 * unit :]

    @pl.when(odd == 1)
    def _():
        double[...] = weight[:, unit:]
        single[...] = weight[:, :unit]

    tokens = tokens.get()
    rows, part = tokens.shape[0], gain_one.get().shape[0]
    token_out[:rows] = tokens[...]
    token_out[rows:] = jnp.zeros((16, tokens.shape[1]), BF16)
    both = [gain.get()[...].astype(F32).reshape(1, part) for gain in (gain_one, gain_two)]
    token_out[rows : rows + 2, :part] = jnp.concatenate(both, axis=0).astype(BF16)


def adapters_kernel(tok, *refs):
    tables, outs = refs[:8], refs[8:]
    down_one, up_one, down_attn, up_attn, down_two, up_two, down_last, up_last = outs
    for n in (1, 5, 6):
        tables[n].get()
    for table, out in ((0, down_one), (2, down_attn), (3, up_attn), (4, down_two), (7, up_last)):
        out[...] = tables[table].get()[...]
    own = lax.axis_index("tok")
    for n in range(tok):

        @pl.when(own == n)
        def _(n=n):
            down_last[...] = tables[6].get()[:, columns_of(n, 0, down_last.shape[1], tok)]
            for kind in range(3):
                size = up_one.shape[2]
                up_one[kind] = tables[1].get()[:, columns_of(n, kind, size, tok)]
            for kind in range(2):
                size = up_two.shape[2]
                up_two[kind] = tables[5].get()[:, columns_of(n, kind, size, tok)]


def columns_of(own, group, size, tok):
    start = (group * tok + own) * size
    return slice(start, start + size)


def qkv_kernel(pieces, kinds, tokens, down, ups, cosine, sine, *refs):
    weights, refs = refs[:pieces], refs[pieces:]
    norm, gain, query, key, value, whole = refs[:6]
    width = query.shape[1]
    if pieces == 1:
        whole[...] = weights[0].get()[...]
    else:
        out_weight = refs[6]
        unit = width // 2
        own = lax.axis_index("tok")
        first = 0
        for n in range(pieces):
            piece = weights[n].get()
            depth = piece.shape[0]
            spot = came_from(n)
            half, part = spot // 4, lax.rem(spot, 4)
            down_at = pl.ds(pl.multiple_of(part * width + first, depth), depth)
            double, single = kinds[3 * own + half], kinds[3 * own + 2]
            whole[double, down_at, :] = piece[:, :width]
            across = pl.ds(pl.multiple_of(half * unit, unit), unit)
            whole[single, down_at, across] = piece[:, width : width + unit]
            across = pl.ds(pl.multiple_of(spot * unit, unit), unit)
            out_weight[first : first + depth, across] = piece[:, width + unit :]
            first = (first + depth) % width
    for kind in range(3):
        product = tn(down.get()[...], ups.get()[kind])
        whole[kind] = (whole[kind].astype(F32) + product).astype(BF16)
    tokens, cosine, sine = tokens.get(), cosine.get(), sine.get()
    count, block = tokens.shape[0], tokens.shape[1] - 16
    for n in range(count):
        part = gain.shape[1] // count
        gain[:, n * part : (n + 1) * part] = tokens[n, block:, :part].astype(F32)[:2]

    def step(n, _):
        at = rows_of(n, block)
        unit, _ = normalized(tokens[n, :block].astype(F32))
        rows = (unit * gain[0:1, :]).astype(BF16)
        norm[at, :] = rows
        cos, sin = widened(cosine[at, :], width), widened(sine[at, :], width)
        for kind, out in enumerate((query, key, value)):
            part = nn(rows, whole[kind])
            if kind < 2:
                part = part * cos + swapped(part) * sin
            if kind == 0:
                part = part.astype(BF16).astype(F32) * 0.125
            out[at, :] = part.astype(BF16)
        return 0

    lax.fori_loop(0, count, step, 0)


def attend_kernel(count, direct, seg_scalar, query, key, value, segments, *refs):
    outs, (log_total, mixed_t, value_t, seg_t) = refs[:count], refs[count:]
    segments = segments.get()
    seg_row = segments[...].astype(F32)
    seg_t[...] = jnp.broadcast_to(seg_row, (128, seg_row.shape[1])).T
    query, key, value = query.get(), key.get(), value.get()
    block = outs[0].shape[0]
    width = query.shape[1]
    heads = width // HEAD_DIM
    value_t[...] = value[...].T
    parts = [slice(head * HEAD_DIM, (head + 1) * HEAD_DIM) for head in range(heads)]

    def step(n, _):
        place = owner(n, direct)
        at = rows_of(place, block)
        rows = query[at, :]
        own = [head_part(rows, head) for head in range(heads)]
        seg_here = segments[:, at].astype(F32)

        def against(m, carry):
            tops, sums, mixed = carry
            keys = rows_of(m, block)
            column = widened(seg_t[keys, :], block)
            bias = jnp.where(column == seg_here, 0.0, -1e30)
            near = key[keys, :]
            scores = [nt(near, part) + bias for part in own]
            now = [
                jnp.maximum(top, jnp.max(part, axis=0, keepdims=True))
                for top, part in zip(tops, scores)
            ]
            raised = [jnp.exp(part - top) for part, top in zip(scores, now)]
            scale = [jnp.exp(before - top) for before, top in zip(tops, now)]
            added = [nn(value_t[part, keys], up.astype(BF16)) for part, up in zip(parts, raised)]
            sums = [
                total * by + jnp.sum(up, axis=0, keepdims=True)
                for total, by, up in zip(sums, scale, raised)
            ]
            mixed = [old * by + new for old, by, new in zip(mixed, scale, added)]
            return now, sums, mixed

        start = (
            [jnp.full((1, block), -2e30, F32)] * heads,
            [jnp.zeros((1, block), F32)] * heads,
            [jnp.zeros((HEAD_DIM, block), F32)] * heads,
        )
        first, last = document_range(place, block, seg_scalar, seg_row)
        tops, sums, mixed = lax.fori_loop(first, last, against, start)
        for head in range(heads):
            log_total[head : head + 1, at] = tops[head] + jnp.log(sums[head])
            mixed_t[n, parts[head], :] = mixed[head] * (1.0 / sums[head])
        to_slot(outs, n, mixed_t[n].T.astype(BF16))
        return 0

    lax.fori_loop(0, count, step, 0)


def features(n, width, direct):
    if not direct:
        return slice(n * width, (n + 1) * width)
    return pl.ds(pl.multiple_of(owner(n, direct) * width, width), width)


def out_kernel(count, direct, inputs, gain, down, up, *refs):
    attn, weights = refs[:count], refs[count : 2 * count]
    middle, norm, narrow = refs[2 * count :]
    down = down.get()
    total = inputs.get()[...].astype(F32)
    thin = jnp.zeros(narrow.shape, F32)
    for n in range(count):
        rows = attn[n].get()[...]
        total = total + nn(rows, weights[n].get()[...])
        thin = thin + nt(rows, down[:, features(n, rows.shape[1], direct)])
    thin = thin.astype(BF16)
    total = total + nn(thin, up.get()[...])
    middle[...] = total
    narrow[...] = thin
    norm[...] = (normalized(total)[0] * gain.get()[1:2, :]).astype(BF16)


def mlp_pre_kernel(packed, direct, down_in, up_in, down_out, up_out, grads, *refs):
    pieces = 9 if packed else 2
    weights, refs = refs[:pieces], refs[pieces:]
    w_in, w_out, grad_early, grad_late = refs
    hidden, width = w_out.shape
    if packed:
        depth, thin = width // 4, width // 8
        first = 0
        for n in range(pieces):
            piece = weights[n].get()
            rows = slice(first, first + piece.shape[0])
            spot = came_from(n)
            across = pl.ds(pl.multiple_of(lax.rem(spot, 4) * depth, depth), depth)
            w_in[spot // 4, rows, across] = piece[:, :depth]
            across = pl.ds(pl.multiple_of(spot * thin, thin), thin)
            w_out[rows, across] = piece[:, depth:]
            first = rows.stop % hidden
    else:
        w_in[...] = weights[0].get()[...]
        w_out[...] = weights[1].get()[...]
    for n in range(2):
        w_in[n] = (w_in[n].astype(F32) + tn(up_in.get()[n], down_in.get()[...])).astype(BF16)
    w_out[...] = (w_out[...].astype(F32) + tn(down_out.get()[...], up_out.get()[...])).astype(BF16)
    grads = grads.get()
    for n in range(grads.shape[0]):
        target = grad_early if n < 2 else grad_late
        target[n if n < 2 else n - 2] = nt(grads[owner(n, direct)], w_out[...])


def mlp_kernel(count, first, w_in, grad_act, *refs):
    norms, backs, (act_out, grad_out) = refs[:count], refs[count : 2 * count], refs[2 * count :]
    w_in, grad_act = w_in.get(), grad_act.get()
    for n in range(count):
        norm = norms[n].get()[...]
        inputs, gate = nt(norm, w_in[0]), nt(norm, w_in[1])
        phi = 0.5 + 0.5 * lax.erf(inputs * (0.5**0.5))
        gelu = inputs * phi
        act_out[n] = (gelu * gate).astype(BF16)
        back_act = grad_act[first + n]
        slope = phi + inputs * (jnp.exp(-0.5 * inputs * inputs) * 0.3989422804014327)
        grad_inputs = (back_act * gate * slope).astype(BF16)
        grad_gate = (back_act * gelu).astype(BF16)
        grad_out[0, n] = grad_inputs
        grad_out[1, n] = grad_gate
        backs[n][...] = (nn(grad_inputs, w_in[0]) + nn(grad_gate, w_in[1])).astype(BF16)


def mlp_terms_kernel(count, first, direct, pick, down_in, up_in, down_out, up_out, *refs):
    acts, grads, out_grad, refs = refs[:2], refs[2:4], refs[4], refs[5:]
    norms, terms = refs[:count], refs[count]
    down_in_grad = down_out_grad = up_out_grad = 0.0
    up_in_grad = [0.0, 0.0]
    down_in, up_in, down_out, up_out = down_in.get(), up_in.get(), down_out.get(), up_out.get()
    for n in range(count):
        norm = norms[n].get()[...]
        narrow = nt(norm, down_in[...]).astype(BF16)
        back = [grads[n // 2].get()[h, n % 2] for h in range(2)]
        inner_in = (nt(back[0], up_in[0]) + nt(back[1], up_in[1])).astype(BF16)
        down_in_grad = down_in_grad + tn(inner_in, norm)
        for h in range(2):
            up_in_grad[h] = up_in_grad[h] + tn(narrow, back[h])
        act = acts[n // 2].get()[n % 2]
        grad = out_grad.get()[owner(first + n, direct)]
        narrow_two = nt(act, down_out[...]).astype(BF16)
        inner = nt(grad, up_out[...]).astype(BF16)
        down_out_grad = down_out_grad + tn(inner, act)
        up_out_grad = up_out_grad + tn(narrow_two, grad)
    at = chunked(terms, 0, up_in_grad[0])
    at = chunked(terms, at, up_in_grad[1])
    at = chunked(terms, at, down_out_grad)
    labelled(terms, at, pick)
    at = chunked(terms, at + 1, down_in_grad)
    chunked(terms, at, up_out_grad)


def mlp_out_kernel(count, w_out, *refs):
    acts, outs = refs[: count // 2], refs[count // 2 :]
    w_out = w_out.get()
    for n in range(count):
        outs[n].ref[...] = nn(acts[n // 2].get()[n % 2], w_out[...]).astype(BF16)
        outs[n].send()


def out_back_kernel(count, parts, direct, middle, out_grad, gain, down, up, narrow, *refs):
    back, refs = refs[:parts], refs[parts:]
    attn, weights = refs[:count], refs[count : 2 * count]
    grad_mid, refs = refs[2 * count], refs[2 * count + 1 :]
    slots, (keep, send, down_grad) = refs[:count], refs[count:]
    total = sum(ref.get()[...].astype(F32) for ref in back)
    grad = out_grad.get()[...].astype(F32)
    grad = grad + norm_back(middle.get()[...], gain.get()[1:2, :], total)
    grad_mid[...] = grad
    low = grad.astype(BF16)
    down = down.get()
    inner = nt(low, up.get()[...]).astype(BF16)
    for n in range(count):
        rows = attn[n].get()[...]
        own = features(n, rows.shape[1], direct)
        slots[n][...] = (nt(low, weights[n].get()[...]) + nn(inner, down[:, own])).astype(BF16)
        down_grad[:, own] = tn(inner, rows)
    half = grad.shape[1] // 256
    halves(keep, half, send, half, tn(narrow.get()[...], low))
    halves(keep, 0, send, 0, down_grad[...])


def attend_back_kernel(
    count, direct, seg_scalar, pick, query, key, value, segments, log_total, mixed_t, cosine, sine,
    down, ups, norm, *refs
):
    grads, (grad_qkv, keep, send) = refs[:count], refs[count : count + 3]
    key_t, seg_t, grad_q, grad_k, grad_v, query_t, grad_all = refs[count + 3 :]
    segments = segments.get()
    seg_row = segments[...].astype(F32)
    seg_t[...] = jnp.broadcast_to(seg_row, (128, seg_row.shape[1])).T
    for ref in (grad_k, grad_v):
        ref[...] = jnp.zeros_like(ref)
    query, key, value = query.get(), key.get(), value.get()
    log_total, mixed_t = log_total.get(), mixed_t.get()
    block = grads[0].get().shape[0]
    width = query.shape[1]
    heads = width // HEAD_DIM
    key_t[...] = key[...].T
    for n in range(count):
        grad_all[n] = grads[n].get()[...]
    parts = [slice(head * HEAD_DIM, (head + 1) * HEAD_DIM) for head in range(heads)]

    def step(n, _):
        place = owner(n, direct)
        at = rows_of(place, block)
        rows, grad = query[at, :], grad_all[n]
        own = [head_part(rows, head) for head in range(heads)]
        own_grad = [head_part(grad, head) for head in range(heads)]
        product = grad.astype(F32).T * mixed_t[n]
        dots = [jnp.sum(product[part], axis=0, keepdims=True) for part in parts]
        query_t[...] = jnp.zeros_like(query_t)
        seg_here = segments[:, at].astype(F32)

        def against(m, _):
            keys = rows_of(m, block)
            column = widened(seg_t[keys, :], block)
            bias = jnp.where(column == seg_here, 0.0, -1e30)
            near, near_value = key[keys, :], value[keys, :]
            probs = [
                jnp.exp(nt(near, own[head]) + bias - log_total[head : head + 1, at])
                for head in range(heads)
            ]
            grad_probs = [nt(near_value, part) for part in own_grad]
            grad_s = [
                (prob * (grad_prob - dot)).astype(BF16)
                for prob, grad_prob, dot in zip(probs, grad_probs, dots)
            ]
            sum_v = sum(nn(prob.astype(BF16), part) for prob, part in zip(probs, own_grad))
            sum_k = sum(nn(part, mine) for part, mine in zip(grad_s, own))
            for head in range(heads):
                query_t[parts[head], :] += nn(key_t[parts[head], keys], grad_s[head])
            grad_k[keys, :] += sum_k
            grad_v[keys, :] += sum_v
            return 0

        first, last = document_range(place, block, seg_scalar, seg_row)
        lax.fori_loop(first, last, against, 0)
        grad_q[at, :] = query_t[...].T * 0.125
        return 0

    lax.fori_loop(0, count, step, 0)
    cosine, sine = cosine.get(), sine.get()

    def finish(n, _):
        at = rows_of(n, block)
        cos, sin = widened(cosine[at, :], width), widened(sine[at, :], width)
        for kind, ref in enumerate((grad_q, grad_k)):
            part = ref[at, :]
            grad_qkv[kind, at, :] = (part * cos - swapped(part) * sin).astype(BF16)
        grad_qkv[2, at, :] = grad_v[at, :].astype(BF16)
        return 0

    lax.fori_loop(0, count, finish, 0)
    norm = norm.get()
    inner = sum(nt(grad_qkv[kind], ups.get()[kind]) for kind in range(3))
    narrow = nt(norm[...], down.get()[...]).astype(BF16)
    at = 0
    for kind in range(3):
        at = chunked(keep, at, tn(narrow, grad_qkv[kind]))
    labelled(keep, at, pick)
    halves(keep, at + 1, send, 0, tn(inner.astype(BF16), norm[...]))


def qkv_back_kernel(count, direct, grad_qkv, weights, *outs):
    block = outs[0].ref.shape[0]
    grad_qkv, weights = grad_qkv.get(), weights.get()
    for n in list(range(1, count, 2)) + list(range(0, count, 2)):
        at = rows_of(owner(n, direct), block)
        total = sum(nt(grad_qkv[kind, at, :], weights[kind]) for kind in range(3))
        outs[n].ref[...] = total.astype(BF16)
        outs[n].send()


def layer_kernel(middle, *refs):
    total = middle.get()[...] + sum(ref.get()[...].astype(F32) for ref in refs[:-1])
    refs[-1][...] = total.astype(BF16)


def last_kernel(inputs, grad_mid, gain, *refs):
    total = sum(ref.get()[...].astype(F32) for ref in refs[:-1])
    back = norm_back(inputs.get()[...].astype(F32), gain.get()[0:1, :], total)
    refs[-1][...] = (grad_mid.get()[...] + back).astype(BF16)


def pair_kernel(local, own, came, out):
    own, came = own.get(), came.get()
    across = lax.axis_index("tok") // 2
    out[pl.ds(across * local, local)] = own[:local]
    out[pl.ds((1 - across) * local, local)] = came[:local]
    out[2 * local :] = (own[local:].astype(F32) + came[local:].astype(F32)).astype(BF16)


def late_kernel(local, keep, came, out_keep, out_came, out):
    keep, out_keep = keep.get(), out_keep.get()
    out[:local] = keep[:local]
    half = keep.shape[0] - local
    total = keep[local:].astype(F32) + came.get()[...].astype(F32)
    out[local : local + half] = total.astype(BF16)
    total = out_keep[...].astype(F32) + out_came.get()[...].astype(F32)
    out[local + half :] = total.astype(BF16)


def stack_kernel(*refs):
    out = refs[-1]
    first = 0
    for n, ref in enumerate(refs[:-1]):
        block = ref.get()
        size = block.shape[0]
        out[came_from(n), first : first + size] = block[...]
        first = (first + size) % out.shape[1]


def spread_kernel(widths, local, count, *refs):
    mine, other, refs = refs[:count], refs[count : 2 * count], refs[2 * count :]
    outs, both = refs[: len(widths)], refs[len(widths)]
    core = lax.rem(lax.axis_index("tok"), 2)
    own = lax.axis_index("seq") // 2
    for n in range(count):
        size = mine[n].get().shape[0]
        at = pl.ds(jnp.bitwise_xor(own, n) * size, size) if count > 1 else slice(None)
        both[core, at] = mine[n].get()[...]
        both[1 - core, at] = other[n].get()[...]
    for out in outs:
        out[...] = jnp.zeros_like(out)

    def step(n, _):
        pick = jnp.max(both[0, n, local - 1].astype(F32)).astype(jnp.int32)
        at, rest = 0, 2 * local
        for out, width in zip(outs, widths):
            if width <= 0:
                chunks = out.shape[2] // 128
                for m in range(chunks):
                    if width == 0:
                        term = both[0, n, rest + m].astype(F32) + both[1, n, rest + m].astype(F32)
                    else:
                        term = both[2 * m // chunks, n, rest + m % (chunks // 2)].astype(F32)
                    out[pick, :, m * 128 : (m + 1) * 128] += term
                rest += chunks if width == 0 else chunks // 2
                continue
            blocks = -(-width // 128)
            for group in range(out.shape[2] // (4 * width)):
                for tok in range(4):
                    first = (group * 4 + tok) * width
                    base = (tok // 2) * local + at
                    parts = [both[tok % 2, n, base + m] for m in range(blocks)]
                    term = jnp.concatenate(parts, axis=1)[:, :width].astype(F32)
                    out[pick, :, first : first + width] += term
                at += blocks
        return 0

    lax.fori_loop(0, both.shape[1], step, 0)


class Exchange:
    def __init__(self, size):
        self.size = size
        self.direct = size == 4

    def swap(self, block, bits):
        pairs = [(n, n ^ bits) for n in range(self.size)]
        return lax.ppermute(block, "tok", pairs)

    def hop(self, block):
        if not self.direct:
            whole = lax.all_gather(block, "tok", axis=0)
            return [whole[n] for n in range(self.size)]
        return [block, self.swap(block, 1), self.swap(block, 2)]

    def land(self, parts):
        if not self.direct:
            return parts
        return parts + [self.swap(parts[2], 1)]

    def turn(self, slots):
        if not self.direct:
            whole = lax.all_to_all(jnp.stack(slots), "tok", 0, 0)
            return [whole[n] for n in range(self.size)]
        return [slots[0]] + [self.swap(slots[n], n) for n in range(1, self.size)]

    def halve(self, slots):
        near, far = self.swap(slots[1], 1), self.swap(slots[3], 1)
        both = (slots[2].astype(F32) + far.astype(F32)).astype(far.dtype)
        return near, both

    def reduce(self, slots):
        if not self.direct:
            return [lax.psum_scatter(jnp.stack(slots), "tok", scatter_dimension=0)]
        near, both = self.halve(slots)
        return [slots[0], near, self.swap(both, 2)]


def meet(*arrays):
    return lax.optimization_barrier(arrays)


class Ring:
    def __init__(self, block):
        self.blocks = [block]
        self.right = self.left = block
        self.half = block.shape[0] // 32 * 16 if block.ndim == 2 else block.shape[0] // 2
        self.ahead = [(RING[n], RING[(n + 1) % len(RING)]) for n in range(len(RING))]
        self.behind = [(b, a) for a, b in self.ahead]

    def step(self):
        step = len(self.blocks) // 2 + 1
        if step == len(RING) // 2:
            self.right, self.left = self.right[: self.half], self.left[self.half :]
        self.right = lax.ppermute(self.right, "seq", self.ahead)
        self.left = lax.ppermute(self.left, "seq", self.behind)
        self.blocks += [self.right, self.left]

    def meet(self, *arrays):
        self.right, self.left, *arrays = meet(self.right, self.left, *arrays)
        if len(self.blocks) > 1:
            self.blocks[-2:] = [self.right, self.left]
        return arrays


def owner_of_columns(seq, tok):
    double, single, seen = [], [], [0] * tok
    kinds = [[0, 0, 0] for _ in range(tok)]
    for s in range(seq):
        first = 3 * s + s % 2
        own = first % seq // 2
        double.append((own, seen[own]))
        kinds[own][seen[own]] = first // seq
        seen[own] += 1
        last = 3 * s + 2 * (1 - s % 2)
        single.append((last % seq // 2, last % 2))
        kinds[last % seq // 2][2] = last // seq
    return double, single, kinds


def body(
    tokens,
    out_grad,
    segments,
    adapter_index,
    qkv_weight,
    out_weight,
    in_weight,
    out2_weight,
    attn_gain,
    mlp_gain,
    qkv_down,
    qkv_up,
    out_down,
    out_up,
    in_down,
    in_up,
    out2_down,
    out2_up,
):
    seq, tok = lax.axis_size("seq"), lax.axis_size("tok")
    own_tok = lax.axis_index("tok")
    move = Exchange(tok)
    direct = move.direct
    fast = direct and seq == 8
    adapters, rank, width = qkv_down.shape
    length = segments.shape[1]
    rows = tokens.shape[1]
    heads = HEADS // tok
    lanes = heads * HEAD_DIM
    hidden = out2_weight.shape[0]
    hidden_all = hidden * tok
    inputs, out_grad = tokens[0], out_grad[0]
    pick = adapter_index[0]
    pieces = lambda columns: -(-columns // 128)
    early_local, late_local = 3 * pieces(hidden) + 1, 3 * pieces(lanes) + 1
    wide = pieces(width)

    sizes = ((width, 0), (lanes, 3), (width, 0), (width, 0), (width, 0), (hidden, 2), (hidden, 1), (width, 0))
    tables = (qkv_down, qkv_up, out_down, out_up, in_down, in_up, out2_down, out2_up)
    if fast:
        adapters_own = call(
            functools.partial(adapters_kernel, tok),
            [
                shape((groups,) * (groups > 1) + (rank, columns), BF16)
                for columns, groups in sizes
            ],
            [Pick(table, adapter_index) for table in tables],
            name="adapters",
        )
    else:

        def chosen(table, columns, groups):
            parts = []
            for group in range(max(groups, 1)):
                start = (group * tok + own_tok) * columns if groups else 0
                parts.append(lax.dynamic_slice(table, (pick, 0, start), (1, rank, columns))[0])
            return jnp.stack(parts) if groups > 1 else parts[0]

        adapters_own = [chosen(table, *size) for table, size in zip(tables, sizes)]

    exponent = jnp.arange(0, HEAD_DIM, 2).astype(F32) / HEAD_DIM
    inverse = 1.0 / THETA**exponent
    phases = jnp.arange(length).astype(F32)[:, None] * jnp.tile(inverse, 4)[None, :]
    sign = jnp.where(jnp.arange(2 * HEAD_DIM) % HEAD_DIM < HEAD_DIM // 2, -1.0, 1.0)
    cosine, sine = jnp.cos(phases), jnp.sin(phases) * sign[None, :]

    if fast:
        unit = width // seq
        double, single, kinds = owner_of_columns(seq, tok)
        kinds = jnp.array(sum(kinds, []), jnp.int32)
        token_block, *parts = call(
            prepare_kernel,
            [
                shape((rows + 16, width), BF16),
                shape((qkv_weight.shape[0], 2 * unit), BF16),
                shape((qkv_weight.shape[0], unit), BF16),
            ],
            [inputs, attn_gain, mlp_gain, qkv_weight],
            name="prepare",
        )
        for n, owners in enumerate((double, single)):
            pairs = [
                (s * tok + t, (owners[s][1] * tok + t) * tok + owners[s][0])
                for s in range(seq)
                for t in range(tok)
            ]
            parts[n] = lax.ppermute(parts[n], ("seq", "tok"), pairs)
        pairs = [
            (s * tok + t, ((s // tok) * tok + t) * tok + s % tok)
            for s in range(seq)
            for t in range(tok)
        ]
        in_piece = lax.ppermute(in_weight.T, ("seq", "tok"), pairs)
        together = meet(token_block, cosine, sine, *adapters_own, in_piece, *parts)
        token_block, cosine, sine, adapters_own = *together[:3], together[3:11]
        in_piece, *parts = together[11:]
        ring = Ring(jnp.concatenate(parts + [out_weight], axis=1))
        ring.step()
        ring.step()
        (out_grad_in,) = ring.meet(out_grad)
        ring.step()
        ring.step()
        mlp_piece = jnp.concatenate([in_piece, out2_weight], axis=1)
        (mlp_piece,) = ring.meet(mlp_piece)
        qkv_pieces = ring.blocks
        mlp_ring = Ring(mlp_piece)
        mlp_ring.step()
    else:

        def columns(weight, count):
            block = lax.all_gather(weight, "seq", axis=1, tiled=True)
            split = block.reshape(block.shape[0], count, tok, -1).transpose(2, 1, 0, 3)
            turned = lax.all_to_all(split, "tok", 0, 0)
            return turned.transpose(1, 0, 2, 3).reshape(count, width, -1)

        gain_rows = jnp.stack([attn_gain, mlp_gain])
        gain_rows = jnp.pad(gain_rows, ((0, 14), (0, width - width // tok)))
        token_block = jnp.concatenate([inputs, gain_rows], axis=0)
        out_grad_in = out_grad
        qkv_pieces = [columns(qkv_weight, 3)]
        kinds = jnp.zeros((1,), jnp.int32)
        own_out = lax.all_gather(out_weight, "seq", axis=1, tiled=True)
        mlp_weights = [
            columns(in_weight, 2).transpose(0, 2, 1),
            lax.all_gather(out2_weight, "seq", axis=1, tiled=True),
        ]
    token_all = lax.all_gather(token_block, "tok", axis=0)
    grad_all = lax.all_gather(out_grad_in, "tok", axis=0)

    down_one, up_one, down_attn, up_attn, down_two, up_two, down_last, up_last = adapters_own

    norm_one, gain, query, key, value, w_qkv, *own_row = call(
        functools.partial(qkv_kernel, len(qkv_pieces)),
        [shape((length, width), BF16), shape((2, width), F32)]
        + [shape((length, lanes), BF16)] * 3
        + [shape((3, width, lanes), BF16)]
        + [shape((lanes, width), BF16)] * fast,
        [kinds, token_all, down_one, up_one, cosine, sine] + qkv_pieces,
        smem=(0,),
        name="qkv",
    )
    if fast:
        query, key, value = mlp_ring.meet(query, key, value)
        mlp_ring.step()
    out_parts = move.hop(own_row[0] if fast else own_out)
    *attn_slots, log_total, mixed_t = call(
        functools.partial(attend_kernel, tok, direct),
        [shape((rows, lanes), BF16)] * tok
        + [shape((heads, length), F32), shape((tok, lanes, rows), F32)],
        [segments, query, key, value, segments],
        smem=(0,),
        scratch=[pltpu.VMEM((lanes, length), BF16), pltpu.VMEM((length, 128), F32)],
        name="attend",
    )
    attn_slots, out_parts = meet(attn_slots, out_parts)
    if fast:
        attn_slots = mlp_ring.meet(*attn_slots)
        mlp_ring.step()
    attn = move.turn(attn_slots)
    out_weights = move.land(out_parts)
    middle, norm_two, narrow_attn = call(
        functools.partial(out_kernel, tok, direct),
        [shape((rows, width), F32), shape((rows, width), BF16), shape((rows, rank), BF16)],
        [inputs, gain, down_attn, up_attn] + attn + out_weights,
        name="out",
    )
    if fast:
        (norm_two,) = mlp_ring.meet(norm_two)
        mlp_ring.step()
        mlp_weights = mlp_ring.blocks
    norm_slots = move.hop(norm_two)
    w_in, w_out, *grad_acts = call(
        functools.partial(mlp_pre_kernel, fast, direct),
        [
            shape((2, hidden, width), BF16),
            shape((hidden, width), BF16),
            shape((2, rows, hidden), F32),
            shape((tok - 2, rows, hidden), F32),
        ],
        [down_two, up_two, down_last, up_last, grad_all] + mlp_weights,
        name="mlp_pre",
    )
    back_slots, acts, grads_z = [], [], []
    for first in range(0, tok, 2):
        *backs, act, grad_z = call(
            functools.partial(mlp_kernel, 2, max(first - 2, 0)),
            [shape((rows, width), BF16)] * 2
            + [shape((2, rows, hidden), BF16), shape((2, 2, rows, hidden), BF16)],
            [w_in, grad_acts[min(first, 1)]] + norm_slots[first : first + 2],
            name="mlp",
        )
        if first == 0:
            *backs, norm_slots[2] = meet(*backs, norm_slots[2])
            norm_slots = move.land(norm_slots)
        back_slots += backs
        acts.append(act)
        grads_z.append(grad_z)
    back_two = move.reduce(back_slots)
    out_slots, early = [], []
    for first in range(0, tok, 4):
        pair = slice(first // 2, first // 2 + 2)
        terms = call(
            functools.partial(mlp_terms_kernel, 4, first, direct),
            [shape((early_local + 2 * wide, rank, 128), BF16 if fast else F32)],
            [adapter_index, down_two, up_two, down_last, up_last]
            + acts[pair]
            + grads_z[pair]
            + [grad_all]
            + norm_slots[first : first + 4],
            smem=(0,),
            name="mlp_terms",
        )[0]
        early.append(terms)
        terms, *acts[pair] = meet(terms, *acts[pair])
        out_slots += call(
            functools.partial(mlp_out_kernel, 4),
            [shape((rows, width), BF16)] * 4,
            [w_out] + acts[pair],
            early=(0, 1, 2, 3),
            name="mlp_out",
        )
    early = sum(early[1:], early[0])
    if fast:
        back_two[2], *out_slots = meet(back_two[2], *out_slots)
        early = call(
            functools.partial(pair_kernel, early_local),
            [shape((early_local + early.shape[0], rank, 128), BF16)],
            [early, move.swap(early, 2)],
            name="pair",
        )[0]
    grad_mid, *rest = call(
        functools.partial(out_back_kernel, tok, len(back_two), direct),
        [shape((rows, width), F32)]
        + [shape((rows, lanes), BF16)] * tok
        + [shape((wide, rank, 128), BF16)] * 2,
        [middle, out_grad, gain, down_attn, up_attn, narrow_attn] + back_two + attn + out_weights,
        scratch=[pltpu.VMEM((rank, width), F32)],
        name="out_back",
    )
    out_keep, out_send = rest[tok:]
    attn_grads = move.turn(rest[:tok])
    if fast:
        attn_grads, out_slots, early = meet(attn_grads, out_slots, early)
        early = lax.all_gather(early, "seq", axis=0)
    out_parts = move.turn(out_slots) if fast else move.reduce(out_slots)
    grad_qkv, keep, send = call(
        functools.partial(attend_back_kernel, tok, direct),
        [
            shape((3, length, lanes), BF16),
            shape((late_local + wide // 2, rank, 128), BF16),
            shape((wide // 2, rank, 128), BF16),
        ],
        [segments, adapter_index, query, key, value, segments, log_total, mixed_t, cosine, sine]
        + [down_one, up_one, norm_one]
        + attn_grads,
        smem=(0, 1),
        scratch=[
            pltpu.VMEM((lanes, length), BF16),
            pltpu.VMEM((length, 128), F32),
            pltpu.VMEM((length, lanes), F32),
            pltpu.VMEM((length, lanes), F32),
            pltpu.VMEM((length, lanes), F32),
            pltpu.VMEM((lanes, rows), F32),
            pltpu.VMEM((tok, rows, lanes), BF16),
        ],
        name="attend_back",
    )

    def slots_of_one(grad_qkv):
        return call(
            functools.partial(qkv_back_kernel, tok, direct),
            [shape((rows, width), BF16)] * tok,
            [grad_qkv, w_qkv],
            early=tuple(range(tok)),
            name="qkv_back",
        )

    def layer_of(out_parts):
        output = [shape((rows, width), BF16)]
        return call(layer_kernel, output, [middle] + out_parts, name="layer")[0]

    def last_of(back_one):
        return call(
            last_kernel,
            [shape((rows, width), BF16)],
            [inputs, grad_mid, gain] + back_one,
            name="last",
        )[0]

    grads = lambda columns: shape((adapters, rank, columns), F32)
    if fast:

        def spread(parts, local, widths, columns):
            return call(
                functools.partial(spread_kernel, widths, local, len(parts)),
                [grads(size) for size in columns],
                parts + [move.swap(part, 1) for part in parts],
                scratch=[pltpu.VMEM((2, seq) + parts[0].shape[1:], BF16)],
                name="spread",
            )

        keep, *out_parts = meet(keep, *out_parts)
        layer_out = layer_of(out_parts)
        late = call(
            functools.partial(late_kernel, late_local),
            [shape((late_local + 3 * wide // 2, rank, 128), BF16)],
            [keep, move.swap(send, 1), out_keep, move.swap(out_send, 1)],
            name="late",
        )[0]
        late_came = move.swap(late, 2)
        late, grad_qkv = meet(late, grad_qkv)
        one_slots = slots_of_one(grad_qkv)
        near, both = move.halve(one_slots)
        both, late_came = meet(both, late_came)
        back_one = [one_slots[0], near, move.swap(both, 2)]
        late = call(
            functools.partial(pair_kernel, late_local),
            [shape((late_local + late.shape[0], rank, 128), BF16)],
            [late, late_came],
            name="pair_late",
        )[0]
        ring = Ring(late)
        ring.step()
        layer_out, back_one[2] = ring.meet(layer_out, back_one[2])
        ring.step()
        input_grad, early = ring.meet(last_of(back_one), early)
        ring.step()
        ring.step()
        in_up_grad, out2_down_grad, in_down_grad, out2_up_grad = spread(
            [early], early_local, (hidden, hidden, 0, 0), (2 * hidden_all, hidden_all, width, width)
        )
        (in_up_grad,) = ring.meet(in_up_grad)
        stacked = shape((seq,) + late.shape, BF16)
        blocks = list(call(stack_kernel, [stacked], ring.blocks, name="stack"))
        qkv_up_grad, qkv_down_grad, out_down_grad, out_up_grad = spread(
            blocks, late_local, (lanes, -1, -1, -1), (3 * width, width, width, width)
        )
    else:
        layer_out = layer_of(out_parts)
        input_grad = last_of(move.reduce(slots_of_one(grad_qkv)))
        picked = (pick == jnp.arange(adapters)).astype(F32)[:, None, None]

        def term(blocks, columns):
            return blocks.astype(F32).transpose(1, 0, 2).reshape(rank, -1)[:, :columns]

        def placed(terms, first, groups, columns):
            total = jnp.zeros((rank, groups * tok * columns), F32)
            for group in range(groups):
                at = first + group * pieces(columns)
                part = term(terms[at : at + pieces(columns)], columns)
                start = (group * tok + own_tok) * columns
                total = lax.dynamic_update_slice(total, part, (0, start))
            return total

        whole = lambda terms, at: term(terms[at : at + wide], width)

        def joined(kept, at, sent, first):
            half = wide // 2
            mine, other = kept[at : at + half], sent[first : first + half]
            swap = own_tok % 2 == 1
            low, high = jnp.where(swap, other, mine), jnp.where(swap, mine, other)
            return term(jnp.concatenate([low, high]), width)

        sums = (
            joined(keep, late_local, send, 0),
            placed(keep, 0, 3, lanes),
            joined(out_keep, 0, out_send, 0),
            joined(out_keep, wide // 2, out_send, wide // 2),
            whole(early, early_local),
            placed(early, 0, 2, hidden),
            placed(early, 2 * pieces(hidden), 1, hidden),
            whole(early, early_local + wide),
        )
        summed = lax.psum(tuple(picked * part[None] for part in sums), ("seq", "tok"))
        qkv_down_grad, qkv_up_grad, out_down_grad, out_up_grad = summed[:4]
        in_down_grad, in_up_grad, out2_down_grad, out2_up_grad = summed[4:]
    return (
        layer_out[None],
        input_grad[None],
        qkv_down_grad,
        qkv_up_grad,
        out_down_grad,
        out_up_grad,
        in_down_grad,
        in_up_grad,
        out2_down_grad,
        out2_up_grad,
    )


def solution(mesh):
    grid = P("tok", "seq")
    split = P("seq", "tok", None)
    return jax.shard_map(
        body,
        mesh=mesh,
        in_specs=(split, split, P("seq", None), P("seq"), grid, grid, grid, grid, P("tok"), P("tok"))
        + (P(),) * 8,
        out_specs=(split, split) + (P(),) * 8,
        check_vma=False,
    )
```

```python
import functools

import jax
import jax.numpy as jnp
from jax import lax
from jax.experimental import pallas as pl
from jax.experimental.pallas import tpu as pltpu
from jax.sharding import PartitionSpec as P

HEADS = 16
HEAD_DIM = 64
EPS = 1e-05
THETA = 160000.0
F32 = jnp.float32
BF16 = jnp.bfloat16
MIB = 1024 * 1024
RING = (0, 2, 4, 6, 7, 5, 3, 1)


def nn(a, b):
    return lax.dot_general(a, b, (((1,), (0,)), ((), ())), preferred_element_type=F32)


def nt(a, b):
    return lax.dot_general(a, b, (((1,), (1,)), ((), ())), preferred_element_type=F32)


def tn(a, b):
    return lax.dot_general(a, b, (((0,), (0,)), ((), ())), preferred_element_type=F32)


def shape(dims, dtype):
    return jax.ShapeDtypeStruct(tuple(dims), dtype)


PIECE = 256 * 1024


def cuts(dims, item):
    size = item
    for n in dims:
        size *= n
    if size <= PIECE * 3 // 2 or len(dims) == 1:
        return [()]
    if len(dims) == 2:
        step = max(dims[0] * PIECE // size // 16 * 16, 16)
        return [(pl.ds(n, min(step, dims[0] - n)),) for n in range(0, dims[0], step)]
    return [(n,) + rest for n in range(dims[0]) for rest in cuts(dims[1:], item)]


def start_copies(source, target, semaphore):
    for at in cuts(target.shape, target.dtype.itemsize):
        one, two = (source.at[at], target.at[at]) if at else (source, target)
        pltpu.make_async_copy(one, two, semaphore).start()
    return pltpu.make_async_copy(source, target, semaphore)


class Late:
    def __init__(self, source, target, semaphore):
        self.target, self.there = target, False
        self.copy = start_copies(source, target, semaphore)

    def get(self):
        if not self.there:
            self.copy.wait()
            self.there = True
        return self.target


class Here:
    def __init__(self, ref):
        self.ref = ref

    def get(self):
        return self.ref

    def send(self):
        pass


class Early:
    def __init__(self, target, source, semaphore):
        self.ref, self.sent = source, False
        self.ends = (source, target, semaphore)

    def send(self):
        if not self.sent:
            self.copy = start_copies(*self.ends)
            self.sent = True


class Pick:
    def __init__(self, table, pick, start=None, size=None):
        self.table, self.pick = table, pick
        self.start, self.size = start, table.shape[2] if size is None else size


def call(kernel, out_shape, args, scratch=(), smem=(), early=(), name=None):
    picks = {n: a for n, a in enumerate(args) if isinstance(a, Pick)}
    operands = [a.table if isinstance(a, Pick) else a for a in args]
    chosen = [next(iter(picks.values())).pick] if picks else []
    late = list(picks)
    buffers = [
        pltpu.VMEM((args[n].table.shape[1], args[n].size), args[n].table.dtype) for n in late
    ]
    buffers += [pltpu.VMEM(out_shape[n].shape, out_shape[n].dtype) for n in early]
    first_in = len(chosen)

    def body(*refs):
        pick, refs = refs[:first_in], refs[first_in:]
        ins, refs = list(refs[: len(args)]), refs[len(args) :]
        outs, refs = list(refs[: len(out_shape)]), refs[len(out_shape) :]
        own, refs = refs[: len(scratch)], refs[len(scratch) :]
        semaphores = refs[-1]
        for at, n in enumerate(late):
            entry = picks[n]
            columns = slice(None) if entry.start is None else pl.ds(entry.start(), entry.size)
            source = ins[n].at[pick[0][0], :, columns]
            ins[n] = Late(source, refs[at], semaphores.at[at])
        for n in range(len(args)):
            if n not in picks and n not in smem:
                ins[n] = Here(ins[n])
        for at, n in enumerate(early, len(late)):
            outs[n] = Early(outs[n], refs[at], semaphores.at[at])
        kernel(*ins, *outs, *own)
        for n in late:
            ins[n].get()
        for n in early:
            outs[n].send()
            outs[n].copy.wait()

    spaces = [pltpu.SMEM] * first_in + [
        pltpu.SMEM if n in smem else pl.ANY if n in picks else pltpu.VMEM
        for n in range(len(args))
    ]
    return pl.pallas_call(
        body,
        out_shape=list(out_shape),
        in_specs=[pl.BlockSpec(memory_space=space) for space in spaces],
        out_specs=[
            pl.BlockSpec(memory_space=pl.ANY if n in early else pltpu.VMEM)
            for n in range(len(out_shape))
        ],
        scratch_shapes=list(scratch)
        + buffers
        + [pltpu.SemaphoreType.DMA((max(len(late) + len(early), 1),))],
        compiler_params=pltpu.CompilerParams(vmem_limit_bytes=60 * MIB),
        cost_estimate=pl.CostEstimate(flops=1, bytes_accessed=1, transcendentals=0),
        name=name,
    )(*chosen, *operands)


def owner(n, direct):
    return jnp.bitwise_xor(lax.axis_index("tok"), n) if direct else n


def rows_of(n, size):
    if isinstance(n, int):
        return pl.ds(n * size, size)
    return pl.ds(pl.multiple_of(n * size, size), size)


def came_from(n):
    own, size = lax.axis_index("seq"), len(RING)
    place = jnp.where(lax.rem(own, 2) == 0, own // 2, size - 1 - own // 2)
    shift = (0, -1, 1, -2, 2, -3, 3, -4, 4)[n]
    came = lax.rem(place + shift + size, size)
    return jnp.where(came < size // 2, 2 * came, 2 * (size - 1 - came) + 1)


def to_slot(refs, index, value):
    for n, ref in enumerate(refs):

        @pl.when(index == n)
        def _(ref=ref):
            ref[...] = value


def normalized(rows):
    mean = jnp.mean(rows, axis=-1, keepdims=True)
    centered = rows - mean
    scale = lax.rsqrt(jnp.mean(centered * centered, axis=-1, keepdims=True) + EPS)
    return centered * scale, scale


def norm_back(rows, gain, grad):
    unit, scale = normalized(rows)
    weighted = grad * gain
    first = jnp.mean(weighted, axis=-1, keepdims=True)
    second = jnp.mean(weighted * unit, axis=-1, keepdims=True)
    return (weighted - first - unit * second) * scale


def swapped(rows):
    width = rows.shape[1]
    if width % 128:
        half = HEAD_DIM // 2
        parts = []
        for start in range(0, width, HEAD_DIM):
            parts += [rows[:, start + half : start + HEAD_DIM], rows[:, start : start + half]]
        return jnp.concatenate(parts, axis=1)
    lane = lax.broadcasted_iota(jnp.int32, rows.shape, 1)
    ahead = pltpu.roll(rows, width - HEAD_DIM // 2, 1)
    behind = pltpu.roll(rows, HEAD_DIM // 2, 1)
    return jnp.where(lane % HEAD_DIM < HEAD_DIM // 2, ahead, behind)


def widened(table, width):
    if width <= table.shape[1]:
        return table[:, :width]
    return jnp.concatenate([table] * (width // table.shape[1]), axis=1)


def head_part(rows, head):
    lane = lax.broadcasted_iota(jnp.int32, rows.shape, 1)
    return jnp.where(lane // HEAD_DIM == head, rows, jnp.zeros_like(rows))


def chunked(ref, base, value):
    count = -(-value.shape[1] // 128)
    for n in range(count):
        part = value[:, n * 128 : (n + 1) * 128].astype(ref.dtype)
        if part.shape[1] < 128:
            ref[base + n] = jnp.zeros(ref.shape[1:], ref.dtype)
            ref[base + n, :, : part.shape[1]] = part
        else:
            ref[base + n] = part
    return base + count


def halves(keep, at, send, first, value):
    core = lax.rem(lax.axis_index("tok"), 2)
    half = value.shape[1] // 256
    for n in range(2 * half):
        part = value[:, n * 128 : (n + 1) * 128].astype(keep.dtype)

        @pl.when(core == n // half)
        def _(part=part, n=n):
            keep[at + n % half] = part

        @pl.when(core != n // half)
        def _(part=part, n=n):
            send[first + n % half] = part


def labelled(ref, at, pick):
    ref[at] = jnp.full(ref.shape[1:], pick[0].astype(F32)).astype(ref.dtype)


def document_range(block, rows, seg_scalar, seg_row):
    first = seg_scalar[0, block * rows].astype(F32)
    last = seg_scalar[0, block * rows + rows - 1].astype(F32)
    below = jnp.sum(jnp.where(seg_row < first, 1.0, 0.0)).astype(jnp.int32)
    upto = jnp.sum(jnp.where(seg_row <= last, 1.0, 0.0)).astype(jnp.int32)
    return below // rows, (upto + rows - 1) // rows


def prepare_kernel(tokens, gain_one, gain_two, weight, token_out, double, single):
    weight, odd = weight.get(), lax.rem(lax.axis_index("seq"), 2)
    unit = single.shape[1]

    @pl.when(odd == 0)
    def _():
        double[...] = weight[:, : 2 * unit]
        single[...] = weight[:, 2 * unit :]

    @pl.when(odd == 1)
    def _():
        double[...] = weight[:, unit:]
        single[...] = weight[:, :unit]

    tokens = tokens.get()
    rows, part = tokens.shape[0], gain_one.get().shape[0]
    token_out[:rows] = tokens[...]
    token_out[rows:] = jnp.zeros((16, tokens.shape[1]), BF16)
    both = [gain.get()[...].astype(F32).reshape(1, part) for gain in (gain_one, gain_two)]
    token_out[rows : rows + 2, :part] = jnp.concatenate(both, axis=0).astype(BF16)


def adapters_kernel(tok, *refs):
    tables, outs = refs[:8], refs[8:]
    down_one, up_one, down_attn, up_attn, down_two, up_two, down_last, up_last = outs
    for n in (1, 5, 6):
        tables[n].get()
    for table, out in ((0, down_one), (2, down_attn), (3, up_attn), (4, down_two), (7, up_last)):
        out[...] = tables[table].get()[...]
    own = lax.axis_index("tok")
    for n in range(tok):

        @pl.when(own == n)
        def _(n=n):
            down_last[...] = tables[6].get()[:, columns_of(n, 0, down_last.shape[1], tok)]
            for kind in range(3):
                size = up_one.shape[2]
                up_one[kind] = tables[1].get()[:, columns_of(n, kind, size, tok)]
            for kind in range(2):
                size = up_two.shape[2]
                up_two[kind] = tables[5].get()[:, columns_of(n, kind, size, tok)]


def columns_of(own, group, size, tok):
    start = (group * tok + own) * size
    return slice(start, start + size)


def qkv_kernel(pieces, kinds, tokens, down, ups, cosine, sine, *refs):
    weights, refs = refs[:pieces], refs[pieces:]
    norm, gain, query, key, value, whole = refs[:6]
    width = query.shape[1]
    if pieces == 1:
        whole[...] = weights[0].get()[...]
    else:
        out_weight = refs[6]
        unit = width // 2
        own = lax.axis_index("tok")
        first = 0
        for n in range(pieces):
            piece = weights[n].get()
            depth = piece.shape[0]
            spot = came_from(n)
            half, part = spot // 4, lax.rem(spot, 4)
            down_at = pl.ds(pl.multiple_of(part * width + first, depth), depth)
            double, single = kinds[3 * own + half], kinds[3 * own + 2]
            whole[double, down_at, :] = piece[:, :width]
            across = pl.ds(pl.multiple_of(half * unit, unit), unit)
            whole[single, down_at, across] = piece[:, width : width + unit]
            across = pl.ds(pl.multiple_of(spot * unit, unit), unit)
            out_weight[first : first + depth, across] = piece[:, width + unit :]
            first = (first + depth) % width
    for kind in range(3):
        product = tn(down.get()[...], ups.get()[kind])
        whole[kind] = (whole[kind].astype(F32) + product).astype(BF16)
    tokens, cosine, sine = tokens.get(), cosine.get(), sine.get()
    count, block = tokens.shape[0], tokens.shape[1] - 16
    for n in range(count):
        part = gain.shape[1] // count
        gain[:, n * part : (n + 1) * part] = tokens[n, block:, :part].astype(F32)[:2]

    def step(n, _):
        at = rows_of(n, block)
        unit, _ = normalized(tokens[n, :block].astype(F32))
        rows = (unit * gain[0:1, :]).astype(BF16)
        norm[at, :] = rows
        cos, sin = widened(cosine[at, :], width), widened(sine[at, :], width)
        for kind, out in enumerate((query, key, value)):
            part = nn(rows, whole[kind])
            if kind < 2:
                part = part * cos + swapped(part) * sin
            if kind == 0:
                part = part.astype(BF16).astype(F32) * 0.125
            out[at, :] = part.astype(BF16)
        return 0

    lax.fori_loop(0, count, step, 0)


def attend_kernel(count, direct, seg_scalar, query, key, value, segments, *refs):
    outs, (log_total, mixed_t, value_t, seg_t) = refs[:count], refs[count:]
    segments = segments.get()
    seg_row = segments[...].astype(F32)
    seg_t[...] = jnp.broadcast_to(seg_row, (128, seg_row.shape[1])).T
    query, key, value = query.get(), key.get(), value.get()
    block = outs[0].shape[0]
    width = query.shape[1]
    heads = width // HEAD_DIM
    value_t[...] = value[...].T
    parts = [slice(head * HEAD_DIM, (head + 1) * HEAD_DIM) for head in range(heads)]

    def step(n, _):
        place = owner(n, direct)
        at = rows_of(place, block)
        rows = query[at, :]
        own = [head_part(rows, head) for head in range(heads)]
        seg_here = segments[:, at].astype(F32)

        def against(m, carry):
            tops, sums, mixed = carry
            keys = rows_of(m, block)
            column = widened(seg_t[keys, :], block)
            bias = jnp.where(column == seg_here, 0.0, -1e30)
            near = key[keys, :]
            scores = [nt(near, part) + bias for part in own]
            now = [
                jnp.maximum(top, jnp.max(part, axis=0, keepdims=True))
                for top, part in zip(tops, scores)
            ]
            raised = [jnp.exp(part - top) for part, top in zip(scores, now)]
            scale = [jnp.exp(before - top) for before, top in zip(tops, now)]
            added = [nn(value_t[part, keys], up.astype(BF16)) for part, up in zip(parts, raised)]
            sums = [
                total * by + jnp.sum(up, axis=0, keepdims=True)
                for total, by, up in zip(sums, scale, raised)
            ]
            mixed = [old * by + new for old, by, new in zip(mixed, scale, added)]
            return now, sums, mixed

        start = (
            [jnp.full((1, block), -2e30, F32)] * heads,
            [jnp.zeros((1, block), F32)] * heads,
            [jnp.zeros((HEAD_DIM, block), F32)] * heads,
        )
        first, last = document_range(place, block, seg_scalar, seg_row)
        tops, sums, mixed = lax.fori_loop(first, last, against, start)
        for head in range(heads):
            log_total[head : head + 1, at] = tops[head] + jnp.log(sums[head])
            mixed_t[n, parts[head], :] = mixed[head] * (1.0 / sums[head])
        to_slot(outs, n, mixed_t[n].T.astype(BF16))
        return 0

    lax.fori_loop(0, count, step, 0)


def features(n, width, direct):
    if not direct:
        return slice(n * width, (n + 1) * width)
    return pl.ds(pl.multiple_of(owner(n, direct) * width, width), width)


def out_kernel(count, direct, inputs, gain, down, up, *refs):
    attn, weights = refs[:count], refs[count : 2 * count]
    middle, norm, narrow = refs[2 * count :]
    down = down.get()
    total = inputs.get()[...].astype(F32)
    thin = jnp.zeros(narrow.shape, F32)
    for n in range(count):
        rows = attn[n].get()[...]
        total = total + nn(rows, weights[n].get()[...])
        thin = thin + nt(rows, down[:, features(n, rows.shape[1], direct)])
    thin = thin.astype(BF16)
    total = total + nn(thin, up.get()[...])
    middle[...] = total
    narrow[...] = thin
    norm[...] = (normalized(total)[0] * gain.get()[1:2, :]).astype(BF16)


def mlp_pre_kernel(packed, direct, down_in, up_in, down_out, up_out, grads, *refs):
    pieces = 9 if packed else 2
    weights, refs = refs[:pieces], refs[pieces:]
    w_in, w_out, grad_early, grad_late = refs
    hidden, width = w_out.shape
    if packed:
        depth, thin = width // 4, width // 8
        first = 0
        for n in range(pieces):
            piece = weights[n].get()
            rows = slice(first, first + piece.shape[0])
            spot = came_from(n)
            across = pl.ds(pl.multiple_of(lax.rem(spot, 4) * depth, depth), depth)
            w_in[spot // 4, rows, across] = piece[:, :depth]
            across = pl.ds(pl.multiple_of(spot * thin, thin), thin)
            w_out[rows, across] = piece[:, depth:]
            first = rows.stop % hidden
    else:
        w_in[...] = weights[0].get()[...]
        w_out[...] = weights[1].get()[...]
    for n in range(2):
        w_in[n] = (w_in[n].astype(F32) + tn(up_in.get()[n], down_in.get()[...])).astype(BF16)
    w_out[...] = (w_out[...].astype(F32) + tn(down_out.get()[...], up_out.get()[...])).astype(BF16)
    grads = grads.get()
    for n in range(grads.shape[0]):
        target = grad_early if n < 2 else grad_late
        target[n if n < 2 else n - 2] = nt(grads[owner(n, direct)], w_out[...])


def mlp_kernel(count, first, w_in, grad_act, *refs):
    norms, backs, (act_out, grad_out) = refs[:count], refs[count : 2 * count], refs[2 * count :]
    w_in, grad_act = w_in.get(), grad_act.get()
    for n in range(count):
        norm = norms[n].get()[...]
        inputs, gate = nt(norm, w_in[0]), nt(norm, w_in[1])
        phi = 0.5 + 0.5 * lax.erf(inputs * (0.5**0.5))
        gelu = inputs * phi
        act_out[n] = (gelu * gate).astype(BF16)
        back_act = grad_act[first + n]
        slope = phi + inputs * (jnp.exp(-0.5 * inputs * inputs) * 0.3989422804014327)
        grad_inputs = (back_act * gate * slope).astype(BF16)
        grad_gate = (back_act * gelu).astype(BF16)
        grad_out[0, n] = grad_inputs
        grad_out[1, n] = grad_gate
        backs[n][...] = (nn(grad_inputs, w_in[0]) + nn(grad_gate, w_in[1])).astype(BF16)


def mlp_terms_kernel(count, first, direct, pick, down_in, up_in, down_out, up_out, *refs):
    acts, grads, out_grad, refs = refs[:2], refs[2:4], refs[4], refs[5:]
    norms, terms = refs[:count], refs[count]
    down_in_grad = down_out_grad = up_out_grad = 0.0
    up_in_grad = [0.0, 0.0]
    down_in, up_in, down_out, up_out = down_in.get(), up_in.get(), down_out.get(), up_out.get()
    for n in range(count):
        norm = norms[n].get()[...]
        narrow = nt(norm, down_in[...]).astype(BF16)
        back = [grads[n // 2].get()[h, n % 2] for h in range(2)]
        inner_in = (nt(back[0], up_in[0]) + nt(back[1], up_in[1])).astype(BF16)
        down_in_grad = down_in_grad + tn(inner_in, norm)
        for h in range(2):
            up_in_grad[h] = up_in_grad[h] + tn(narrow, back[h])
        act = acts[n // 2].get()[n % 2]
        grad = out_grad.get()[owner(first + n, direct)]
        narrow_two = nt(act, down_out[...]).astype(BF16)
        inner = nt(grad, up_out[...]).astype(BF16)
        down_out_grad = down_out_grad + tn(inner, act)
        up_out_grad = up_out_grad + tn(narrow_two, grad)
    at = chunked(terms, 0, up_in_grad[0])
    at = chunked(terms, at, up_in_grad[1])
    at = chunked(terms, at, down_out_grad)
    labelled(terms, at, pick)
    at = chunked(terms, at + 1, down_in_grad)
    chunked(terms, at, up_out_grad)


def mlp_out_kernel(count, w_out, *refs):
    acts, outs = refs[: count // 2], refs[count // 2 :]
    w_out = w_out.get()
    for n in range(count):
        outs[n].ref[...] = nn(acts[n // 2].get()[n % 2], w_out[...]).astype(BF16)
        outs[n].send()


def out_back_kernel(count, parts, direct, middle, out_grad, gain, down, up, narrow, *refs):
    back, refs = refs[:parts], refs[parts:]
    attn, weights = refs[:count], refs[count : 2 * count]
    grad_mid, refs = refs[2 * count], refs[2 * count + 1 :]
    slots, (keep, send, down_grad) = refs[:count], refs[count:]
    total = sum(ref.get()[...].astype(F32) for ref in back)
    grad = out_grad.get()[...].astype(F32)
    grad = grad + norm_back(middle.get()[...], gain.get()[1:2, :], total)
    grad_mid[...] = grad
    low = grad.astype(BF16)
    down = down.get()
    inner = nt(low, up.get()[...]).astype(BF16)
    for n in range(count):
        rows = attn[n].get()[...]
        own = features(n, rows.shape[1], direct)
        slots[n][...] = (nt(low, weights[n].get()[...]) + nn(inner, down[:, own])).astype(BF16)
        down_grad[:, own] = tn(inner, rows)
    half = grad.shape[1] // 256
    halves(keep, half, send, half, tn(narrow.get()[...], low))
    halves(keep, 0, send, 0, down_grad[...])


def attend_back_kernel(
    count, direct, seg_scalar, pick, query, key, value, segments, log_total, mixed_t, cosine, sine,
    down, ups, norm, *refs
):
    grads, (grad_qkv, keep, send) = refs[:count], refs[count : count + 3]
    key_t, seg_t, grad_q, grad_k, grad_v, query_t, grad_all = refs[count + 3 :]
    segments = segments.get()
    seg_row = segments[...].astype(F32)
    seg_t[...] = jnp.broadcast_to(seg_row, (128, seg_row.shape[1])).T
    for ref in (grad_k, grad_v):
        ref[...] = jnp.zeros_like(ref)
    query, key, value = query.get(), key.get(), value.get()
    log_total, mixed_t = log_total.get(), mixed_t.get()
    block = grads[0].get().shape[0]
    width = query.shape[1]
    heads = width // HEAD_DIM
    key_t[...] = key[...].T
    for n in range(count):
        grad_all[n] = grads[n].get()[...]
    parts = [slice(head * HEAD_DIM, (head + 1) * HEAD_DIM) for head in range(heads)]

    def step(n, _):
        place = owner(n, direct)
        at = rows_of(place, block)
        rows, grad = query[at, :], grad_all[n]
        own = [head_part(rows, head) for head in range(heads)]
        own_grad = [head_part(grad, head) for head in range(heads)]
        product = grad.astype(F32).T * mixed_t[n]
        dots = [jnp.sum(product[part], axis=0, keepdims=True) for part in parts]
        query_t[...] = jnp.zeros_like(query_t)
        seg_here = segments[:, at].astype(F32)

        def against(m, _):
            keys = rows_of(m, block)
            column = widened(seg_t[keys, :], block)
            bias = jnp.where(column == seg_here, 0.0, -1e30)
            near, near_value = key[keys, :], value[keys, :]
            probs = [
                jnp.exp(nt(near, own[head]) + bias - log_total[head : head + 1, at])
                for head in range(heads)
            ]
            grad_probs = [nt(near_value, part) for part in own_grad]
            grad_s = [
                (prob * (grad_prob - dot)).astype(BF16)
                for prob, grad_prob, dot in zip(probs, grad_probs, dots)
            ]
            sum_v = sum(nn(prob.astype(BF16), part) for prob, part in zip(probs, own_grad))
            sum_k = sum(nn(part, mine) for part, mine in zip(grad_s, own))
            for head in range(heads):
                query_t[parts[head], :] += nn(key_t[parts[head], keys], grad_s[head])
            grad_k[keys, :] += sum_k
            grad_v[keys, :] += sum_v
            return 0

        first, last = document_range(place, block, seg_scalar, seg_row)
        lax.fori_loop(first, last, against, 0)
        grad_q[at, :] = query_t[...].T * 0.125
        return 0

    lax.fori_loop(0, count, step, 0)
    cosine, sine = cosine.get(), sine.get()

    def finish(n, _):
        at = rows_of(n, block)
        cos, sin = widened(cosine[at, :], width), widened(sine[at, :], width)
        for kind, ref in enumerate((grad_q, grad_k)):
            part = ref[at, :]
            grad_qkv[kind, at, :] = (part * cos - swapped(part) * sin).astype(BF16)
        grad_qkv[2, at, :] = grad_v[at, :].astype(BF16)
        return 0

    lax.fori_loop(0, count, finish, 0)
    norm = norm.get()
    inner = sum(nt(grad_qkv[kind], ups.get()[kind]) for kind in range(3))
    narrow = nt(norm[...], down.get()[...]).astype(BF16)
    at = 0
    for kind in range(3):
        at = chunked(keep, at, tn(narrow, grad_qkv[kind]))
    labelled(keep, at, pick)
    halves(keep, at + 1, send, 0, tn(inner.astype(BF16), norm[...]))


def qkv_back_kernel(count, direct, grad_qkv, weights, *outs):
    block = outs[0].ref.shape[0]
    grad_qkv, weights = grad_qkv.get(), weights.get()
    for n in list(range(1, count, 2)) + list(range(0, count, 2)):
        at = rows_of(owner(n, direct), block)
        total = sum(nt(grad_qkv[kind, at, :], weights[kind]) for kind in range(3))
        outs[n].ref[...] = total.astype(BF16)
        outs[n].send()


def layer_kernel(middle, *refs):
    total = middle.get()[...] + sum(ref.get()[...].astype(F32) for ref in refs[:-1])
    refs[-1][...] = total.astype(BF16)


def last_kernel(inputs, grad_mid, gain, *refs):
    total = sum(ref.get()[...].astype(F32) for ref in refs[:-1])
    back = norm_back(inputs.get()[...].astype(F32), gain.get()[0:1, :], total)
    refs[-1][...] = (grad_mid.get()[...] + back).astype(BF16)


def pair_kernel(local, own, came, out):
    own, came = own.get(), came.get()
    across = lax.axis_index("tok") // 2
    out[pl.ds(across * local, local)] = own[:local]
    out[pl.ds((1 - across) * local, local)] = came[:local]
    out[2 * local :] = (own[local:].astype(F32) + came[local:].astype(F32)).astype(BF16)


def late_kernel(local, keep, came, out_keep, out_came, out):
    keep, out_keep = keep.get(), out_keep.get()
    out[:local] = keep[:local]
    half = keep.shape[0] - local
    total = keep[local:].astype(F32) + came.get()[...].astype(F32)
    out[local : local + half] = total.astype(BF16)
    total = out_keep[...].astype(F32) + out_came.get()[...].astype(F32)
    out[local + half :] = total.astype(BF16)


def stack_kernel(*refs):
    out = refs[-1]
    first = 0
    for n, ref in enumerate(refs[:-1]):
        block = ref.get()
        size = block.shape[0]
        out[came_from(n), first : first + size] = block[...]
        first = (first + size) % out.shape[1]


def spread_kernel(widths, local, count, *refs):
    mine, other, refs = refs[:count], refs[count : 2 * count], refs[2 * count :]
    outs, both = refs[: len(widths)], refs[len(widths)]
    core = lax.rem(lax.axis_index("tok"), 2)
    own = lax.axis_index("seq") // 2
    for n in range(count):
        size = mine[n].get().shape[0]
        at = pl.ds(jnp.bitwise_xor(own, n) * size, size) if count > 1 else slice(None)
        both[core, at] = mine[n].get()[...]
        both[1 - core, at] = other[n].get()[...]
    for out in outs:
        out[...] = jnp.zeros_like(out)

    def step(n, _):
        pick = jnp.max(both[0, n, local - 1].astype(F32)).astype(jnp.int32)
        at, rest = 0, 2 * local
        for out, width in zip(outs, widths):
            if width <= 0:
                chunks = out.shape[2] // 128
                for m in range(chunks):
                    if width == 0:
                        term = both[0, n, rest + m].astype(F32) + both[1, n, rest + m].astype(F32)
                    else:
                        term = both[2 * m // chunks, n, rest + m % (chunks // 2)].astype(F32)
                    out[pick, :, m * 128 : (m + 1) * 128] += term
                rest += chunks if width == 0 else chunks // 2
                continue
            blocks = -(-width // 128)
            for group in range(out.shape[2] // (4 * width)):
                for tok in range(4):
                    first = (group * 4 + tok) * width
                    base = (tok // 2) * local + at
                    parts = [both[tok % 2, n, base + m] for m in range(blocks)]
                    term = jnp.concatenate(parts, axis=1)[:, :width].astype(F32)
                    out[pick, :, first : first + width] += term
                at += blocks
        return 0

    lax.fori_loop(0, both.shape[1], step, 0)


class Exchange:
    def __init__(self, size):
        self.size = size
        self.direct = size == 4

    def swap(self, block, bits):
        pairs = [(n, n ^ bits) for n in range(self.size)]
        return lax.ppermute(block, "tok", pairs)

    def hop(self, block):
        if not self.direct:
            whole = lax.all_gather(block, "tok", axis=0)
            return [whole[n] for n in range(self.size)]
        return [block, self.swap(block, 1), self.swap(block, 2)]

    def land(self, parts):
        if not self.direct:
            return parts
        return parts + [self.swap(parts[2], 1)]

    def turn(self, slots):
        if not self.direct:
            whole = lax.all_to_all(jnp.stack(slots), "tok", 0, 0)
            return [whole[n] for n in range(self.size)]
        return [slots[0]] + [self.swap(slots[n], n) for n in range(1, self.size)]

    def halve(self, slots):
        near, far = self.swap(slots[1], 1), self.swap(slots[3], 1)
        both = (slots[2].astype(F32) + far.astype(F32)).astype(far.dtype)
        return near, both

    def reduce(self, slots):
        if not self.direct:
            return [lax.psum_scatter(jnp.stack(slots), "tok", scatter_dimension=0)]
        near, both = self.halve(slots)
        return [slots[0], near, self.swap(both, 2)]


def meet(*arrays):
    return lax.optimization_barrier(arrays)


class Ring:
    def __init__(self, block):
        self.blocks = [block]
        self.right = self.left = block
        self.half = block.shape[0] // 32 * 16 if block.ndim == 2 else block.shape[0] // 2
        self.ahead = [(RING[n], RING[(n + 1) % len(RING)]) for n in range(len(RING))]
        self.behind = [(b, a) for a, b in self.ahead]

    def step(self):
        step = len(self.blocks) // 2 + 1
        if step == len(RING) // 2:
            self.right, self.left = self.right[: self.half], self.left[self.half :]
        self.right = lax.ppermute(self.right, "seq", self.ahead)
        self.left = lax.ppermute(self.left, "seq", self.behind)
        self.blocks += [self.right, self.left]

    def meet(self, *arrays):
        self.right, self.left, *arrays = meet(self.right, self.left, *arrays)
        if len(self.blocks) > 1:
            self.blocks[-2:] = [self.right, self.left]
        return arrays


def owner_of_columns(seq, tok):
    double, single, seen = [], [], [0] * tok
    kinds = [[0, 0, 0] for _ in range(tok)]
    for s in range(seq):
        first = 3 * s + s % 2
        own = first % seq // 2
        double.append((own, seen[own]))
        kinds[own][seen[own]] = first // seq
        seen[own] += 1
        last = 3 * s + 2 * (1 - s % 2)
        single.append((last % seq // 2, last % 2))
        kinds[last % seq // 2][2] = last // seq
    return double, single, kinds


def body(
    tokens,
    out_grad,
    segments,
    adapter_index,
    qkv_weight,
    out_weight,
    in_weight,
    out2_weight,
    attn_gain,
    mlp_gain,
    qkv_down,
    qkv_up,
    out_down,
    out_up,
    in_down,
    in_up,
    out2_down,
    out2_up,
):
    seq, tok = lax.axis_size("seq"), lax.axis_size("tok")
    own_tok = lax.axis_index("tok")
    move = Exchange(tok)
    direct = move.direct
    fast = direct and seq == 8
    adapters, rank, width = qkv_down.shape
    length = segments.shape[1]
    rows = tokens.shape[1]
    heads = HEADS // tok
    lanes = heads * HEAD_DIM
    hidden = out2_weight.shape[0]
    hidden_all = hidden * tok
    inputs, out_grad = tokens[0], out_grad[0]
    pick = adapter_index[0]
    pieces = lambda columns: -(-columns // 128)
    early_local, late_local = 3 * pieces(hidden) + 1, 3 * pieces(lanes) + 1
    wide = pieces(width)

    sizes = ((width, 0), (lanes, 3), (width, 0), (width, 0), (width, 0), (hidden, 2), (hidden, 1), (width, 0))
    tables = (qkv_down, qkv_up, out_down, out_up, in_down, in_up, out2_down, out2_up)
    if fast:
        adapters_own = call(
            functools.partial(adapters_kernel, tok),
            [
                shape((groups,) * (groups > 1) + (rank, columns), BF16)
                for columns, groups in sizes
            ],
            [Pick(table, adapter_index) for table in tables],
            name="adapters",
        )
    else:

        def chosen(table, columns, groups):
            parts = []
            for group in range(max(groups, 1)):
                start = (group * tok + own_tok) * columns if groups else 0
                parts.append(lax.dynamic_slice(table, (pick, 0, start), (1, rank, columns))[0])
            return jnp.stack(parts) if groups > 1 else parts[0]

        adapters_own = [chosen(table, *size) for table, size in zip(tables, sizes)]

    exponent = jnp.arange(0, HEAD_DIM, 2).astype(F32) / HEAD_DIM
    inverse = 1.0 / THETA**exponent
    phases = jnp.arange(length).astype(F32)[:, None] * jnp.tile(inverse, 4)[None, :]
    sign = jnp.where(jnp.arange(2 * HEAD_DIM) % HEAD_DIM < HEAD_DIM // 2, -1.0, 1.0)
    cosine, sine = jnp.cos(phases), jnp.sin(phases) * sign[None, :]

    if fast:
        unit = width // seq
        double, single, kinds = owner_of_columns(seq, tok)
        kinds = jnp.array(sum(kinds, []), jnp.int32)
        token_block, *parts = call(
            prepare_kernel,
            [
                shape((rows + 16, width), BF16),
                shape((qkv_weight.shape[0], 2 * unit), BF16),
                shape((qkv_weight.shape[0], unit), BF16),
            ],
            [inputs, attn_gain, mlp_gain, qkv_weight],
            name="prepare",
        )
        for n, owners in enumerate((double, single)):
            pairs = [
                (s * tok + t, (owners[s][1] * tok + t) * tok + owners[s][0])
                for s in range(seq)
                for t in range(tok)
            ]
            parts[n] = lax.ppermute(parts[n], ("seq", "tok"), pairs)
        pairs = [
            (s * tok + t, ((s // tok) * tok + t) * tok + s % tok)
            for s in range(seq)
            for t in range(tok)
        ]
        in_piece = lax.ppermute(in_weight.T, ("seq", "tok"), pairs)
        together = meet(token_block, cosine, sine, *adapters_own, in_piece, *parts)
        token_block, cosine, sine, adapters_own = *together[:3], together[3:11]
        in_piece, *parts = together[11:]
        ring = Ring(jnp.concatenate(parts + [out_weight], axis=1))
        ring.step()
        ring.step()
        (out_grad_in,) = ring.meet(out_grad)
        ring.step()
        ring.step()
        mlp_piece = jnp.concatenate([in_piece, out2_weight], axis=1)
        (mlp_piece,) = ring.meet(mlp_piece)
        qkv_pieces = ring.blocks
        mlp_ring = Ring(mlp_piece)
        mlp_ring.step()
    else:

        def columns(weight, count):
            block = lax.all_gather(weight, "seq", axis=1, tiled=True)
            split = block.reshape(block.shape[0], count, tok, -1).transpose(2, 1, 0, 3)
            turned = lax.all_to_all(split, "tok", 0, 0)
            return turned.transpose(1, 0, 2, 3).reshape(count, width, -1)

        gain_rows = jnp.stack([attn_gain, mlp_gain])
        gain_rows = jnp.pad(gain_rows, ((0, 14), (0, width - width // tok)))
        token_block = jnp.concatenate([inputs, gain_rows], axis=0)
        out_grad_in = out_grad
        qkv_pieces = [columns(qkv_weight, 3)]
        kinds = jnp.zeros((1,), jnp.int32)
        own_out = lax.all_gather(out_weight, "seq", axis=1, tiled=True)
        mlp_weights = [
            columns(in_weight, 2).transpose(0, 2, 1),
            lax.all_gather(out2_weight, "seq", axis=1, tiled=True),
        ]
    token_all = lax.all_gather(token_block, "tok", axis=0)
    grad_all = lax.all_gather(out_grad_in, "tok", axis=0)

    down_one, up_one, down_attn, up_attn, down_two, up_two, down_last, up_last = adapters_own

    norm_one, gain, query, key, value, w_qkv, *own_row = call(
        functools.partial(qkv_kernel, len(qkv_pieces)),
        [shape((length, width), BF16), shape((2, width), F32)]
        + [shape((length, lanes), BF16)] * 3
        + [shape((3, width, lanes), BF16)]
        + [shape((lanes, width), BF16)] * fast,
        [kinds, token_all, down_one, up_one, cosine, sine] + qkv_pieces,
        smem=(0,),
        name="qkv",
    )
    if fast:
        query, key, value = mlp_ring.meet(query, key, value)
        mlp_ring.step()
    out_parts = move.hop(own_row[0] if fast else own_out)
    *attn_slots, log_total, mixed_t = call(
        functools.partial(attend_kernel, tok, direct),
        [shape((rows, lanes), BF16)] * tok
        + [shape((heads, length), F32), shape((tok, lanes, rows), F32)],
        [segments, query, key, value, segments],
        smem=(0,),
        scratch=[pltpu.VMEM((lanes, length), BF16), pltpu.VMEM((length, 128), F32)],
        name="attend",
    )
    attn_slots, out_parts = meet(attn_slots, out_parts)
    if fast:
        attn_slots = mlp_ring.meet(*attn_slots)
        mlp_ring.step()
    attn = move.turn(attn_slots)
    out_weights = move.land(out_parts)
    middle, norm_two, narrow_attn = call(
        functools.partial(out_kernel, tok, direct),
        [shape((rows, width), F32), shape((rows, width), BF16), shape((rows, rank), BF16)],
        [inputs, gain, down_attn, up_attn] + attn + out_weights,
        name="out",
    )
    if fast:
        (norm_two,) = mlp_ring.meet(norm_two)
        mlp_ring.step()
        mlp_weights = mlp_ring.blocks
    norm_slots = move.hop(norm_two)
    w_in, w_out, *grad_acts = call(
        functools.partial(mlp_pre_kernel, fast, direct),
        [
            shape((2, hidden, width), BF16),
            shape((hidden, width), BF16),
            shape((2, rows, hidden), F32),
            shape((tok - 2, rows, hidden), F32),
        ],
        [down_two, up_two, down_last, up_last, grad_all] + mlp_weights,
        name="mlp_pre",
    )
    back_slots, acts, grads_z = [], [], []
    for first in range(0, tok, 2):
        *backs, act, grad_z = call(
            functools.partial(mlp_kernel, 2, max(first - 2, 0)),
            [shape((rows, width), BF16)] * 2
            + [shape((2, rows, hidden), BF16), shape((2, 2, rows, hidden), BF16)],
            [w_in, grad_acts[min(first, 1)]] + norm_slots[first : first + 2],
            name="mlp",
        )
        if first == 0:
            *backs, norm_slots[2] = meet(*backs, norm_slots[2])
            norm_slots = move.land(norm_slots)
        back_slots += backs
        acts.append(act)
        grads_z.append(grad_z)
    back_two = move.reduce(back_slots)
    out_slots, early = [], []
    for first in range(0, tok, 4):
        pair = slice(first // 2, first // 2 + 2)
        terms = call(
            functools.partial(mlp_terms_kernel, 4, first, direct),
            [shape((early_local + 2 * wide, rank, 128), BF16 if fast else F32)],
            [adapter_index, down_two, up_two, down_last, up_last]
            + acts[pair]
            + grads_z[pair]
            + [grad_all]
            + norm_slots[first : first + 4],
            smem=(0,),
            name="mlp_terms",
        )[0]
        early.append(terms)
    early = sum(early[1:], early[0])
    if fast:
        early = call(
            functools.partial(pair_kernel, early_local),
            [shape((early_local + early.shape[0], rank, 128), BF16)],
            [early, move.swap(early, 2)],
            name="pair",
        )[0]
    grad_mid, *rest = call(
        functools.partial(out_back_kernel, tok, len(back_two), direct),
        [shape((rows, width), F32)]
        + [shape((rows, lanes), BF16)] * tok
        + [shape((wide, rank, 128), BF16)] * 2,
        [middle, out_grad, gain, down_attn, up_attn, narrow_attn] + back_two + attn + out_weights,
        scratch=[pltpu.VMEM((rank, width), F32)],
        name="out_back",
    )
    rest[0], *acts = meet(rest[0], *acts)
    for first in range(0, tok, 4):
        out_slots += call(
            functools.partial(mlp_out_kernel, 4),
            [shape((rows, width), BF16)] * 4,
            [w_out] + acts[first // 2 : first // 2 + 2],
            early=(0, 1, 2, 3),
            name="mlp_out",
        )
    out_keep, out_send = rest[tok:]
    attn_grads = move.turn(rest[:tok])
    if fast:
        attn_grads, out_slots, early = meet(attn_grads, out_slots, early)
        early = lax.all_gather(early, "seq", axis=0)
    out_parts = move.turn(out_slots) if fast else move.reduce(out_slots)
    grad_qkv, keep, send = call(
        functools.partial(attend_back_kernel, tok, direct),
        [
            shape((3, length, lanes), BF16),
            shape((late_local + wide // 2, rank, 128), BF16),
            shape((wide // 2, rank, 128), BF16),
        ],
        [segments, adapter_index, query, key, value, segments, log_total, mixed_t, cosine, sine]
        + [down_one, up_one, norm_one]
        + attn_grads,
        smem=(0, 1),
        scratch=[
            pltpu.VMEM((lanes, length), BF16),
            pltpu.VMEM((length, 128), F32),
            pltpu.VMEM((length, lanes), F32),
            pltpu.VMEM((length, lanes), F32),
            pltpu.VMEM((length, lanes), F32),
            pltpu.VMEM((lanes, rows), F32),
            pltpu.VMEM((tok, rows, lanes), BF16),
        ],
        name="attend_back",
    )

    def slots_of_one(grad_qkv):
        return call(
            functools.partial(qkv_back_kernel, tok, direct),
            [shape((rows, width), BF16)] * tok,
            [grad_qkv, w_qkv],
            early=tuple(range(tok)),
            name="qkv_back",
        )

    def layer_of(out_parts):
        output = [shape((rows, width), BF16)]
        return call(layer_kernel, output, [middle] + out_parts, name="layer")[0]

    def last_of(back_one):
        return call(
            last_kernel,
            [shape((rows, width), BF16)],
            [inputs, grad_mid, gain] + back_one,
            name="last",
        )[0]

    grads = lambda columns: shape((adapters, rank, columns), F32)
    if fast:

        def spread(parts, local, widths, columns):
            return call(
                functools.partial(spread_kernel, widths, local, len(parts)),
                [grads(size) for size in columns],
                parts + [move.swap(part, 1) for part in parts],
                scratch=[pltpu.VMEM((2, seq) + parts[0].shape[1:], BF16)],
                name="spread",
            )

        keep, *out_parts = meet(keep, *out_parts)
        layer_out = layer_of(out_parts)
        late = call(
            functools.partial(late_kernel, late_local),
            [shape((late_local + 3 * wide // 2, rank, 128), BF16)],
            [keep, move.swap(send, 1), out_keep, move.swap(out_send, 1)],
            name="late",
        )[0]
        late_came = move.swap(late, 2)
        late, grad_qkv = meet(late, grad_qkv)
        one_slots = slots_of_one(grad_qkv)
        near, both = move.halve(one_slots)
        both, late_came = meet(both, late_came)
        back_one = [one_slots[0], near, move.swap(both, 2)]
        late = call(
            functools.partial(pair_kernel, late_local),
            [shape((late_local + late.shape[0], rank, 128), BF16)],
            [late, late_came],
            name="pair_late",
        )[0]
        ring = Ring(late)
        ring.step()
        layer_out, back_one[2] = ring.meet(layer_out, back_one[2])
        ring.step()
        input_grad, early = ring.meet(last_of(back_one), early)
        ring.step()
        ring.step()
        in_up_grad, out2_down_grad, in_down_grad, out2_up_grad = spread(
            [early], early_local, (hidden, hidden, 0, 0), (2 * hidden_all, hidden_all, width, width)
        )
        (in_up_grad,) = ring.meet(in_up_grad)
        stacked = shape((seq,) + late.shape, BF16)
        blocks = list(call(stack_kernel, [stacked], ring.blocks, name="stack"))
        qkv_up_grad, qkv_down_grad, out_down_grad, out_up_grad = spread(
            blocks, late_local, (lanes, -1, -1, -1), (3 * width, width, width, width)
        )
    else:
        layer_out = layer_of(out_parts)
        input_grad = last_of(move.reduce(slots_of_one(grad_qkv)))
        picked = (pick == jnp.arange(adapters)).astype(F32)[:, None, None]

        def term(blocks, columns):
            return blocks.astype(F32).transpose(1, 0, 2).reshape(rank, -1)[:, :columns]

        def placed(terms, first, groups, columns):
            total = jnp.zeros((rank, groups * tok * columns), F32)
            for group in range(groups):
                at = first + group * pieces(columns)
                part = term(terms[at : at + pieces(columns)], columns)
                start = (group * tok + own_tok) * columns
                total = lax.dynamic_update_slice(total, part, (0, start))
            return total

        whole = lambda terms, at: term(terms[at : at + wide], width)

        def joined(kept, at, sent, first):
            half = wide // 2
            mine, other = kept[at : at + half], sent[first : first + half]
            swap = own_tok % 2 == 1
            low, high = jnp.where(swap, other, mine), jnp.where(swap, mine, other)
            return term(jnp.concatenate([low, high]), width)

        sums = (
            joined(keep, late_local, send, 0),
            placed(keep, 0, 3, lanes),
            joined(out_keep, 0, out_send, 0),
            joined(out_keep, wide // 2, out_send, wide // 2),
            whole(early, early_local),
            placed(early, 0, 2, hidden),
            placed(early, 2 * pieces(hidden), 1, hidden),
            whole(early, early_local + wide),
        )
        summed = lax.psum(tuple(picked * part[None] for part in sums), ("seq", "tok"))
        qkv_down_grad, qkv_up_grad, out_down_grad, out_up_grad = summed[:4]
        in_down_grad, in_up_grad, out2_down_grad, out2_up_grad = summed[4:]
    return (
        layer_out[None],
        input_grad[None],
        qkv_down_grad,
        qkv_up_grad,
        out_down_grad,
        out_up_grad,
        in_down_grad,
        in_up_grad,
        out2_down_grad,
        out2_up_grad,
    )


def solution(mesh):
    grid = P("tok", "seq")
    split = P("seq", "tok", None)
    return jax.shard_map(
        body,
        mesh=mesh,
        in_specs=(split, split, P("seq", None), P("seq"), grid, grid, grid, grid, P("tok"), P("tok"))
        + (P(),) * 8,
        out_specs=(split, split) + (P(),) * 8,
        check_vma=False,
    )
```

```python
import functools

import jax
import jax.numpy as jnp
from jax import lax
from jax.experimental import pallas as pl
from jax.experimental.pallas import tpu as pltpu
from jax.sharding import PartitionSpec as P

HEADS = 16
HEAD_DIM = 64
EPS = 1e-05
THETA = 160000.0
F32 = jnp.float32
BF16 = jnp.bfloat16
MIB = 1024 * 1024
RING = (0, 2, 4, 6, 7, 5, 3, 1)


def nn(a, b):
    return lax.dot_general(a, b, (((1,), (0,)), ((), ())), preferred_element_type=F32)


def nt(a, b):
    return lax.dot_general(a, b, (((1,), (1,)), ((), ())), preferred_element_type=F32)


def tn(a, b):
    return lax.dot_general(a, b, (((0,), (0,)), ((), ())), preferred_element_type=F32)


def shape(dims, dtype):
    return jax.ShapeDtypeStruct(tuple(dims), dtype)


PIECE = 256 * 1024


def cuts(dims, item):
    size = item
    for n in dims:
        size *= n
    if size <= PIECE * 3 // 2 or len(dims) == 1:
        return [()]
    if len(dims) == 2:
        step = max(dims[0] * PIECE // size // 16 * 16, 16)
        return [(pl.ds(n, min(step, dims[0] - n)),) for n in range(0, dims[0], step)]
    return [(n,) + rest for n in range(dims[0]) for rest in cuts(dims[1:], item)]


def start_copies(source, target, semaphore):
    for at in cuts(target.shape, target.dtype.itemsize):
        one, two = (source.at[at], target.at[at]) if at else (source, target)
        pltpu.make_async_copy(one, two, semaphore).start()
    return pltpu.make_async_copy(source, target, semaphore)


class Late:
    def __init__(self, source, target, semaphore):
        self.target, self.there = target, False
        self.copy = start_copies(source, target, semaphore)

    def get(self):
        if not self.there:
            self.copy.wait()
            self.there = True
        return self.target


class Here:
    def __init__(self, ref):
        self.ref = ref

    def get(self):
        return self.ref

    def send(self):
        pass


class Early:
    def __init__(self, target, source, semaphore):
        self.ref, self.sent = source, False
        self.ends = (source, target, semaphore)

    def send(self):
        if not self.sent:
            self.copy = start_copies(*self.ends)
            self.sent = True


class Pick:
    def __init__(self, table, pick, start=None, size=None):
        self.table, self.pick = table, pick
        self.start, self.size = start, table.shape[2] if size is None else size


def call(kernel, out_shape, args, scratch=(), smem=(), early=(), name=None):
    picks = {n: a for n, a in enumerate(args) if isinstance(a, Pick)}
    operands = [a.table if isinstance(a, Pick) else a for a in args]
    chosen = [next(iter(picks.values())).pick] if picks else []
    late = list(picks)
    buffers = [
        pltpu.VMEM((args[n].table.shape[1], args[n].size), args[n].table.dtype) for n in late
    ]
    buffers += [pltpu.VMEM(out_shape[n].shape, out_shape[n].dtype) for n in early]
    first_in = len(chosen)

    def body(*refs):
        pick, refs = refs[:first_in], refs[first_in:]
        ins, refs = list(refs[: len(args)]), refs[len(args) :]
        outs, refs = list(refs[: len(out_shape)]), refs[len(out_shape) :]
        own, refs = refs[: len(scratch)], refs[len(scratch) :]
        semaphores = refs[-1]
        for at, n in enumerate(late):
            entry = picks[n]
            columns = slice(None) if entry.start is None else pl.ds(entry.start(), entry.size)
            source = ins[n].at[pick[0][0], :, columns]
            ins[n] = Late(source, refs[at], semaphores.at[at])
        for n in range(len(args)):
            if n not in picks and n not in smem:
                ins[n] = Here(ins[n])
        for at, n in enumerate(early, len(late)):
            outs[n] = Early(outs[n], refs[at], semaphores.at[at])
        kernel(*ins, *outs, *own)
        for n in late:
            ins[n].get()
        for n in early:
            outs[n].send()
            outs[n].copy.wait()

    spaces = [pltpu.SMEM] * first_in + [
        pltpu.SMEM if n in smem else pl.ANY if n in picks else pltpu.VMEM
        for n in range(len(args))
    ]
    return pl.pallas_call(
        body,
        out_shape=list(out_shape),
        in_specs=[pl.BlockSpec(memory_space=space) for space in spaces],
        out_specs=[
            pl.BlockSpec(memory_space=pl.ANY if n in early else pltpu.VMEM)
            for n in range(len(out_shape))
        ],
        scratch_shapes=list(scratch)
        + buffers
        + [pltpu.SemaphoreType.DMA((max(len(late) + len(early), 1),))],
        compiler_params=pltpu.CompilerParams(vmem_limit_bytes=60 * MIB),
        cost_estimate=pl.CostEstimate(flops=1, bytes_accessed=1, transcendentals=0),
        name=name,
    )(*chosen, *operands)


def owner(n, direct):
    return jnp.bitwise_xor(lax.axis_index("tok"), n) if direct else n


def rows_of(n, size):
    if isinstance(n, int):
        return pl.ds(n * size, size)
    return pl.ds(pl.multiple_of(n * size, size), size)


def came_from(n):
    own, size = lax.axis_index("seq"), len(RING)
    place = jnp.where(lax.rem(own, 2) == 0, own // 2, size - 1 - own // 2)
    shift = (0, -1, 1, -2, 2, -3, 3, -4, 4)[n]
    came = lax.rem(place + shift + size, size)
    return jnp.where(came < size // 2, 2 * came, 2 * (size - 1 - came) + 1)


def to_slot(refs, index, value):
    for n, ref in enumerate(refs):

        @pl.when(index == n)
        def _(ref=ref):
            ref[...] = value


def normalized(rows):
    mean = jnp.mean(rows, axis=-1, keepdims=True)
    centered = rows - mean
    scale = lax.rsqrt(jnp.mean(centered * centered, axis=-1, keepdims=True) + EPS)
    return centered * scale, scale


def norm_back(rows, gain, grad):
    unit, scale = normalized(rows)
    weighted = grad * gain
    first = jnp.mean(weighted, axis=-1, keepdims=True)
    second = jnp.mean(weighted * unit, axis=-1, keepdims=True)
    return (weighted - first - unit * second) * scale


def swapped(rows):
    width = rows.shape[1]
    if width % 128:
        half = HEAD_DIM // 2
        parts = []
        for start in range(0, width, HEAD_DIM):
            parts += [rows[:, start + half : start + HEAD_DIM], rows[:, start : start + half]]
        return jnp.concatenate(parts, axis=1)
    lane = lax.broadcasted_iota(jnp.int32, rows.shape, 1)
    ahead = pltpu.roll(rows, width - HEAD_DIM // 2, 1)
    behind = pltpu.roll(rows, HEAD_DIM // 2, 1)
    return jnp.where(lane % HEAD_DIM < HEAD_DIM // 2, ahead, behind)


def widened(table, width):
    if width <= table.shape[1]:
        return table[:, :width]
    return jnp.concatenate([table] * (width // table.shape[1]), axis=1)


def head_part(rows, head):
    lane = lax.broadcasted_iota(jnp.int32, rows.shape, 1)
    return jnp.where(lane // HEAD_DIM == head, rows, jnp.zeros_like(rows))


def chunked(ref, base, value):
    count = -(-value.shape[1] // 128)
    for n in range(count):
        part = value[:, n * 128 : (n + 1) * 128].astype(ref.dtype)
        if part.shape[1] < 128:
            ref[base + n] = jnp.zeros(ref.shape[1:], ref.dtype)
            ref[base + n, :, : part.shape[1]] = part
        else:
            ref[base + n] = part
    return base + count


def halves(keep, at, send, first, value):
    core = lax.rem(lax.axis_index("tok"), 2)
    half = value.shape[1] // 256
    for n in range(2 * half):
        part = value[:, n * 128 : (n + 1) * 128].astype(keep.dtype)

        @pl.when(core == n // half)
        def _(part=part, n=n):
            keep[at + n % half] = part

        @pl.when(core != n // half)
        def _(part=part, n=n):
            send[first + n % half] = part


def labelled(ref, at, pick):
    ref[at] = jnp.full(ref.shape[1:], pick[0].astype(F32)).astype(ref.dtype)


def document_range(block, rows, seg_scalar, seg_row):
    first = seg_scalar[0, block * rows].astype(F32)
    last = seg_scalar[0, block * rows + rows - 1].astype(F32)
    below = jnp.sum(jnp.where(seg_row < first, 1.0, 0.0)).astype(jnp.int32)
    upto = jnp.sum(jnp.where(seg_row <= last, 1.0, 0.0)).astype(jnp.int32)
    return below // rows, (upto + rows - 1) // rows


def prepare_kernel(tokens, gain_one, gain_two, weight, token_out, double, single):
    weight, odd = weight.get(), lax.rem(lax.axis_index("seq"), 2)
    unit = single.shape[1]

    @pl.when(odd == 0)
    def _():
        double[...] = weight[:, : 2 * unit]
        single[...] = weight[:, 2 * unit :]

    @pl.when(odd == 1)
    def _():
        double[...] = weight[:, unit:]
        single[...] = weight[:, :unit]

    tokens = tokens.get()
    rows, part = tokens.shape[0], gain_one.get().shape[0]
    token_out[:rows] = tokens[...]
    token_out[rows:] = jnp.zeros((16, tokens.shape[1]), BF16)
    both = [gain.get()[...].astype(F32).reshape(1, part) for gain in (gain_one, gain_two)]
    token_out[rows : rows + 2, :part] = jnp.concatenate(both, axis=0).astype(BF16)


def adapters_kernel(tok, *refs):
    tables, outs = refs[:8], refs[8:]
    down_one, up_one, down_attn, up_attn, down_two, up_two, down_last, up_last = outs
    for n in (1, 5, 6):
        tables[n].get()
    for table, out in ((0, down_one), (2, down_attn), (3, up_attn), (4, down_two), (7, up_last)):
        out[...] = tables[table].get()[...]
    own = lax.axis_index("tok")
    for n in range(tok):

        @pl.when(own == n)
        def _(n=n):
            down_last[...] = tables[6].get()[:, columns_of(n, 0, down_last.shape[1], tok)]
            for kind in range(3):
                size = up_one.shape[2]
                up_one[kind] = tables[1].get()[:, columns_of(n, kind, size, tok)]
            for kind in range(2):
                size = up_two.shape[2]
                up_two[kind] = tables[5].get()[:, columns_of(n, kind, size, tok)]


def columns_of(own, group, size, tok):
    start = (group * tok + own) * size
    return slice(start, start + size)


def qkv_kernel(pieces, kinds, tokens, down, ups, cosine, sine, *refs):
    weights, refs = refs[:pieces], refs[pieces:]
    norm, gain, query, key, value, whole = refs[:6]
    width = query.shape[1]
    if pieces == 1:
        whole[...] = weights[0].get()[...]
    else:
        out_weight = refs[6]
        unit = width // 2
        own = lax.axis_index("tok")
        first = 0
        for n in range(pieces):
            piece = weights[n].get()
            depth = piece.shape[0]
            spot = came_from(n)
            half, part = spot // 4, lax.rem(spot, 4)
            down_at = pl.ds(pl.multiple_of(part * width + first, depth), depth)
            double, single = kinds[3 * own + half], kinds[3 * own + 2]
            whole[double, down_at, :] = piece[:, :width]
            across = pl.ds(pl.multiple_of(half * unit, unit), unit)
            whole[single, down_at, across] = piece[:, width : width + unit]
            across = pl.ds(pl.multiple_of(spot * unit, unit), unit)
            out_weight[first : first + depth, across] = piece[:, width + unit :]
            first = (first + depth) % width
    for kind in range(3):
        product = tn(down.get()[...], ups.get()[kind])
        whole[kind] = (whole[kind].astype(F32) + product).astype(BF16)
    tokens, cosine, sine = tokens.get(), cosine.get(), sine.get()
    count, block = tokens.shape[0], tokens.shape[1] - 16
    for n in range(count):
        part = gain.shape[1] // count
        gain[:, n * part : (n + 1) * part] = tokens[n, block:, :part].astype(F32)[:2]

    def step(n, _):
        at = rows_of(n, block)
        unit, _ = normalized(tokens[n, :block].astype(F32))
        rows = (unit * gain[0:1, :]).astype(BF16)
        norm[at, :] = rows
        cos, sin = widened(cosine[at, :], width), widened(sine[at, :], width)
        for kind, out in enumerate((query, key, value)):
            part = nn(rows, whole[kind])
            if kind < 2:
                part = part * cos + swapped(part) * sin
            if kind == 0:
                part = part.astype(BF16).astype(F32) * 0.125
            out[at, :] = part.astype(BF16)
        return 0

    lax.fori_loop(0, count, step, 0)


def attend_kernel(count, direct, seg_scalar, query, key, value, segments, *refs):
    outs, (log_total, mixed_t, value_t, seg_t) = refs[:count], refs[count:]
    segments = segments.get()
    seg_row = segments[...].astype(F32)
    seg_t[...] = jnp.broadcast_to(seg_row, (128, seg_row.shape[1])).T
    query, key, value = query.get(), key.get(), value.get()
    block = outs[0].shape[0]
    width = query.shape[1]
    heads = width // HEAD_DIM
    value_t[...] = value[...].T
    parts = [slice(head * HEAD_DIM, (head + 1) * HEAD_DIM) for head in range(heads)]

    def step(n, _):
        place = owner(n, direct)
        at = rows_of(place, block)
        rows = query[at, :]
        own = [head_part(rows, head) for head in range(heads)]
        seg_here = segments[:, at].astype(F32)

        def against(m, carry):
            tops, sums, mixed = carry
            keys = rows_of(m, block)
            column = widened(seg_t[keys, :], block)
            bias = jnp.where(column == seg_here, 0.0, -1e30)
            near = key[keys, :]
            scores = [nt(near, part) + bias for part in own]
            now = [
                jnp.maximum(top, jnp.max(part, axis=0, keepdims=True))
                for top, part in zip(tops, scores)
            ]
            raised = [jnp.exp(part - top) for part, top in zip(scores, now)]
            scale = [jnp.exp(before - top) for before, top in zip(tops, now)]
            added = [nn(value_t[part, keys], up.astype(BF16)) for part, up in zip(parts, raised)]
            sums = [
                total * by + jnp.sum(up, axis=0, keepdims=True)
                for total, by, up in zip(sums, scale, raised)
            ]
            mixed = [old * by + new for old, by, new in zip(mixed, scale, added)]
            return now, sums, mixed

        start = (
            [jnp.full((1, block), -2e30, F32)] * heads,
            [jnp.zeros((1, block), F32)] * heads,
            [jnp.zeros((HEAD_DIM, block), F32)] * heads,
        )
        first, last = document_range(place, block, seg_scalar, seg_row)
        tops, sums, mixed = lax.fori_loop(first, last, against, start)
        for head in range(heads):
            log_total[head : head + 1, at] = tops[head] + jnp.log(sums[head])
            mixed_t[n, parts[head], :] = mixed[head] * (1.0 / sums[head])
        to_slot(outs, n, mixed_t[n].T.astype(BF16))
        return 0

    lax.fori_loop(0, count, step, 0)


def features(n, width, direct):
    if not direct:
        return slice(n * width, (n + 1) * width)
    return pl.ds(pl.multiple_of(owner(n, direct) * width, width), width)


def out_kernel(count, direct, inputs, gain, down, up, *refs):
    attn, weights = refs[:count], refs[count : 2 * count]
    middle, norm, narrow = refs[2 * count :]
    down = down.get()
    total = inputs.get()[...].astype(F32)
    thin = jnp.zeros(narrow.shape, F32)
    for n in range(count):
        rows = attn[n].get()[...]
        total = total + nn(rows, weights[n].get()[...])
        thin = thin + nt(rows, down[:, features(n, rows.shape[1], direct)])
    thin = thin.astype(BF16)
    total = total + nn(thin, up.get()[...])
    middle[...] = total
    narrow[...] = thin
    norm[...] = (normalized(total)[0] * gain.get()[1:2, :]).astype(BF16)


def mlp_pre_kernel(packed, direct, down_in, up_in, down_out, up_out, grads, *refs):
    pieces = 9 if packed else 2
    weights, refs = refs[:pieces], refs[pieces:]
    w_in, w_out, grad_early, grad_late = refs
    hidden, width = w_out.shape
    if packed:
        depth, thin = width // 4, width // 8
        first = 0
        for n in range(pieces):
            piece = weights[n].get()
            rows = slice(first, first + piece.shape[0])
            spot = came_from(n)
            across = pl.ds(pl.multiple_of(lax.rem(spot, 4) * depth, depth), depth)
            w_in[spot // 4, rows, across] = piece[:, :depth]
            across = pl.ds(pl.multiple_of(spot * thin, thin), thin)
            w_out[rows, across] = piece[:, depth:]
            first = rows.stop % hidden
    else:
        w_in[...] = weights[0].get()[...]
        w_out[...] = weights[1].get()[...]
    for n in range(2):
        w_in[n] = (w_in[n].astype(F32) + tn(up_in.get()[n], down_in.get()[...])).astype(BF16)
    w_out[...] = (w_out[...].astype(F32) + tn(down_out.get()[...], up_out.get()[...])).astype(BF16)
    grads = grads.get()
    for n in range(grads.shape[0]):
        target = grad_early if n < 2 else grad_late
        target[n if n < 2 else n - 2] = nt(grads[owner(n, direct)], w_out[...])


def mlp_kernel(count, first, w_in, grad_act, *refs):
    norms, backs, (act_out, grad_out) = refs[:count], refs[count : 2 * count], refs[2 * count :]
    w_in, grad_act = w_in.get(), grad_act.get()
    for n in range(count):
        norm = norms[n].get()[...]
        inputs, gate = nt(norm, w_in[0]), nt(norm, w_in[1])
        phi = 0.5 + 0.5 * lax.erf(inputs * (0.5**0.5))
        gelu = inputs * phi
        act_out[n] = (gelu * gate).astype(BF16)
        back_act = grad_act[first + n]
        slope = phi + inputs * (jnp.exp(-0.5 * inputs * inputs) * 0.3989422804014327)
        grad_inputs = (back_act * gate * slope).astype(BF16)
        grad_gate = (back_act * gelu).astype(BF16)
        grad_out[0, n] = grad_inputs
        grad_out[1, n] = grad_gate
        backs[n][...] = (nn(grad_inputs, w_in[0]) + nn(grad_gate, w_in[1])).astype(BF16)


def mlp_terms_kernel(count, first, direct, pick, down_in, up_in, down_out, up_out, *refs):
    acts, grads, out_grad, refs = refs[:2], refs[2:4], refs[4], refs[5:]
    norms, terms = refs[:count], refs[count]
    down_in_grad = down_out_grad = up_out_grad = 0.0
    up_in_grad = [0.0, 0.0]
    down_in, up_in, down_out, up_out = down_in.get(), up_in.get(), down_out.get(), up_out.get()
    for n in range(count):
        norm = norms[n].get()[...]
        narrow = nt(norm, down_in[...]).astype(BF16)
        back = [grads[n // 2].get()[h, n % 2] for h in range(2)]
        inner_in = (nt(back[0], up_in[0]) + nt(back[1], up_in[1])).astype(BF16)
        down_in_grad = down_in_grad + tn(inner_in, norm)
        for h in range(2):
            up_in_grad[h] = up_in_grad[h] + tn(narrow, back[h])
        act = acts[n // 2].get()[n % 2]
        grad = out_grad.get()[owner(first + n, direct)]
        narrow_two = nt(act, down_out[...]).astype(BF16)
        inner = nt(grad, up_out[...]).astype(BF16)
        down_out_grad = down_out_grad + tn(inner, act)
        up_out_grad = up_out_grad + tn(narrow_two, grad)
    at = chunked(terms, 0, up_in_grad[0])
    at = chunked(terms, at, up_in_grad[1])
    at = chunked(terms, at, down_out_grad)
    labelled(terms, at, pick)
    at = chunked(terms, at + 1, down_in_grad)
    chunked(terms, at, up_out_grad)


def mlp_out_kernel(count, w_out, *refs):
    acts, outs = refs[: count // 2], refs[count // 2 :]
    w_out = w_out.get()
    for n in range(count):
        outs[n].ref[...] = nn(acts[n // 2].get()[n % 2], w_out[...]).astype(BF16)
        outs[n].send()


def out_back_kernel(count, parts, direct, middle, out_grad, gain, down, up, narrow, *refs):
    back, refs = refs[:parts], refs[parts:]
    attn, weights = refs[:count], refs[count : 2 * count]
    grad_mid, refs = refs[2 * count], refs[2 * count + 1 :]
    slots, (keep, send, down_grad) = refs[:count], refs[count:]
    total = sum(ref.get()[...].astype(F32) for ref in back)
    grad = out_grad.get()[...].astype(F32)
    grad = grad + norm_back(middle.get()[...], gain.get()[1:2, :], total)
    grad_mid[...] = grad
    low = grad.astype(BF16)
    down = down.get()
    inner = nt(low, up.get()[...]).astype(BF16)
    for n in range(count):
        rows = attn[n].get()[...]
        own = features(n, rows.shape[1], direct)
        slots[n][...] = (nt(low, weights[n].get()[...]) + nn(inner, down[:, own])).astype(BF16)
        down_grad[:, own] = tn(inner, rows)
    half = grad.shape[1] // 256
    halves(keep, half, send, half, tn(narrow.get()[...], low))
    halves(keep, 0, send, 0, down_grad[...])


def attend_back_kernel(
    count, direct, seg_scalar, pick, query, key, value, segments, log_total, mixed_t, cosine, sine,
    down, ups, norm, *refs
):
    grads, (grad_qkv, keep, send) = refs[:count], refs[count : count + 3]
    key_t, seg_t, grad_q, grad_k, grad_v, query_t, grad_all = refs[count + 3 :]
    segments = segments.get()
    seg_row = segments[...].astype(F32)
    seg_t[...] = jnp.broadcast_to(seg_row, (128, seg_row.shape[1])).T
    for ref in (grad_k, grad_v):
        ref[...] = jnp.zeros_like(ref)
    query, key, value = query.get(), key.get(), value.get()
    log_total, mixed_t = log_total.get(), mixed_t.get()
    block = grads[0].get().shape[0]
    width = query.shape[1]
    heads = width // HEAD_DIM
    key_t[...] = key[...].T
    for n in range(count):
        grad_all[n] = grads[n].get()[...]
    parts = [slice(head * HEAD_DIM, (head + 1) * HEAD_DIM) for head in range(heads)]

    def step(n, _):
        place = owner(n, direct)
        at = rows_of(place, block)
        rows, grad = query[at, :], grad_all[n]
        own = [head_part(rows, head) for head in range(heads)]
        own_grad = [head_part(grad, head) for head in range(heads)]
        product = grad.astype(F32).T * mixed_t[n]
        dots = [jnp.sum(product[part], axis=0, keepdims=True) for part in parts]
        query_t[...] = jnp.zeros_like(query_t)
        seg_here = segments[:, at].astype(F32)

        def against(m, _):
            keys = rows_of(m, block)
            column = widened(seg_t[keys, :], block)
            bias = jnp.where(column == seg_here, 0.0, -1e30)
            near, near_value = key[keys, :], value[keys, :]
            probs = [
                jnp.exp(nt(near, own[head]) + bias - log_total[head : head + 1, at])
                for head in range(heads)
            ]
            grad_probs = [nt(near_value, part) for part in own_grad]
            grad_s = [
                (prob * (grad_prob - dot)).astype(BF16)
                for prob, grad_prob, dot in zip(probs, grad_probs, dots)
            ]
            sum_v = sum(nn(prob.astype(BF16), part) for prob, part in zip(probs, own_grad))
            sum_k = sum(nn(part, mine) for part, mine in zip(grad_s, own))
            for head in range(heads):
                query_t[parts[head], :] += nn(key_t[parts[head], keys], grad_s[head])
            grad_k[keys, :] += sum_k
            grad_v[keys, :] += sum_v
            return 0

        first, last = document_range(place, block, seg_scalar, seg_row)
        lax.fori_loop(first, last, against, 0)
        grad_q[at, :] = query_t[...].T * 0.125
        return 0

    lax.fori_loop(0, count, step, 0)
    cosine, sine = cosine.get(), sine.get()

    def finish(n, _):
        at = rows_of(n, block)
        cos, sin = widened(cosine[at, :], width), widened(sine[at, :], width)
        for kind, ref in enumerate((grad_q, grad_k)):
            part = ref[at, :]
            grad_qkv[kind, at, :] = (part * cos - swapped(part) * sin).astype(BF16)
        grad_qkv[2, at, :] = grad_v[at, :].astype(BF16)
        return 0

    lax.fori_loop(0, count, finish, 0)
    norm = norm.get()
    inner = sum(nt(grad_qkv[kind], ups.get()[kind]) for kind in range(3))
    narrow = nt(norm[...], down.get()[...]).astype(BF16)
    at = 0
    for kind in range(3):
        at = chunked(keep, at, tn(narrow, grad_qkv[kind]))
    labelled(keep, at, pick)
    halves(keep, at + 1, send, 0, tn(inner.astype(BF16), norm[...]))


def qkv_back_kernel(count, direct, grad_qkv, weights, *outs):
    block = outs[0].ref.shape[0]
    grad_qkv, weights = grad_qkv.get(), weights.get()
    for n in list(range(1, count, 2)) + list(range(0, count, 2)):
        at = rows_of(owner(n, direct), block)
        total = sum(nt(grad_qkv[kind, at, :], weights[kind]) for kind in range(3))
        outs[n].ref[...] = total.astype(BF16)
        outs[n].send()


def layer_kernel(middle, *refs):
    total = middle.get()[...] + sum(ref.get()[...].astype(F32) for ref in refs[:-1])
    refs[-1][...] = total.astype(BF16)


def last_kernel(inputs, grad_mid, gain, *refs):
    total = sum(ref.get()[...].astype(F32) for ref in refs[:-1])
    back = norm_back(inputs.get()[...].astype(F32), gain.get()[0:1, :], total)
    refs[-1][...] = (grad_mid.get()[...] + back).astype(BF16)


def pair_kernel(local, own, came, out):
    own, came = own.get(), came.get()
    across = lax.axis_index("tok") // 2
    out[pl.ds(across * local, local)] = own[:local]
    out[pl.ds((1 - across) * local, local)] = came[:local]
    out[2 * local :] = (own[local:].astype(F32) + came[local:].astype(F32)).astype(BF16)


def late_kernel(local, keep, came, out_keep, out_came, out):
    keep, out_keep = keep.get(), out_keep.get()
    out[:local] = keep[:local]
    half = keep.shape[0] - local
    total = keep[local:].astype(F32) + came.get()[...].astype(F32)
    out[local : local + half] = total.astype(BF16)
    total = out_keep[...].astype(F32) + out_came.get()[...].astype(F32)
    out[local + half :] = total.astype(BF16)


def stack_kernel(*refs):
    out = refs[-1]
    first = 0
    for n, ref in enumerate(refs[:-1]):
        block = ref.get()
        size = block.shape[0]
        out[came_from(n), first : first + size] = block[...]
        first = (first + size) % out.shape[1]


def spread_kernel(widths, local, count, *refs):
    mine, other, refs = refs[:count], refs[count : 2 * count], refs[2 * count :]
    outs, both = refs[: len(widths)], refs[len(widths)]
    core = lax.rem(lax.axis_index("tok"), 2)
    own = lax.axis_index("seq") // 2
    for n in range(count):
        size = mine[n].get().shape[0]
        at = pl.ds(jnp.bitwise_xor(own, n) * size, size) if count > 1 else slice(None)
        both[core, at] = mine[n].get()[...]
        both[1 - core, at] = other[n].get()[...]
    for out in outs:
        out[...] = jnp.zeros_like(out)

    def step(n, _):
        pick = jnp.max(both[0, n, local - 1].astype(F32)).astype(jnp.int32)
        at, rest = 0, 2 * local
        for out, width in zip(outs, widths):
            if width <= 0:
                chunks = out.shape[2] // 128
                for m in range(chunks):
                    if width == 0:
                        term = both[0, n, rest + m].astype(F32) + both[1, n, rest + m].astype(F32)
                    else:
                        term = both[2 * m // chunks, n, rest + m % (chunks // 2)].astype(F32)
                    out[pick, :, m * 128 : (m + 1) * 128] += term
                rest += chunks if width == 0 else chunks // 2
                continue
            blocks = -(-width // 128)
            for group in range(out.shape[2] // (4 * width)):
                for tok in range(4):
                    first = (group * 4 + tok) * width
                    base = (tok // 2) * local + at
                    parts = [both[tok % 2, n, base + m] for m in range(blocks)]
                    term = jnp.concatenate(parts, axis=1)[:, :width].astype(F32)
                    out[pick, :, first : first + width] += term
                at += blocks
        return 0

    lax.fori_loop(0, both.shape[1], step, 0)


class Exchange:
    def __init__(self, size):
        self.size = size
        self.direct = size == 4

    def swap(self, block, bits):
        pairs = [(n, n ^ bits) for n in range(self.size)]
        return lax.ppermute(block, "tok", pairs)

    def hop(self, block):
        if not self.direct:
            whole = lax.all_gather(block, "tok", axis=0)
            return [whole[n] for n in range(self.size)]
        return [block, self.swap(block, 1), self.swap(block, 2)]

    def land(self, parts):
        if not self.direct:
            return parts
        return parts + [self.swap(parts[2], 1)]

    def turn(self, slots):
        if not self.direct:
            whole = lax.all_to_all(jnp.stack(slots), "tok", 0, 0)
            return [whole[n] for n in range(self.size)]
        return [slots[0]] + [self.swap(slots[n], n) for n in range(1, self.size)]

    def halve(self, slots):
        near, far = self.swap(slots[1], 1), self.swap(slots[3], 1)
        both = (slots[2].astype(F32) + far.astype(F32)).astype(far.dtype)
        return near, both

    def reduce(self, slots):
        if not self.direct:
            return [lax.psum_scatter(jnp.stack(slots), "tok", scatter_dimension=0)]
        near, both = self.halve(slots)
        return [slots[0], near, self.swap(both, 2)]


def meet(*arrays):
    return lax.optimization_barrier(arrays)


class Ring:
    def __init__(self, block):
        self.blocks = [block]
        self.right = self.left = block
        self.half = block.shape[0] // 32 * 16 if block.ndim == 2 else block.shape[0] // 2
        self.ahead = [(RING[n], RING[(n + 1) % len(RING)]) for n in range(len(RING))]
        self.behind = [(b, a) for a, b in self.ahead]

    def step(self):
        step = len(self.blocks) // 2 + 1
        if step == len(RING) // 2:
            self.right, self.left = self.right[: self.half], self.left[self.half :]
        self.right = lax.ppermute(self.right, "seq", self.ahead)
        self.left = lax.ppermute(self.left, "seq", self.behind)
        self.blocks += [self.right, self.left]

    def meet(self, *arrays):
        self.right, self.left, *arrays = meet(self.right, self.left, *arrays)
        if len(self.blocks) > 1:
            self.blocks[-2:] = [self.right, self.left]
        return arrays


def owner_of_columns(seq, tok):
    double, single, seen = [], [], [0] * tok
    kinds = [[0, 0, 0] for _ in range(tok)]
    for s in range(seq):
        first = 3 * s + s % 2
        own = first % seq // 2
        double.append((own, seen[own]))
        kinds[own][seen[own]] = first // seq
        seen[own] += 1
        last = 3 * s + 2 * (1 - s % 2)
        single.append((last % seq // 2, last % 2))
        kinds[last % seq // 2][2] = last // seq
    return double, single, kinds


def body(
    tokens,
    out_grad,
    segments,
    adapter_index,
    qkv_weight,
    out_weight,
    in_weight,
    out2_weight,
    attn_gain,
    mlp_gain,
    qkv_down,
    qkv_up,
    out_down,
    out_up,
    in_down,
    in_up,
    out2_down,
    out2_up,
):
    seq, tok = lax.axis_size("seq"), lax.axis_size("tok")
    own_tok = lax.axis_index("tok")
    move = Exchange(tok)
    direct = move.direct
    fast = direct and seq == 8
    adapters, rank, width = qkv_down.shape
    length = segments.shape[1]
    rows = tokens.shape[1]
    heads = HEADS // tok
    lanes = heads * HEAD_DIM
    hidden = out2_weight.shape[0]
    hidden_all = hidden * tok
    inputs, out_grad = tokens[0], out_grad[0]
    pick = adapter_index[0]
    pieces = lambda columns: -(-columns // 128)
    early_local, late_local = 3 * pieces(hidden) + 1, 3 * pieces(lanes) + 1
    wide = pieces(width)

    sizes = ((width, 0), (lanes, 3), (width, 0), (width, 0), (width, 0), (hidden, 2), (hidden, 1), (width, 0))
    tables = (qkv_down, qkv_up, out_down, out_up, in_down, in_up, out2_down, out2_up)
    if fast:
        adapters_own = call(
            functools.partial(adapters_kernel, tok),
            [
                shape((groups,) * (groups > 1) + (rank, columns), BF16)
                for columns, groups in sizes
            ],
            [Pick(table, adapter_index) for table in tables],
            name="adapters",
        )
    else:

        def chosen(table, columns, groups):
            parts = []
            for group in range(max(groups, 1)):
                start = (group * tok + own_tok) * columns if groups else 0
                parts.append(lax.dynamic_slice(table, (pick, 0, start), (1, rank, columns))[0])
            return jnp.stack(parts) if groups > 1 else parts[0]

        adapters_own = [chosen(table, *size) for table, size in zip(tables, sizes)]

    exponent = jnp.arange(0, HEAD_DIM, 2).astype(F32) / HEAD_DIM
    inverse = 1.0 / THETA**exponent
    phases = jnp.arange(length).astype(F32)[:, None] * jnp.tile(inverse, 4)[None, :]
    sign = jnp.where(jnp.arange(2 * HEAD_DIM) % HEAD_DIM < HEAD_DIM // 2, -1.0, 1.0)
    cosine, sine = jnp.cos(phases), jnp.sin(phases) * sign[None, :]

    if fast:
        unit = width // seq
        double, single, kinds = owner_of_columns(seq, tok)
        kinds = jnp.array(sum(kinds, []), jnp.int32)
        token_block, *parts = call(
            prepare_kernel,
            [
                shape((rows + 16, width), BF16),
                shape((qkv_weight.shape[0], 2 * unit), BF16),
                shape((qkv_weight.shape[0], unit), BF16),
            ],
            [inputs, attn_gain, mlp_gain, qkv_weight],
            name="prepare",
        )
        in_weight, *parts = meet(in_weight, *parts)
        for n, owners in enumerate((double, single)):
            pairs = [
                (s * tok + t, (owners[s][1] * tok + t) * tok + owners[s][0])
                for s in range(seq)
                for t in range(tok)
            ]
            parts[n] = lax.ppermute(parts[n], ("seq", "tok"), pairs)
        pairs = [
            (s * tok + t, ((s // tok) * tok + t) * tok + s % tok)
            for s in range(seq)
            for t in range(tok)
        ]
        in_piece = lax.ppermute(in_weight.T, ("seq", "tok"), pairs)
        together = meet(token_block, cosine, sine, *adapters_own, in_piece, *parts)
        token_block, cosine, sine, adapters_own = *together[:3], together[3:11]
        in_piece, *parts = together[11:]
        ring = Ring(jnp.concatenate(parts + [out_weight], axis=1))
        ring.step()
        ring.step()
        (out_grad_in,) = ring.meet(out_grad)
        ring.step()
        ring.step()
        mlp_piece = jnp.concatenate([in_piece, out2_weight], axis=1)
        (mlp_piece,) = ring.meet(mlp_piece)
        qkv_pieces = ring.blocks
        mlp_ring = Ring(mlp_piece)
        mlp_ring.step()
    else:

        def columns(weight, count):
            block = lax.all_gather(weight, "seq", axis=1, tiled=True)
            split = block.reshape(block.shape[0], count, tok, -1).transpose(2, 1, 0, 3)
            turned = lax.all_to_all(split, "tok", 0, 0)
            return turned.transpose(1, 0, 2, 3).reshape(count, width, -1)

        gain_rows = jnp.stack([attn_gain, mlp_gain])
        gain_rows = jnp.pad(gain_rows, ((0, 14), (0, width - width // tok)))
        token_block = jnp.concatenate([inputs, gain_rows], axis=0)
        out_grad_in = out_grad
        qkv_pieces = [columns(qkv_weight, 3)]
        kinds = jnp.zeros((1,), jnp.int32)
        own_out = lax.all_gather(out_weight, "seq", axis=1, tiled=True)
        mlp_weights = [
            columns(in_weight, 2).transpose(0, 2, 1),
            lax.all_gather(out2_weight, "seq", axis=1, tiled=True),
        ]
    token_all = lax.all_gather(token_block, "tok", axis=0)
    grad_all = lax.all_gather(out_grad_in, "tok", axis=0)

    down_one, up_one, down_attn, up_attn, down_two, up_two, down_last, up_last = adapters_own

    norm_one, gain, query, key, value, w_qkv, *own_row = call(
        functools.partial(qkv_kernel, len(qkv_pieces)),
        [shape((length, width), BF16), shape((2, width), F32)]
        + [shape((length, lanes), BF16)] * 3
        + [shape((3, width, lanes), BF16)]
        + [shape((lanes, width), BF16)] * fast,
        [kinds, token_all, down_one, up_one, cosine, sine] + qkv_pieces,
        smem=(0,),
        name="qkv",
    )
    if fast:
        query, key, value = mlp_ring.meet(query, key, value)
        mlp_ring.step()
    out_parts = move.hop(own_row[0] if fast else own_out)
    *attn_slots, log_total, mixed_t = call(
        functools.partial(attend_kernel, tok, direct),
        [shape((rows, lanes), BF16)] * tok
        + [shape((heads, length), F32), shape((tok, lanes, rows), F32)],
        [segments, query, key, value, segments],
        smem=(0,),
        scratch=[pltpu.VMEM((lanes, length), BF16), pltpu.VMEM((length, 128), F32)],
        name="attend",
    )
    attn_slots, out_parts = meet(attn_slots, out_parts)
    if fast:
        attn_slots = mlp_ring.meet(*attn_slots)
        mlp_ring.step()
    attn = move.turn(attn_slots)
    out_weights = move.land(out_parts)
    middle, norm_two, narrow_attn = call(
        functools.partial(out_kernel, tok, direct),
        [shape((rows, width), F32), shape((rows, width), BF16), shape((rows, rank), BF16)],
        [inputs, gain, down_attn, up_attn] + attn + out_weights,
        name="out",
    )
    if fast:
        (norm_two,) = mlp_ring.meet(norm_two)
        mlp_ring.step()
        mlp_weights = mlp_ring.blocks
    norm_slots = move.hop(norm_two)
    w_in, w_out, *grad_acts = call(
        functools.partial(mlp_pre_kernel, fast, direct),
        [
            shape((2, hidden, width), BF16),
            shape((hidden, width), BF16),
            shape((2, rows, hidden), F32),
            shape((tok - 2, rows, hidden), F32),
        ],
        [down_two, up_two, down_last, up_last, grad_all] + mlp_weights,
        name="mlp_pre",
    )
    back_slots, acts, grads_z = [], [], []
    for first in range(0, tok, 2):
        *backs, act, grad_z = call(
            functools.partial(mlp_kernel, 2, max(first - 2, 0)),
            [shape((rows, width), BF16)] * 2
            + [shape((2, rows, hidden), BF16), shape((2, 2, rows, hidden), BF16)],
            [w_in, grad_acts[min(first, 1)]] + norm_slots[first : first + 2],
            name="mlp",
        )
        if first == 0:
            *backs, norm_slots[2] = meet(*backs, norm_slots[2])
            norm_slots = move.land(norm_slots)
        back_slots += backs
        acts.append(act)
        grads_z.append(grad_z)
    back_two = move.reduce(back_slots)
    out_slots, early = [], []
    for first in range(0, tok, 4):
        pair = slice(first // 2, first // 2 + 2)
        terms = call(
            functools.partial(mlp_terms_kernel, 4, first, direct),
            [shape((early_local + 2 * wide, rank, 128), BF16 if fast else F32)],
            [adapter_index, down_two, up_two, down_last, up_last]
            + acts[pair]
            + grads_z[pair]
            + [grad_all]
            + norm_slots[first : first + 4],
            smem=(0,),
            name="mlp_terms",
        )[0]
        early.append(terms)
    early = sum(early[1:], early[0])
    if fast:
        early = call(
            functools.partial(pair_kernel, early_local),
            [shape((early_local + early.shape[0], rank, 128), BF16)],
            [early, move.swap(early, 2)],
            name="pair",
        )[0]
    grad_mid, *rest = call(
        functools.partial(out_back_kernel, tok, len(back_two), direct),
        [shape((rows, width), F32)]
        + [shape((rows, lanes), BF16)] * tok
        + [shape((wide, rank, 128), BF16)] * 2,
        [middle, out_grad, gain, down_attn, up_attn, narrow_attn] + back_two + attn + out_weights,
        scratch=[pltpu.VMEM((rank, width), F32)],
        name="out_back",
    )
    rest[0], *acts = meet(rest[0], *acts)
    for first in range(0, tok, 4):
        out_slots += call(
            functools.partial(mlp_out_kernel, 4),
            [shape((rows, width), BF16)] * 4,
            [w_out] + acts[first // 2 : first // 2 + 2],
            early=(0, 1, 2, 3),
            name="mlp_out",
        )
    out_keep, out_send = rest[tok:]
    attn_grads = move.turn(rest[:tok])
    if fast:
        attn_grads, out_slots, early = meet(attn_grads, out_slots, early)
        early = lax.all_gather(early, "seq", axis=0)
    out_parts = move.turn(out_slots) if fast else move.reduce(out_slots)
    grad_qkv, keep, send = call(
        functools.partial(attend_back_kernel, tok, direct),
        [
            shape((3, length, lanes), BF16),
            shape((late_local + wide // 2, rank, 128), BF16),
            shape((wide // 2, rank, 128), BF16),
        ],
        [segments, adapter_index, query, key, value, segments, log_total, mixed_t, cosine, sine]
        + [down_one, up_one, norm_one]
        + attn_grads,
        smem=(0, 1),
        scratch=[
            pltpu.VMEM((lanes, length), BF16),
            pltpu.VMEM((length, 128), F32),
            pltpu.VMEM((length, lanes), F32),
            pltpu.VMEM((length, lanes), F32),
            pltpu.VMEM((length, lanes), F32),
            pltpu.VMEM((lanes, rows), F32),
            pltpu.VMEM((tok, rows, lanes), BF16),
        ],
        name="attend_back",
    )

    def slots_of_one(grad_qkv):
        return call(
            functools.partial(qkv_back_kernel, tok, direct),
            [shape((rows, width), BF16)] * tok,
            [grad_qkv, w_qkv],
            early=tuple(range(tok)),
            name="qkv_back",
        )

    def layer_of(out_parts):
        output = [shape((rows, width), BF16)]
        return call(layer_kernel, output, [middle] + out_parts, name="layer")[0]

    def last_of(back_one):
        return call(
            last_kernel,
            [shape((rows, width), BF16)],
            [inputs, grad_mid, gain] + back_one,
            name="last",
        )[0]

    grads = lambda columns: shape((adapters, rank, columns), F32)
    if fast:

        def spread(parts, local, widths, columns):
            return call(
                functools.partial(spread_kernel, widths, local, len(parts)),
                [grads(size) for size in columns],
                parts + [move.swap(part, 1) for part in parts],
                scratch=[pltpu.VMEM((2, seq) + parts[0].shape[1:], BF16)],
                name="spread",
            )

        keep, *out_parts = meet(keep, *out_parts)
        layer_out = layer_of(out_parts)
        late = call(
            functools.partial(late_kernel, late_local),
            [shape((late_local + 3 * wide // 2, rank, 128), BF16)],
            [keep, move.swap(send, 1), out_keep, move.swap(out_send, 1)],
            name="late",
        )[0]
        late_came = move.swap(late, 2)
        late, grad_qkv = meet(late, grad_qkv)
        one_slots = slots_of_one(grad_qkv)
        near, both = move.halve(one_slots)
        both, late_came = meet(both, late_came)
        back_one = [one_slots[0], near, move.swap(both, 2)]
        late = call(
            functools.partial(pair_kernel, late_local),
            [shape((late_local + late.shape[0], rank, 128), BF16)],
            [late, late_came],
            name="pair_late",
        )[0]
        ring = Ring(late)
        ring.step()
        layer_out, back_one[2] = ring.meet(layer_out, back_one[2])
        ring.step()
        input_grad, early = ring.meet(last_of(back_one), early)
        ring.step()
        ring.step()
        in_up_grad, out2_down_grad, in_down_grad, out2_up_grad = spread(
            [early], early_local, (hidden, hidden, 0, 0), (2 * hidden_all, hidden_all, width, width)
        )
        (in_up_grad,) = ring.meet(in_up_grad)
        stacked = shape((seq,) + late.shape, BF16)
        blocks = list(call(stack_kernel, [stacked], ring.blocks, name="stack"))
        qkv_up_grad, qkv_down_grad, out_down_grad, out_up_grad = spread(
            blocks, late_local, (lanes, -1, -1, -1), (3 * width, width, width, width)
        )
    else:
        layer_out = layer_of(out_parts)
        input_grad = last_of(move.reduce(slots_of_one(grad_qkv)))
        picked = (pick == jnp.arange(adapters)).astype(F32)[:, None, None]

        def term(blocks, columns):
            return blocks.astype(F32).transpose(1, 0, 2).reshape(rank, -1)[:, :columns]

        def placed(terms, first, groups, columns):
            total = jnp.zeros((rank, groups * tok * columns), F32)
            for group in range(groups):
                at = first + group * pieces(columns)
                part = term(terms[at : at + pieces(columns)], columns)
                start = (group * tok + own_tok) * columns
                total = lax.dynamic_update_slice(total, part, (0, start))
            return total

        whole = lambda terms, at: term(terms[at : at + wide], width)

        def joined(kept, at, sent, first):
            half = wide // 2
            mine, other = kept[at : at + half], sent[first : first + half]
            swap = own_tok % 2 == 1
            low, high = jnp.where(swap, other, mine), jnp.where(swap, mine, other)
            return term(jnp.concatenate([low, high]), width)

        sums = (
            joined(keep, late_local, send, 0),
            placed(keep, 0, 3, lanes),
            joined(out_keep, 0, out_send, 0),
            joined(out_keep, wide // 2, out_send, wide // 2),
            whole(early, early_local),
            placed(early, 0, 2, hidden),
            placed(early, 2 * pieces(hidden), 1, hidden),
            whole(early, early_local + wide),
        )
        summed = lax.psum(tuple(picked * part[None] for part in sums), ("seq", "tok"))
        qkv_down_grad, qkv_up_grad, out_down_grad, out_up_grad = summed[:4]
        in_down_grad, in_up_grad, out2_down_grad, out2_up_grad = summed[4:]
    return (
        layer_out[None],
        input_grad[None],
        qkv_down_grad,
        qkv_up_grad,
        out_down_grad,
        out_up_grad,
        in_down_grad,
        in_up_grad,
        out2_down_grad,
        out2_up_grad,
    )


def solution(mesh):
    grid = P("tok", "seq")
    split = P("seq", "tok", None)
    return jax.shard_map(
        body,
        mesh=mesh,
        in_specs=(split, split, P("seq", None), P("seq"), grid, grid, grid, grid, P("tok"), P("tok"))
        + (P(),) * 8,
        out_specs=(split, split) + (P(),) * 8,
        check_vma=False,
    )
```
